32 devices in a mesh: basin: 8 (over y, x, core), tile: 4 (over z).
Axes of the slice: x: 2, y: 2, z: 4, core: 2. Of those that a mesh axis runs over, the one named last changes fastest.
Arguments:
- tile_water: float32 [8, 64, 4096], P('basin', None, 'tile'), may hold values from 0.1 to 3
- tile_frac: float32 [8, 64, 4096], P('basin', None, 'tile'), may hold values from 0.01 to 0.12
- tile_cell: int32 [8, 64, 4096], P('basin', None, 'tile'), may hold values from 0 to 255
- storage: float32 [8, 64, 256], P('basin', 'tile'), may hold values from 0 to 2
- kappa: float32 [8, 64, 256], P('basin', 'tile'), may hold values from 0.4 to 1
- inverse: float32 [8, 64, 256, 256], P('basin', 'tile'), may hold values from -0.25 to 1.15
- cell_mask: int32 [8, 64, 256], P('basin', 'tile'), may hold values 0 or 1
- upstream: int32 [8, 64], P('basin', 'tile'), may hold values from 0 to 15, as said below
Outputs:
- level: float32 [8, 64, 256], P('basin', 'tile')
- discharge: float32 [8, 64, 256], P('basin', 'tile')
The draws below stay inside these ranges and needn't reach their ends.
Inputs may be any that keep to these rules, and one draw needn't show every extreme that they name: `upstream`: for each reach position and each group of 16 consecutive chains, the values form a permutation of 0 to 15.
All inputs are finite; a program needn't handle non-finite values. No bound on the sum of `cell_mask` on one device may be relied on, other than what follows from the above.
Results may differ from the reference program's by a relative error of at most 0.0001.
Values sent between devices are 32-bit elements; how exact they have to be, the bound alone decides.
A program may use at most 64 MiB of HBM per device.

```python
import math
import jax
import jax.numpy as jnp
from jax import lax

BLOCK = 256
CH_DEV = 16
SUBSTEPS = 3
CHAINS = 64
POSITIONS = 8
TPB = 4096


def draw_inverse(key, part):
    shape = (POSITIONS, CHAINS, BLOCK, BLOCK)
    noise = jnp.clip(jax.random.normal(key, shape, jnp.float32), -4.0, 4.0) * (0.3 / BLOCK ** 0.5)
    return noise + 0.9 * jnp.eye(BLOCK, dtype=jnp.float32)


def draw_upstream(key, part):
    keys = jax.random.split(jax.random.fold_in(key, 7), POSITIONS * (CHAINS // CH_DEV))
    perms = jax.vmap(lambda single: jax.random.permutation(single, CH_DEV))(keys)
    return perms.reshape(POSITIONS, CHAINS).astype(jnp.int32)


def plant(values, stream_key, least, high):
    longest = values.shape.index(max(values.shape))
    spots = []
    for shift in (0, 1):
        where = [jax.random.randint(jax.random.fold_in(stream_key, axis), (), 0, length) for axis, length in enumerate(values.shape)]
        where[longest] = (where[longest] + shift) % values.shape[longest]
        spots.append(tuple(where))
    return values.at[spots[0]].set(least).at[spots[1]].set(high)


def shard_levels(stream_key, extent, shards, least, largest):
    def one(axis_at, shards_of):
        steps = jax.random.uniform(jax.random.fold_in(jax.random.fold_in(stream_key, 6), axis_at), (shards_of,), jnp.float32, least / len(shards), largest / len(shards))
        return jnp.repeat(jnp.exp(steps), extent[axis_at] // shards_of).reshape((-1,) + (1,) * (len(extent) - axis_at - 1))

    level = one(*shards[0])
    for cut in shards[1:]:
        level = level * one(*cut)
    return level


def setup_inputs(seed: int = 0) -> dict:
    streams_of = jax.random.split(jax.random.key(seed), 9)
    return {
        "tile_water": jnp.clip(jnp.exp(math.log(3.0) - 3.4011974 * jax.random.uniform(streams_of[0], (POSITIONS, CHAINS, TPB), jnp.float32) ** shard_levels(streams_of[0], (POSITIONS, CHAINS, TPB), ((0, 8), (2, 4)), -0.2, 0.2)), 0.1, 3.0),
        "tile_frac": jnp.clip(jnp.exp(math.log(0.12) - 2.4849066 * jax.random.uniform(streams_of[1], (POSITIONS, CHAINS, TPB), jnp.float32) ** shard_levels(streams_of[1], (POSITIONS, CHAINS, TPB), ((0, 8), (2, 4)), -0.2, 0.2)), 0.01, 0.12),
        "tile_cell": plant(jax.random.randint(streams_of[2], (POSITIONS, CHAINS, TPB), 0, BLOCK), jax.random.fold_in(streams_of[2], 1), 0, BLOCK - 1).astype(jnp.int32),
        "storage": jnp.clip(2.0 * jax.random.uniform(streams_of[3], (POSITIONS, CHAINS, BLOCK), jnp.float32) ** shard_levels(streams_of[3], (POSITIONS, CHAINS, BLOCK), ((0, 8), (1, 4)), -0.2, 0.2), 0.0, 2.0),
        "kappa": jnp.clip(0.4 + 0.6 * jax.random.uniform(streams_of[4], (POSITIONS, CHAINS, BLOCK), jnp.float32) ** shard_levels(streams_of[4], (POSITIONS, CHAINS, BLOCK), ((0, 8), (1, 4)), -0.2, 0.2), 0.4, 1.0),
        "inverse": draw_inverse(jax.random.fold_in(streams_of[8], 71), 0),
        "cell_mask": plant((jax.random.randint(streams_of[6], (POSITIONS, CHAINS, BLOCK), 0, 8) < 7).astype(jnp.int32), jax.random.fold_in(streams_of[6], 1), 0, 1),
        "upstream": draw_upstream(jax.random.fold_in(streams_of[8], 71), 0),
    }


time_step = 0.5


def reference(tile_water, tile_frac, tile_cell, storage, kappa, inverse, cell_mask, upstream):
    npos, chains, width = storage.shape
    blocks = jnp.arange(npos * chains, dtype=jnp.int32).reshape(npos, chains, 1)
    ids = (blocks * width + tile_cell).reshape(-1)
    runoff = jax.ops.segment_sum((tile_frac * tile_water).reshape(-1), ids, num_segments=npos * chains * width)
    forcing = time_step * runoff.reshape(npos, chains, width)
    mask = cell_mask.astype(jnp.float32)
    groups = (jnp.arange(chains, dtype=jnp.int32) // CH_DEV) * CH_DEV
    sources = upstream + groups[None, :]
    level = storage
    discharge = storage
    for substep in range(SUBSTEPS):
        def advance(previous, items):
            lev, force, msk, rate, matrix, src = items
            inflow = jnp.take(previous, src, axis=0)
            vector = lev + force + inflow
            wet = msk * jnp.einsum("cjk,ck->cj", matrix, vector, precision=lax.Precision.HIGHEST)
            outflow = rate * wet
            return outflow, (wet - outflow, outflow)
        start = jnp.zeros((chains, width), jnp.float32)
        _, (level, discharge) = lax.scan(advance, start, (level, forcing, mask, kappa, inverse, sources))
    return level, discharge
```

```python
import functools

import jax
import jax.numpy as jnp
from jax import lax
from jax.experimental import pallas as pl
from jax.experimental.pallas import tpu as pltpu
from jax.sharding import PartitionSpec as P

SUBSTEPS = 3
time_step = 0.5
MESH = pl.DeviceIdType.MESH
NT = (((1,), (1,)), ((), ()))


def two_terms(value):
    head = value.astype(jnp.bfloat16)
    return head, (value - head.astype(jnp.float32)).astype(jnp.bfloat16)


def iota(shape, axis):
    return lax.broadcasted_iota(jnp.int32, shape, axis)


def kernel(npos, nset, water_hbm, frac_hbm, cell_hbm, storage_hbm, kappa_hbm, inverse_hbm, mask_hbm, upstream_hbm,
           out_ref,
           storage_ref, kappa_ref, mask_ref, upstream_ref, water, frac, cell, inverse, heads, tails, part, arrived, flow, inflow,
           small_sem, tile_sem, inverse_sem, part_send, part_recv, flow_send, flow_recv):
    rows, width = storage_ref.shape[1], storage_ref.shape[2]
    low = 1 << (width.bit_length() // 2)
    high = width // low
    here = lax.axis_index("basin")
    mine = lax.axis_index("tile")

    barrier = pltpu.get_barrier_semaphore()
    for step in range(1, nset):
        pl.semaphore_signal(barrier, inc=1, device_id={"tile": lax.rem(mine + step, nset)}, device_id_type=MESH)

    @pl.when(here > 0)
    def _():
        pl.semaphore_signal(barrier, inc=1, device_id={"basin": here - 1}, device_id_type=MESH)

    @pl.when(here < npos - 1)
    def _():
        pl.semaphore_signal(barrier, inc=1, device_id={"basin": here + 1}, device_id_type=MESH)

    steps = list(range(1, nset)) + [0]
    loads = []
    for order, step in enumerate(steps):
        owner = lax.rem(mine + step, nset)
        where = pl.ds(pl.multiple_of(owner * rows, rows), rows)
        group = []
        for at, (source, target) in enumerate(((cell_hbm, cell), (water_hbm, water), (frac_hbm, frac))):
            copy = pltpu.make_async_copy(source.at[0, where], target.at[order], tile_sem.at[order, at])
            copy.start()
            group.append(copy)
        loads.append(group)
    small_loads = []
    for at, (source, target) in enumerate(((storage_hbm, storage_ref), (kappa_hbm, kappa_ref), (mask_hbm, mask_ref), (upstream_hbm, upstream_ref))):
        copy = pltpu.make_async_copy(source, target, small_sem.at[at])
        copy.start()
        small_loads.append(copy)
    matrix_loads = []
    for chain in range(rows):
        copy = pltpu.make_async_copy(inverse_hbm.at[0, chain], inverse.at[chain], inverse_sem.at[chain])
        copy.start()
        matrix_loads.append(copy)

    same = lax.rem(iota((high * rows, low * rows), 0), rows) == lax.rem(iota((high * rows, low * rows), 1), rows)
    spread = (iota((low * rows, width), 0) // rows == lax.rem(iota((low * rows, width), 1), low)).astype(jnp.bfloat16)
    block = iota((rows, width), 1) // low

    def cell_sums(order):
        cells = cell[order]
        upper = (cells // low).astype(jnp.float32).astype(jnp.bfloat16)
        lower = lax.rem(cells, low).astype(jnp.float32).astype(jnp.bfloat16)
        head, tail = two_terms(frac[order] * water[order])
        zero = jnp.zeros_like(head)
        one = jnp.ones_like(head)
        picks = [upper == jnp.bfloat16(at) for at in range(high)]
        left = jnp.concatenate([jnp.where(pick, head, zero) for pick in picks] + [jnp.where(pick, tail, zero) for pick in picks], axis=0)
        right = jnp.concatenate([jnp.where(lower == jnp.bfloat16(at), one, zero) for at in range(low)], axis=0)
        both = lax.dot_general(left, right, NT, preferred_element_type=jnp.float32)
        crossed = jnp.where(same, both[: high * rows] + both[high * rows:], 0.0)
        head, tail = two_terms(crossed)
        packed = jnp.dot(jnp.concatenate([head, tail], axis=0), spread, preferred_element_type=jnp.float32)
        packed = packed[: high * rows] + packed[high * rows:]
        total = packed[:rows]
        for at in range(1, high):
            total = jnp.where(block == at, packed[at * rows:(at + 1) * rows], total)
        return total

    sends = []
    own = None
    for order, step in enumerate(steps):
        for copy in loads[order]:
            copy.wait()
        if step == 0:
            for copy in matrix_loads + small_loads:
                copy.wait()
            own = cell_sums(order)
            for chain in range(rows):
                head, tail = two_terms(inverse[chain].T)
                heads[chain] = head
                tails[chain] = tail
            continue
        sums = cell_sums(order)
        part[step - 1] = sums
        if order == 0:
            pl.semaphore_wait(barrier, nset - 1 + jnp.minimum(here, 1) + jnp.minimum(npos - 1 - here, 1))
        copy = pltpu.make_async_remote_copy(
            src_ref=part.at[step - 1], dst_ref=arrived.at[step - 1],
            send_sem=part_send.at[step - 1], recv_sem=part_recv.at[step - 1],
            device_id={"tile": lax.rem(mine + step, nset)}, device_id_type=MESH)
        copy.start()
        sends.append(copy)

    row = iota((rows, width), 0)
    links = jnp.zeros((rows, width), jnp.int32)
    for chain in range(rows):
        links = jnp.where(row == chain, upstream_ref[0, chain], links)
    live = mask_ref[0].astype(jnp.float32)
    rates = kappa_ref[0]
    half = rows // 2
    picked = [lax.rem(iota((2 * half, width), 0), half) == chain for chain in range(half)]

    runoff = own
    for at, copy in enumerate(sends):
        copy.wait_recv()
        runoff = runoff + arrived[at]
    forcing = time_step * runoff

    def product(vector):
        head = vector.astype(jnp.bfloat16).astype(jnp.float32)
        tail = vector - head
        starts = range(0, rows, half)
        lefts = [jnp.concatenate([head[start:start + half], tail[start:start + half]], axis=0).astype(jnp.bfloat16) for start in starts]
        totals = [jnp.zeros((2 * half, width), jnp.float32) for _ in starts]
        for chain in range(half):
            for at, start in enumerate(starts):
                single = jnp.where(picked[chain], lefts[at], jnp.zeros_like(lefts[at]))
                totals[at] += jnp.dot(single, heads[start + chain], preferred_element_type=jnp.float32)
            for at, start in enumerate(starts):
                single = jnp.where(picked[chain], lefts[at], jnp.zeros_like(lefts[at]))
                totals[at] += jnp.dot(single, tails[start + chain], preferred_element_type=jnp.float32)
        return jnp.concatenate([total[:half] + total[half:] for total in totals], axis=0)

    @pl.when(here == 0)
    def _():
        inflow[...] = jnp.zeros_like(inflow)

    level = storage_ref[0]
    outflow = level
    for substep in range(SUBSTEPS):
        copy = pltpu.make_async_remote_copy(
            src_ref=flow.at[substep], dst_ref=inflow.at[substep],
            send_sem=flow_send.at[substep], recv_sem=flow_recv.at[substep],
            device_id={"basin": lax.rem(here + 1, npos)}, device_id_type=MESH)

        @pl.when(here > 0)
        def _():
            copy.wait_recv()

        came = inflow[substep]
        incoming = jnp.broadcast_to(came[:1], (rows, width))
        for chain in range(1, rows):
            incoming = jnp.where(links == chain, jnp.broadcast_to(came[chain:chain + 1], (rows, width)), incoming)
        wet = live * product(level + forcing + incoming)
        outflow = rates * wet
        level = wet - outflow

        @pl.when(here < npos - 1)
        def _():
            flow[substep] = outflow
            copy.start()

    out_ref[0] = level
    out_ref[1] = outflow

    for copy in sends:
        copy.wait_send()

    @pl.when(here < npos - 1)
    def _():
        for substep in range(SUBSTEPS):
            pltpu.make_async_remote_copy(
                src_ref=flow.at[substep], dst_ref=inflow.at[substep],
                send_sem=flow_send.at[substep], recv_sem=flow_recv.at[substep],
                device_id={"basin": lax.rem(here + 1, npos)}, device_id_type=MESH).wait_send()


def solution(mesh):
    npos, nset = mesh.shape["basin"], mesh.shape["tile"]

    def local(tile_water, tile_frac, tile_cell, storage, kappa, inverse, cell_mask, upstream):
        rows, width = storage.shape[1:]
        tiles = tile_water.shape[2]
        anywhere = pl.BlockSpec(memory_space=pltpu.HBM)
        vmem = pl.BlockSpec(memory_space=pltpu.VMEM)
        out = pl.pallas_call(
            functools.partial(kernel, npos, nset),
            out_shape=pltpu.VMEM((2, rows, width), jnp.float32),
            in_specs=[anywhere] * 8,
            out_specs=vmem,
            scratch_shapes=[
                pltpu.VMEM(storage.shape, jnp.float32),
                pltpu.VMEM(kappa.shape, jnp.float32),
                pltpu.VMEM(cell_mask.shape, jnp.int32),
                pltpu.SMEM(upstream.shape, jnp.int32),
                pltpu.VMEM((nset, rows, tiles), jnp.float32),
                pltpu.VMEM((nset, rows, tiles), jnp.float32),
                pltpu.VMEM((nset, rows, tiles), jnp.int32),
                pltpu.VMEM((rows, width, width), jnp.float32),
                pltpu.VMEM((rows, width, width), jnp.bfloat16),
                pltpu.VMEM((rows, width, width), jnp.bfloat16),
                pltpu.VMEM((nset - 1, rows, width), jnp.float32),
                pltpu.VMEM((nset - 1, rows, width), jnp.float32),
                pltpu.VMEM((SUBSTEPS, rows, width), jnp.float32),
                pltpu.VMEM((SUBSTEPS, rows, width), jnp.float32),
                pltpu.SemaphoreType.DMA((4,)),
                pltpu.SemaphoreType.DMA((nset, 3)),
                pltpu.SemaphoreType.DMA((rows,)),
                pltpu.SemaphoreType.DMA((nset - 1,)),
                pltpu.SemaphoreType.DMA((nset - 1,)),
                pltpu.SemaphoreType.DMA((SUBSTEPS,)),
                pltpu.SemaphoreType.DMA((SUBSTEPS,)),
            ],
            compiler_params=pltpu.CompilerParams(collective_id=0, has_side_effects=True),
        )(tile_water, tile_frac, tile_cell, storage, kappa, inverse, cell_mask, upstream)
        return out[:1], out[1:]

    tiled = P("basin", None, "tile")
    chain = P("basin", "tile", None)
    return jax.shard_map(
        local,
        mesh=mesh,
        in_specs=(tiled, tiled, tiled, chain, chain, P("basin", "tile", None, None), chain, P("basin", "tile")),
        out_specs=(chain, chain),
        check_vma=False,
    )
```

```python
import functools

import jax
import jax.numpy as jnp
from jax import lax
from jax.experimental import pallas as pl
from jax.experimental.pallas import tpu as pltpu
from jax.sharding import PartitionSpec as P

SUBSTEPS = 3
time_step = 0.5
MESH = pl.DeviceIdType.MESH
NT = (((1,), (1,)), ((), ()))


def two_terms(value):
    head = value.astype(jnp.bfloat16)
    return head, (value - head.astype(jnp.float32)).astype(jnp.bfloat16)


def iota(shape, axis):
    return lax.broadcasted_iota(jnp.int32, shape, axis)


def kernel(npos, nset, water_hbm, frac_hbm, cell_hbm, storage_hbm, kappa_hbm, inverse_hbm, mask_hbm, upstream_hbm,
           out_ref,
           storage_ref, kappa_ref, mask_ref, upstream_ref, water, frac, cell, inverse, heads, tails, part, arrived, flow, inflow,
           small_sem, tile_sem, inverse_sem, part_send, part_recv, flow_send, flow_recv):
    rows, width = storage_ref.shape[1], storage_ref.shape[2]
    low = 1 << (width.bit_length() // 2)
    high = width // low
    here = lax.axis_index("basin")
    mine = lax.axis_index("tile")

    barrier = pltpu.get_barrier_semaphore()
    for step in range(1, nset):
        pl.semaphore_signal(barrier, inc=1, device_id={"tile": lax.rem(mine + step, nset)}, device_id_type=MESH)

    @pl.when(here > 0)
    def _():
        pl.semaphore_signal(barrier, inc=1, device_id={"basin": here - 1}, device_id_type=MESH)

    @pl.when(here < npos - 1)
    def _():
        pl.semaphore_signal(barrier, inc=1, device_id={"basin": here + 1}, device_id_type=MESH)

    steps = list(range(1, nset)) + [0]
    loads = []
    for order, step in enumerate(steps):
        owner = lax.rem(mine + step, nset)
        where = pl.ds(pl.multiple_of(owner * rows, rows), rows)
        group = []
        for at, (source, target) in enumerate(((cell_hbm, cell), (water_hbm, water), (frac_hbm, frac))):
            copy = pltpu.make_async_copy(source.at[0, where], target.at[order], tile_sem.at[order, at])
            copy.start()
            group.append(copy)
        loads.append(group)
    small_loads = []
    for at, (source, target) in enumerate(((storage_hbm, storage_ref), (kappa_hbm, kappa_ref), (mask_hbm, mask_ref), (upstream_hbm, upstream_ref))):
        copy = pltpu.make_async_copy(source, target, small_sem.at[at])
        copy.start()
        small_loads.append(copy)
    matrix_loads = []
    for chain in range(rows):
        copy = pltpu.make_async_copy(inverse_hbm.at[0, chain], inverse.at[chain], inverse_sem.at[chain])
        copy.start()
        matrix_loads.append(copy)

    same = lax.rem(iota((high * rows, low * rows), 0), rows) == lax.rem(iota((high * rows, low * rows), 1), rows)
    spread = (iota((low * rows, width), 0) // rows == lax.rem(iota((low * rows, width), 1), low)).astype(jnp.bfloat16)
    block = iota((rows, width), 1) // low

    def cell_sums(order):
        cells = cell[order]
        upper = (cells // low).astype(jnp.float32).astype(jnp.bfloat16)
        lower = lax.rem(cells, low).astype(jnp.float32).astype(jnp.bfloat16)
        head, tail = two_terms(frac[order] * water[order])
        zero = jnp.zeros_like(head)
        one = jnp.ones_like(head)
        picks = [upper == jnp.bfloat16(at) for at in range(high)]
        left = jnp.concatenate([jnp.where(pick, head, zero) for pick in picks] + [jnp.where(pick, tail, zero) for pick in picks], axis=0)
        right = jnp.concatenate([jnp.where(lower == jnp.bfloat16(at), one, zero) for at in range(low)], axis=0)
        both = lax.dot_general(left, right, NT, preferred_element_type=jnp.float32)
        crossed = jnp.where(same, both[: high * rows] + both[high * rows:], 0.0)
        head, tail = two_terms(crossed)
        packed = jnp.dot(jnp.concatenate([head, tail], axis=0), spread, preferred_element_type=jnp.float32)
        packed = packed[: high * rows] + packed[high * rows:]
        total = packed[:rows]
        for at in range(1, high):
            total = jnp.where(block == at, packed[at * rows:(at + 1) * rows], total)
        return total

    sends = []
    own = None
    for order, step in enumerate(steps):
        for copy in loads[order]:
            copy.wait()
        if step == 0:
            for copy in matrix_loads + small_loads:
                copy.wait()
            own = cell_sums(order)
            for chain in range(rows // 2):
                head, tail = two_terms(inverse[chain].T)
                heads[chain] = head
                tails[chain] = tail
            continue
        sums = cell_sums(order)
        part[step - 1] = sums
        if order == 0:
            pl.semaphore_wait(barrier, nset - 1 + jnp.minimum(here, 1) + jnp.minimum(npos - 1 - here, 1))
        copy = pltpu.make_async_remote_copy(
            src_ref=part.at[step - 1], dst_ref=arrived.at[step - 1],
            send_sem=part_send.at[step - 1], recv_sem=part_recv.at[step - 1],
            device_id={"tile": lax.rem(mine + step, nset)}, device_id_type=MESH)
        copy.start()
        sends.append(copy)

    row = iota((rows, width), 0)
    links = jnp.zeros((rows, width), jnp.int32)
    for chain in range(rows):
        links = jnp.where(row == chain, upstream_ref[0, chain], links)
    live = mask_ref[0].astype(jnp.float32)
    rates = kappa_ref[0]
    half = rows // 2
    picked = [lax.rem(iota((2 * half, width), 0), half) == chain for chain in range(half)]

    runoff = own
    for at, copy in enumerate(sends):
        copy.wait_recv()
        runoff = runoff + arrived[at]
    forcing = time_step * runoff

    def product(vector):
        head = vector.astype(jnp.bfloat16).astype(jnp.float32)
        tail = vector - head
        left = jnp.concatenate([head[:half], tail[:half]], axis=0).astype(jnp.bfloat16)
        first = jnp.zeros((2 * half, width), jnp.float32)
        second = jnp.zeros((2 * half, width), jnp.float32)
        reduced = []
        for chain in range(rows - half):
            if chain < half:
                single = jnp.where(picked[chain], left, jnp.zeros_like(left))
                first += jnp.dot(single, heads[chain], preferred_element_type=jnp.float32)
                second += jnp.dot(single, tails[chain], preferred_element_type=jnp.float32)
            other = half + chain
            reduced.append(jnp.sum(inverse[other] * vector[other:other + 1], axis=1)[None])
        total = first + second
        return jnp.concatenate([total[:half] + total[half:]] + reduced, axis=0)

    @pl.when(here == 0)
    def _():
        inflow[...] = jnp.zeros_like(inflow)

    level = storage_ref[0]
    outflow = level
    for substep in range(SUBSTEPS):
        copy = pltpu.make_async_remote_copy(
            src_ref=flow.at[substep], dst_ref=inflow.at[substep],
            send_sem=flow_send.at[substep], recv_sem=flow_recv.at[substep],
            device_id={"basin": lax.rem(here + 1, npos)}, device_id_type=MESH)

        @pl.when(here > 0)
        def _():
            copy.wait_recv()

        came = inflow[substep]
        incoming = jnp.broadcast_to(came[:1], (rows, width))
        for chain in range(1, rows):
            incoming = jnp.where(links == chain, jnp.broadcast_to(came[chain:chain + 1], (rows, width)), incoming)
        wet = live * product(level + forcing + incoming)
        outflow = rates * wet
        level = wet - outflow

        @pl.when(here < npos - 1)
        def _():
            flow[substep] = outflow
            copy.start()

    out_ref[0] = level
    out_ref[1] = outflow

    for copy in sends:
        copy.wait_send()

    @pl.when(here < npos - 1)
    def _():
        for substep in range(SUBSTEPS):
            pltpu.make_async_remote_copy(
                src_ref=flow.at[substep], dst_ref=inflow.at[substep],
                send_sem=flow_send.at[substep], recv_sem=flow_recv.at[substep],
                device_id={"basin": lax.rem(here + 1, npos)}, device_id_type=MESH).wait_send()


def solution(mesh):
    npos, nset = mesh.shape["basin"], mesh.shape["tile"]

    def local(tile_water, tile_frac, tile_cell, storage, kappa, inverse, cell_mask, upstream):
        rows, width = storage.shape[1:]
        tiles = tile_water.shape[2]
        anywhere = pl.BlockSpec(memory_space=pltpu.HBM)
        vmem = pl.BlockSpec(memory_space=pltpu.VMEM)
        out = pl.pallas_call(
            functools.partial(kernel, npos, nset),
            out_shape=pltpu.VMEM((2, rows, width), jnp.float32),
            in_specs=[anywhere] * 8,
            out_specs=vmem,
            scratch_shapes=[
                pltpu.VMEM(storage.shape, jnp.float32),
                pltpu.VMEM(kappa.shape, jnp.float32),
                pltpu.VMEM(cell_mask.shape, jnp.int32),
                pltpu.SMEM(upstream.shape, jnp.int32),
                pltpu.VMEM((nset, rows, tiles), jnp.float32),
                pltpu.VMEM((nset, rows, tiles), jnp.float32),
                pltpu.VMEM((nset, rows, tiles), jnp.int32),
                pltpu.VMEM((rows, width, width), jnp.float32),
                pltpu.VMEM((rows // 2, width, width), jnp.bfloat16),
                pltpu.VMEM((rows // 2, width, width), jnp.bfloat16),
                pltpu.VMEM((nset - 1, rows, width), jnp.float32),
                pltpu.VMEM((nset - 1, rows, width), jnp.float32),
                pltpu.VMEM((SUBSTEPS, rows, width), jnp.float32),
                pltpu.VMEM((SUBSTEPS, rows, width), jnp.float32),
                pltpu.SemaphoreType.DMA((4,)),
                pltpu.SemaphoreType.DMA((nset, 3)),
                pltpu.SemaphoreType.DMA((rows,)),
                pltpu.SemaphoreType.DMA((nset - 1,)),
                pltpu.SemaphoreType.DMA((nset - 1,)),
                pltpu.SemaphoreType.DMA((SUBSTEPS,)),
                pltpu.SemaphoreType.DMA((SUBSTEPS,)),
            ],
            compiler_params=pltpu.CompilerParams(collective_id=0, has_side_effects=True),
        )(tile_water, tile_frac, tile_cell, storage, kappa, inverse, cell_mask, upstream)
        return out[:1], out[1:]

    tiled = P("basin", None, "tile")
    chain = P("basin", "tile", None)
    return jax.shard_map(
        local,
        mesh=mesh,
        in_specs=(tiled, tiled, tiled, chain, chain, P("basin", "tile", None, None), chain, P("basin", "tile")),
        out_specs=(chain, chain),
        check_vma=False,
    )
```

```python
import functools

import jax
import jax.numpy as jnp
from jax import lax
from jax.experimental import pallas as pl
from jax.experimental.pallas import tpu as pltpu
from jax.sharding import PartitionSpec as P

SUBSTEPS = 3
time_step = 0.5
MESH = pl.DeviceIdType.MESH
NT = (((1,), (1,)), ((), ()))


def two_terms(value):
    head = value.astype(jnp.bfloat16)
    return head, (value - head.astype(jnp.float32)).astype(jnp.bfloat16)


def iota(shape, axis):
    return lax.broadcasted_iota(jnp.int32, shape, axis)


def kernel(npos, nset, water_hbm, frac_hbm, cell_hbm, storage_hbm, kappa_hbm, inverse_hbm, mask_hbm, upstream_hbm,
           out_ref,
           storage_ref, kappa_ref, mask_ref, upstream_ref, water, frac, cell, inverse, heads, tails, part, arrived, flow, inflow, level_ref, forcing_ref, came_ref, own_ref,
           small_sem, tile_sem, inverse_sem, part_send, part_recv, flow_send, flow_recv):
    rows, width = storage_ref.shape[1], storage_ref.shape[2]
    low = 1 << (width.bit_length() // 2)
    high = width // low
    here = lax.axis_index("basin")
    mine = lax.axis_index("tile")

    barrier = pltpu.get_barrier_semaphore()
    for step in range(1, nset):
        pl.semaphore_signal(barrier, inc=1, device_id={"tile": lax.rem(mine + step, nset)}, device_id_type=MESH)

    @pl.when(here > 0)
    def _():
        pl.semaphore_signal(barrier, inc=1, device_id={"basin": here - 1}, device_id_type=MESH)

    @pl.when(here < npos - 1)
    def _():
        pl.semaphore_signal(barrier, inc=1, device_id={"basin": here + 1}, device_id_type=MESH)

    steps = list(range(1, nset)) + [0]
    loads = []
    for order, step in enumerate(steps):
        owner = lax.rem(mine + step, nset)
        where = pl.ds(pl.multiple_of(owner * rows, rows), rows)
        group = []
        for at, (source, target) in enumerate(((cell_hbm, cell), (water_hbm, water), (frac_hbm, frac))):
            copy = pltpu.make_async_copy(source.at[0, where], target.at[order], tile_sem.at[order, at])
            copy.start()
            group.append(copy)
        loads.append(group)
    small_loads = []
    for at, (source, target) in enumerate(((storage_hbm, storage_ref), (kappa_hbm, kappa_ref), (mask_hbm, mask_ref), (upstream_hbm, upstream_ref))):
        copy = pltpu.make_async_copy(source, target, small_sem.at[at])
        copy.start()
        small_loads.append(copy)
    matrix_loads = []
    for chain in range(rows):
        copy = pltpu.make_async_copy(inverse_hbm.at[0, chain], inverse.at[chain], inverse_sem.at[chain])
        copy.start()
        matrix_loads.append(copy)

    same = lax.rem(iota((high * rows, low * rows), 0), rows) == lax.rem(iota((high * rows, low * rows), 1), rows)
    spread = (iota((low * rows, width), 0) // rows == lax.rem(iota((low * rows, width), 1), low)).astype(jnp.bfloat16)
    block = iota((rows, width), 1) // low

    def cell_sums(order):
        cells = cell[order]
        upper = (cells // low).astype(jnp.float32).astype(jnp.bfloat16)
        lower = lax.rem(cells, low).astype(jnp.float32).astype(jnp.bfloat16)
        head, tail = two_terms(frac[order] * water[order])
        zero = jnp.zeros_like(head)
        one = jnp.ones_like(head)
        picks = [upper == jnp.bfloat16(at) for at in range(high)]
        left = jnp.concatenate([jnp.where(pick, head, zero) for pick in picks] + [jnp.where(pick, tail, zero) for pick in picks], axis=0)
        right = jnp.concatenate([jnp.where(lower == jnp.bfloat16(at), one, zero) for at in range(low)], axis=0)
        both = lax.dot_general(left, right, NT, preferred_element_type=jnp.float32)
        crossed = jnp.where(same, both[: high * rows] + both[high * rows:], 0.0)
        head, tail = two_terms(crossed)
        packed = jnp.dot(jnp.concatenate([head, tail], axis=0), spread, preferred_element_type=jnp.float32)
        packed = packed[: high * rows] + packed[high * rows:]
        total = packed[:rows]
        for at in range(1, high):
            total = jnp.where(block == at, packed[at * rows:(at + 1) * rows], total)
        return total

    sends = []
    own = None
    for order, step in enumerate(steps):
        for copy in loads[order]:
            copy.wait()
        if step == 0:
            for copy in matrix_loads + small_loads:
                copy.wait()
            own = cell_sums(order)
            for chain in range(rows // 2):
                head, tail = two_terms(inverse[chain].T)
                heads[chain] = head
                tails[chain] = tail
            continue
        sums = cell_sums(order)
        part[step - 1] = sums
        if order == 0:
            pl.semaphore_wait(barrier, nset - 1 + jnp.minimum(here, 1) + jnp.minimum(npos - 1 - here, 1))
        copy = pltpu.make_async_remote_copy(
            src_ref=part.at[step - 1], dst_ref=arrived.at[step - 1],
            send_sem=part_send.at[step - 1], recv_sem=part_recv.at[step - 1],
            device_id={"tile": lax.rem(mine + step, nset)}, device_id_type=MESH)
        copy.start()
        sends.append(copy)

    row = iota((rows, width), 0)
    links = jnp.zeros((rows, width), jnp.int32)
    for chain in range(rows):
        links = jnp.where(row == chain, upstream_ref[0, chain], links)
    live = mask_ref[0].astype(jnp.float32)
    rates = kappa_ref[0]
    half = rows // 2
    picked = [lax.rem(iota((2 * half, width), 0), half) == chain for chain in range(half)]

    def product(vector):
        head = vector.astype(jnp.bfloat16).astype(jnp.float32)
        tail = vector - head
        left = jnp.concatenate([head[:half], tail[:half]], axis=0).astype(jnp.bfloat16)
        first = jnp.zeros((2 * half, width), jnp.float32)
        second = jnp.zeros((2 * half, width), jnp.float32)
        reduced = []
        for chain in range(rows - half):
            if chain < half:
                single = jnp.where(picked[chain], left, jnp.zeros_like(left))
                first += jnp.dot(single, heads[chain], preferred_element_type=jnp.float32)
                second += jnp.dot(single, tails[chain], preferred_element_type=jnp.float32)
            other = half + chain
            reduced.append(jnp.sum(inverse[other] * vector[other:other + 1], axis=1)[None])
        total = first + second
        return jnp.concatenate([total[:half] + total[half:]] + reduced, axis=0)

    came_ref[...] = jnp.zeros_like(came_ref)
    forcing_ref[...] = jnp.zeros_like(forcing_ref)
    own_ref[...] = own
    level_ref[...] = storage_ref[0]

    def flow_copy(substep):
        return pltpu.make_async_remote_copy(
            src_ref=flow.at[substep], dst_ref=inflow.at[substep],
            send_sem=flow_send.at[substep], recv_sem=flow_recv.at[substep],
            device_id={"basin": lax.rem(here + 1, npos)}, device_id_type=MESH)

    def turn(at, carry):
        substep = jnp.maximum(at - 1, 0)
        real = at > 0

        @pl.when(jnp.logical_and(real, here > 0))
        def _():
            flow_copy(substep).wait_recv()
            came_ref[...] = inflow[substep]

        @pl.when(at == 1)
        def _():
            runoff = own_ref[...]
            for step, copy in enumerate(sends):
                copy.wait_recv()
                runoff = runoff + arrived[step]
            forcing_ref[...] = time_step * runoff

        came = came_ref[...]
        incoming = jnp.broadcast_to(came[:1], (rows, width))
        for chain in range(1, rows):
            incoming = jnp.where(links == chain, jnp.broadcast_to(came[chain:chain + 1], (rows, width)), incoming)
        wet = live * product(level_ref[...] + forcing_ref[...] + incoming)
        outflow = rates * wet

        @pl.when(jnp.logical_and(real, here < npos - 1))
        def _():
            flow[substep] = outflow
            flow_copy(substep).start()

        @pl.when(real)
        def _():
            level_ref[...] = wet - outflow
            out_ref[0] = wet - outflow
            out_ref[1] = outflow

        return carry

    lax.fori_loop(0, SUBSTEPS + 1, turn, 0)

    for copy in sends:
        copy.wait_send()

    @pl.when(here < npos - 1)
    def _():
        for substep in range(SUBSTEPS):
            flow_copy(substep).wait_send()


def solution(mesh):
    npos, nset = mesh.shape["basin"], mesh.shape["tile"]

    def local(tile_water, tile_frac, tile_cell, storage, kappa, inverse, cell_mask, upstream):
        rows, width = storage.shape[1:]
        tiles = tile_water.shape[2]
        anywhere = pl.BlockSpec(memory_space=pltpu.HBM)
        vmem = pl.BlockSpec(memory_space=pltpu.VMEM)
        out = pl.pallas_call(
            functools.partial(kernel, npos, nset),
            out_shape=pltpu.VMEM((2, rows, width), jnp.float32),
            in_specs=[anywhere] * 8,
            out_specs=vmem,
            scratch_shapes=[
                pltpu.VMEM(storage.shape, jnp.float32),
                pltpu.VMEM(kappa.shape, jnp.float32),
                pltpu.VMEM(cell_mask.shape, jnp.int32),
                pltpu.SMEM(upstream.shape, jnp.int32),
                pltpu.VMEM((nset, rows, tiles), jnp.float32),
                pltpu.VMEM((nset, rows, tiles), jnp.float32),
                pltpu.VMEM((nset, rows, tiles), jnp.int32),
                pltpu.VMEM((rows, width, width), jnp.float32),
                pltpu.VMEM((rows // 2, width, width), jnp.bfloat16),
                pltpu.VMEM((rows // 2, width, width), jnp.bfloat16),
                pltpu.VMEM((nset - 1, rows, width), jnp.float32),
                pltpu.VMEM((nset - 1, rows, width), jnp.float32),
                pltpu.VMEM((SUBSTEPS, rows, width), jnp.float32),
                pltpu.VMEM((SUBSTEPS, rows, width), jnp.float32),
                pltpu.VMEM((rows, width), jnp.float32),
                pltpu.VMEM((rows, width), jnp.float32),
                pltpu.VMEM((rows, width), jnp.float32),
                pltpu.VMEM((rows, width), jnp.float32),
                pltpu.SemaphoreType.DMA((4,)),
                pltpu.SemaphoreType.DMA((nset, 3)),
                pltpu.SemaphoreType.DMA((rows,)),
                pltpu.SemaphoreType.DMA((nset - 1,)),
                pltpu.SemaphoreType.DMA((nset - 1,)),
                pltpu.SemaphoreType.DMA((SUBSTEPS,)),
                pltpu.SemaphoreType.DMA((SUBSTEPS,)),
            ],
            compiler_params=pltpu.CompilerParams(collective_id=0, has_side_effects=True),
        )(tile_water, tile_frac, tile_cell, storage, kappa, inverse, cell_mask, upstream)
        return out[:1], out[1:]

    tiled = P("basin", None, "tile")
    chain = P("basin", "tile", None)
    return jax.shard_map(
        local,
        mesh=mesh,
        in_specs=(tiled, tiled, tiled, chain, chain, P("basin", "tile", None, None), chain, P("basin", "tile")),
        out_specs=(chain, chain),
        check_vma=False,
    )
```

```python
import functools

import jax
import jax.numpy as jnp
from jax import lax
from jax.experimental import pallas as pl
from jax.experimental.pallas import tpu as pltpu
from jax.sharding import PartitionSpec as P

SUBSTEPS = 3
time_step = 0.5
MESH = pl.DeviceIdType.MESH
NT = (((1,), (1,)), ((), ()))
UP, OWN = 0, 1
RATE, LIVE, LINK, FORCE, START = range(5)


def two_terms(value):
    head = value.astype(jnp.bfloat16)
    return head, (value - head.astype(jnp.float32)).astype(jnp.bfloat16)


def iota(shape, axis):
    return lax.broadcasted_iota(jnp.int32, shape, axis)


def kernel(npos, nset, water_hbm, frac_hbm, cell_hbm, storage_hbm, kappa_hbm, inverse_hbm, mask_hbm, upstream_hbm,
           out_ref,
           storage_ref, kappa_ref, mask_ref, upstream_ref, water, frac, cell, inverse, heads, tails, part, arrived, flow, inflow,
           fixed, level_ref, came_ref, own_ref,
           small_sem, tile_sem, inverse_sem, part_send, part_recv, flow_send, flow_recv, push_send, push_recv, fixed_send, fixed_recv, go):
    rows, width = storage_ref.shape[1], storage_ref.shape[2]
    low = 1 << (width.bit_length() // 2)
    high = width // low
    half = rows // 2
    here = lax.axis_index("basin")
    mine = lax.axis_index("tile")
    odd = lax.rem(here, 2) == 1
    paired = jnp.logical_and(odd, here > 2)
    pushes = jnp.logical_and(jnp.logical_and(jnp.logical_not(odd), here > 1), here < npos - 1)
    to_next = jnp.logical_and(jnp.logical_or(odd, here == 0), here < npos - 1)
    to_second = jnp.logical_and(odd, here < npos - 2)

    barrier = pltpu.get_barrier_semaphore()
    report = here + pushes.astype(jnp.int32)
    for step in range(1, nset):
        pl.semaphore_signal(barrier, inc=1, device_id={"basin": report, "tile": lax.rem(mine + step, nset)}, device_id_type=MESH)

    @pl.when(pushes)
    def _():
        pl.semaphore_signal(barrier, inc=1, device_id={"basin": here + 1}, device_id_type=MESH)

    @pl.when(here > 0)
    def _():
        pl.semaphore_signal(barrier, inc=1, device_id={"basin": here - 1}, device_id_type=MESH)

    @pl.when(paired)
    def _():
        pl.semaphore_signal(barrier, inc=1, device_id={"basin": here - 2}, device_id_type=MESH)

    def tile_loads(order):
        owner = lax.rem(mine + order + 1, nset)
        where = pl.ds(pl.multiple_of(owner * rows, rows), rows)
        return [
            pltpu.make_async_copy(source.at[0, where], target.at[order], tile_sem.at[order, at])
            for at, (source, target) in enumerate(((cell_hbm, cell), (water_hbm, water), (frac_hbm, frac)))]

    for order in range(nset):
        for copy in tile_loads(order):
            copy.start()
    small_loads = []
    for at, (source, target) in enumerate(((storage_hbm, storage_ref), (kappa_hbm, kappa_ref), (mask_hbm, mask_ref), (upstream_hbm, upstream_ref))):
        copy = pltpu.make_async_copy(source, target, small_sem.at[at])
        copy.start()
        small_loads.append(copy)

    def matrix_load(chain):
        return pltpu.make_async_copy(inverse_hbm.at[0, chain], inverse.at[OWN, chain], inverse_sem.at[chain])

    def matrix_push(chain):
        return pltpu.make_async_remote_copy(
            src_ref=inverse_hbm.at[0, chain], dst_ref=inverse.at[UP, chain],
            send_sem=push_send.at[chain], recv_sem=push_recv.at[chain],
            device_id={"basin": lax.rem(here + 1, npos)}, device_id_type=MESH)

    def fixed_push():
        return pltpu.make_async_remote_copy(
            src_ref=fixed.at[OWN], dst_ref=fixed.at[UP], send_sem=fixed_send, recv_sem=fixed_recv,
            device_id={"basin": lax.rem(here + 1, npos)}, device_id_type=MESH)

    def part_copy(order):
        return pltpu.make_async_remote_copy(
            src_ref=part.at[order], dst_ref=arrived.at[order],
            send_sem=part_send.at[order], recv_sem=part_recv.at[order],
            device_id={"tile": lax.rem(mine + order + 1, nset)}, device_id_type=MESH)

    def flow_copy(substep, ahead):
        return pltpu.make_async_remote_copy(
            src_ref=flow.at[substep], dst_ref=inflow.at[substep],
            send_sem=flow_send.at[ahead - 1, substep], recv_sem=flow_recv.at[substep],
            device_id={"basin": lax.rem(here + ahead, npos)}, device_id_type=MESH)

    def each_chain(do):
        def one(chain, carry):
            do(chain)
            return carry
        lax.fori_loop(0, rows, one, 0)

    each_chain(lambda chain: matrix_load(chain).start())

    @pl.when(pushes)
    def _():
        pl.semaphore_wait(barrier, 1)
        each_chain(lambda chain: matrix_push(chain).start())

    same = lax.rem(iota((high * rows, low * rows), 0), rows) == lax.rem(iota((high * rows, low * rows), 1), rows)
    spread = (iota((low * rows, width), 0) // rows == lax.rem(iota((low * rows, width), 1), low)).astype(jnp.bfloat16)
    block = iota((rows, width), 1) // low

    def cell_sums(order):
        cells = cell[order]
        upper = (cells // low).astype(jnp.float32).astype(jnp.bfloat16)
        lower = lax.rem(cells, low).astype(jnp.float32).astype(jnp.bfloat16)
        head, tail = two_terms(frac[order] * water[order])
        zero = jnp.zeros_like(head)
        one = jnp.ones_like(head)
        picks = [upper == jnp.bfloat16(at) for at in range(high)]
        left = jnp.concatenate([jnp.where(pick, head, zero) for pick in picks] + [jnp.where(pick, tail, zero) for pick in picks], axis=0)
        right = jnp.concatenate([jnp.where(lower == jnp.bfloat16(at), one, zero) for at in range(low)], axis=0)
        both = lax.dot_general(left, right, NT, preferred_element_type=jnp.float32)
        crossed = jnp.where(same, both[: high * rows] + both[high * rows:], 0.0)
        head, tail = two_terms(crossed)
        packed = jnp.dot(jnp.concatenate([head, tail], axis=0), spread, preferred_element_type=jnp.float32)
        packed = packed[: high * rows] + packed[high * rows:]
        total = packed[:rows]
        for at in range(1, high):
            total = jnp.where(block == at, packed[at * rows:(at + 1) * rows], total)
        return total

    def group(order, carry):
        for copy in tile_loads(order):
            copy.wait()
        sums = cell_sums(order)

        @pl.when(jnp.logical_and(order == 0, jnp.logical_not(pushes)))
        def _():
            pl.semaphore_wait(barrier, (nset - 1) * (1 + paired.astype(jnp.int32)) + paired.astype(jnp.int32)
                              + to_next.astype(jnp.int32) + to_second.astype(jnp.int32))

            @pl.when(paired)
            def _():
                pl.semaphore_signal(go, inc=1, device_id={"basin": here - 1}, device_id_type=MESH)

        @pl.when(jnp.logical_and(order == 0, pushes))
        def _():
            pl.semaphore_wait(go, 1)

        @pl.when(order < nset - 1)
        def _():
            part[order] = sums
            part_copy(order).start()

        @pl.when(order == nset - 1)
        def _():
            own_ref[...] = sums

        return carry

    lax.fori_loop(0, nset, group, 0)

    for copy in small_loads:
        copy.wait()
    row = iota((rows, width), 0)
    links = jnp.zeros((rows, width), jnp.int32)
    for chain in range(rows):
        links = jnp.where(row == chain, upstream_ref[0, chain], links)
    fixed[OWN, LINK] = links.astype(jnp.float32)
    fixed[OWN, LIVE] = mask_ref[0].astype(jnp.float32)
    fixed[OWN, RATE] = kappa_ref[0]
    fixed[OWN, START] = storage_ref[0]
    fixed[OWN, FORCE] = jnp.zeros((rows, width), jnp.float32)
    level_ref[OWN] = storage_ref[0]
    came_ref[...] = jnp.zeros_like(came_ref)

    def prepare(slot, ready):
        def one(chain, carry):
            ready(chain)
            head, tail = two_terms(inverse[slot, chain].T)
            heads[slot, chain] = head
            tails[slot, chain] = tail
            return carry

        def rest(chain, carry):
            ready(chain)
            return carry
        lax.fori_loop(0, half, one, 0)
        lax.fori_loop(half, rows, rest, 0)

    prepare(OWN, lambda chain: matrix_load(chain).wait())

    picked = [lax.rem(iota((2 * half, width), 0), half) == chain for chain in range(half)]

    def product(slot, vector):
        head = vector.astype(jnp.bfloat16).astype(jnp.float32)
        tail = vector - head
        left = jnp.concatenate([head[:half], tail[:half]], axis=0).astype(jnp.bfloat16)
        first = jnp.zeros((2 * half, width), jnp.float32)
        second = jnp.zeros((2 * half, width), jnp.float32)
        reduced = []
        for chain in range(rows - half):
            if chain < half:
                single = jnp.where(picked[chain], left, jnp.zeros_like(left))
                first += jnp.dot(single, heads[slot, chain], preferred_element_type=jnp.float32)
                second += jnp.dot(single, tails[slot, chain], preferred_element_type=jnp.float32)
            other = half + chain
            reduced.append(jnp.sum(inverse[slot, other] * vector[other:other + 1], axis=1)[None])
        total = first + second
        return jnp.concatenate([total[:half] + total[half:]] + reduced, axis=0)

    def turn(at, carry):
        real = at > 0
        count = jnp.maximum(at - 1, 0)
        slot = jnp.where(jnp.logical_and(paired, real), lax.rem(count, 2), OWN)
        substep = jnp.where(paired, count // 2, count)
        leads = jnp.logical_or(jnp.logical_not(paired), slot == UP)

        @pl.when(at == 1)
        def _():
            runoff = own_ref[...]
            for order in range(nset - 1):
                part_copy(order).wait_recv()
                runoff = runoff + arrived[order]
            fixed[OWN, FORCE] = time_step * runoff

            @pl.when(pushes)
            def _():
                fixed_push().start()

            @pl.when(paired)
            def _():
                prepare(UP, lambda chain: matrix_push(chain).wait_recv())
                fixed_push().wait_recv()
                level_ref[UP] = fixed[UP, START]

        @pl.when(jnp.logical_and(real, jnp.logical_and(leads, here > 0)))
        def _():
            flow_copy(substep, 1).wait_recv()
            came_ref[...] = inflow[substep]

        came = came_ref[...]
        links = fixed[slot, LINK]
        incoming = jnp.broadcast_to(came[:1], (rows, width))
        for chain in range(1, rows):
            incoming = jnp.where(links == float(chain), jnp.broadcast_to(came[chain:chain + 1], (rows, width)), incoming)
        wet = fixed[slot, LIVE] * product(slot, level_ref[slot] + fixed[slot, FORCE] + incoming)
        outflow = fixed[slot, RATE] * wet

        @pl.when(jnp.logical_and(real, slot == OWN))
        def _():
            flow[substep] = outflow

            @pl.when(to_second)
            def _():
                flow_copy(substep, 2).start()

            @pl.when(to_next)
            def _():
                flow_copy(substep, 1).start()

            out_ref[0] = wet - outflow
            out_ref[1] = outflow

        @pl.when(real)
        def _():
            level_ref[slot] = wet - outflow

        @pl.when(jnp.logical_and(real, slot == UP))
        def _():
            came_ref[...] = outflow

        return carry

    lax.fori_loop(0, 1 + jnp.where(paired, 2 * SUBSTEPS, SUBSTEPS), turn, 0)

    for order in range(nset - 1):
        part_copy(order).wait_send()

    @pl.when(pushes)
    def _():
        each_chain(lambda chain: matrix_push(chain).wait_send())
        fixed_push().wait_send()

    @pl.when(to_next)
    def _():
        for substep in range(SUBSTEPS):
            flow_copy(substep, 1).wait_send()

    @pl.when(to_second)
    def _():
        for substep in range(SUBSTEPS):
            flow_copy(substep, 2).wait_send()


def solution(mesh):
    npos, nset = mesh.shape["basin"], mesh.shape["tile"]

    def local(tile_water, tile_frac, tile_cell, storage, kappa, inverse, cell_mask, upstream):
        rows, width = storage.shape[1:]
        tiles = tile_water.shape[2]
        anywhere = pl.BlockSpec(memory_space=pltpu.HBM)
        vmem = pl.BlockSpec(memory_space=pltpu.VMEM)
        others = max(nset - 1, 1)
        out = pl.pallas_call(
            functools.partial(kernel, npos, nset),
            out_shape=pltpu.VMEM((2, rows, width), jnp.float32),
            in_specs=[anywhere] * 8,
            out_specs=vmem,
            scratch_shapes=[
                pltpu.VMEM(storage.shape, jnp.float32),
                pltpu.VMEM(kappa.shape, jnp.float32),
                pltpu.VMEM(cell_mask.shape, jnp.int32),
                pltpu.SMEM(upstream.shape, jnp.int32),
                pltpu.VMEM((nset, rows, tiles), jnp.float32),
                pltpu.VMEM((nset, rows, tiles), jnp.float32),
                pltpu.VMEM((nset, rows, tiles), jnp.int32),
                pltpu.VMEM((2, rows, width, width), jnp.float32),
                pltpu.VMEM((2, rows // 2, width, width), jnp.bfloat16),
                pltpu.VMEM((2, rows // 2, width, width), jnp.bfloat16),
                pltpu.VMEM((others, rows, width), jnp.float32),
                pltpu.VMEM((others, rows, width), jnp.float32),
                pltpu.VMEM((SUBSTEPS, rows, width), jnp.float32),
                pltpu.VMEM((SUBSTEPS, rows, width), jnp.float32),
                pltpu.VMEM((2, 5, rows, width), jnp.float32),
                pltpu.VMEM((2, rows, width), jnp.float32),
                pltpu.VMEM((rows, width), jnp.float32),
                pltpu.VMEM((rows, width), jnp.float32),
                pltpu.SemaphoreType.DMA((4,)),
                pltpu.SemaphoreType.DMA((nset, 3)),
                pltpu.SemaphoreType.DMA((rows,)),
                pltpu.SemaphoreType.DMA((others,)),
                pltpu.SemaphoreType.DMA((others,)),
                pltpu.SemaphoreType.DMA((2, SUBSTEPS)),
                pltpu.SemaphoreType.DMA((SUBSTEPS,)),
                pltpu.SemaphoreType.DMA((rows,)),
                pltpu.SemaphoreType.DMA((rows,)),
                pltpu.SemaphoreType.DMA(()),
                pltpu.SemaphoreType.DMA(()),
                pltpu.SemaphoreType.REGULAR,
            ],
            compiler_params=pltpu.CompilerParams(collective_id=0, has_side_effects=True, vmem_limit_bytes=60 * 2**20),
        )(tile_water, tile_frac, tile_cell, storage, kappa, inverse, cell_mask, upstream)
        return out[:1], out[1:]

    tiled = P("basin", None, "tile")
    chain = P("basin", "tile", None)
    return jax.shard_map(
        local,
        mesh=mesh,
        in_specs=(tiled, tiled, tiled, chain, chain, P("basin", "tile", None, None), chain, P("basin", "tile")),
        out_specs=(chain, chain),
        check_vma=False,
    )
```

```python
import functools

import jax
import jax.numpy as jnp
from jax import lax
from jax.experimental import pallas as pl
from jax.experimental.pallas import tpu as pltpu
from jax.sharding import PartitionSpec as P

SUBSTEPS = 3
time_step = 0.5
MESH = pl.DeviceIdType.MESH
NT = (((1,), (1,)), ((), ()))
UP, OWN = 0, 1
RATE, LIVE, LINK, FORCE, START = range(5)


def two_terms(value):
    head = value.astype(jnp.bfloat16)
    return head, (value - head.astype(jnp.float32)).astype(jnp.bfloat16)


def iota(shape, axis):
    return lax.broadcasted_iota(jnp.int32, shape, axis)


def kernel(npos, nset, water_hbm, frac_hbm, cell_hbm, storage_hbm, kappa_hbm, inverse_hbm, mask_hbm, upstream_hbm,
           out_ref,
           storage_ref, kappa_ref, mask_ref, upstream_ref, water, frac, cell, inverse, heads, tails, part, arrived, flow, inflow,
           fixed, level_ref, own_ref,
           small_sem, tile_sem, inverse_sem, part_send, part_recv, flow_send, flow_recv, push_send, push_recv, fixed_send, fixed_recv, go):
    rows, width = storage_ref.shape[1], storage_ref.shape[2]
    low = 1 << (width.bit_length() // 2)
    high = width // low
    half = rows // 2
    here = lax.axis_index("basin")
    mine = lax.axis_index("tile")
    odd = lax.rem(here, 2) == 1
    paired = jnp.logical_and(odd, here > 2)
    pushes = jnp.logical_and(jnp.logical_and(jnp.logical_not(odd), here > 1), here < npos - 1)
    to_next = jnp.logical_and(jnp.logical_or(odd, here == 0), here < npos - 1)
    to_second = jnp.logical_and(odd, here < npos - 2)

    barrier = pltpu.get_barrier_semaphore()
    report = here + pushes.astype(jnp.int32)
    for step in range(1, nset):
        pl.semaphore_signal(barrier, inc=1, device_id={"basin": report, "tile": lax.rem(mine + step, nset)}, device_id_type=MESH)

    @pl.when(pushes)
    def _():
        pl.semaphore_signal(barrier, inc=1, device_id={"basin": here + 1}, device_id_type=MESH)

    @pl.when(here > 0)
    def _():
        pl.semaphore_signal(barrier, inc=1, device_id={"basin": here - 1}, device_id_type=MESH)

    @pl.when(paired)
    def _():
        pl.semaphore_signal(barrier, inc=1, device_id={"basin": here - 2}, device_id_type=MESH)

    def tile_loads(order):
        owner = lax.rem(mine + order + 1, nset)
        where = pl.ds(pl.multiple_of(owner * rows, rows), rows)
        return [
            pltpu.make_async_copy(source.at[0, where], target.at[order], tile_sem.at[order, at])
            for at, (source, target) in enumerate(((cell_hbm, cell), (water_hbm, water), (frac_hbm, frac)))]

    for order in range(nset):
        for copy in tile_loads(order):
            copy.start()
    small_loads = []
    for at, (source, target) in enumerate(((storage_hbm, storage_ref), (kappa_hbm, kappa_ref), (mask_hbm, mask_ref), (upstream_hbm, upstream_ref))):
        small_loads.append(pltpu.make_async_copy(source, target, small_sem.at[at]))

    matrix_load = pltpu.make_async_copy(inverse_hbm.at[0], inverse.at[OWN], inverse_sem.at[0])

    def matrix_push(chain):
        return pltpu.make_async_remote_copy(
            src_ref=inverse_hbm.at[0, chain], dst_ref=inverse.at[UP, chain],
            send_sem=push_send.at[chain], recv_sem=push_recv.at[chain],
            device_id={"basin": lax.rem(here + 1, npos)}, device_id_type=MESH)

    def fixed_push():
        return pltpu.make_async_remote_copy(
            src_ref=fixed.at[OWN], dst_ref=fixed.at[UP], send_sem=fixed_send, recv_sem=fixed_recv,
            device_id={"basin": lax.rem(here + 1, npos)}, device_id_type=MESH)

    def part_copy(order):
        return pltpu.make_async_remote_copy(
            src_ref=part.at[order], dst_ref=arrived.at[order],
            send_sem=part_send.at[order], recv_sem=part_recv.at[order],
            device_id={"tile": lax.rem(mine + order + 1, nset)}, device_id_type=MESH)

    def flow_copy(substep, ahead):
        return pltpu.make_async_remote_copy(
            src_ref=flow.at[substep], dst_ref=inflow.at[substep],
            send_sem=flow_send.at[ahead - 1, substep], recv_sem=flow_recv.at[substep],
            device_id={"basin": lax.rem(here + ahead, npos)}, device_id_type=MESH)

    def each_chain(do):
        def one(chain, carry):
            do(chain)
            return carry
        lax.fori_loop(0, rows, one, 0)

    @pl.when(pushes)
    def _():
        pl.semaphore_wait(barrier, 1)
        each_chain(lambda chain: matrix_push(chain).start())

    same = lax.rem(iota((high * rows, low * rows), 0), rows) == lax.rem(iota((high * rows, low * rows), 1), rows)
    spread = (iota((low * rows, width), 0) // rows == lax.rem(iota((low * rows, width), 1), low)).astype(jnp.bfloat16)
    block = iota((rows, width), 1) // low

    def cell_sums(order):
        cells = cell[order]
        upper = (cells // low).astype(jnp.float32).astype(jnp.bfloat16)
        lower = lax.rem(cells, low).astype(jnp.float32).astype(jnp.bfloat16)
        head, tail = two_terms(frac[order] * water[order])
        zero = jnp.zeros_like(head)
        one = jnp.ones_like(head)
        picks = [upper == jnp.bfloat16(at) for at in range(high)]
        left = jnp.concatenate([jnp.where(pick, head, zero) for pick in picks] + [jnp.where(pick, tail, zero) for pick in picks], axis=0)
        right = jnp.concatenate([jnp.where(lower == jnp.bfloat16(at), one, zero) for at in range(low)], axis=0)
        both = lax.dot_general(left, right, NT, preferred_element_type=jnp.float32)
        crossed = jnp.where(same, both[: high * rows] + both[high * rows:], 0.0)
        head, tail = two_terms(crossed)
        packed = jnp.dot(jnp.concatenate([head, tail], axis=0), spread, preferred_element_type=jnp.float32)
        packed = packed[: high * rows] + packed[high * rows:]
        total = packed[:rows]
        for at in range(1, high):
            total = jnp.where(block == at, packed[at * rows:(at + 1) * rows], total)
        return total

    hold = nset - 1 - mine

    def group(order, carry):
        for copy in tile_loads(order):
            copy.wait()
        sums = cell_sums(order)

        @pl.when(order < nset - 1)
        def _():
            part[order] = sums

        @pl.when(order == nset - 1)
        def _():
            own_ref[...] = sums

        @pl.when(jnp.logical_and(order == hold, jnp.logical_not(pushes)))
        def _():
            pl.semaphore_wait(barrier, (nset - 1) * (1 + paired.astype(jnp.int32)) + paired.astype(jnp.int32)
                              + to_next.astype(jnp.int32) + to_second.astype(jnp.int32))

            @pl.when(paired)
            def _():
                pl.semaphore_signal(go, inc=1, device_id={"basin": here - 1}, device_id_type=MESH)

        @pl.when(jnp.logical_and(order == hold, pushes))
        def _():
            pl.semaphore_wait(go, 1)

        for done in reversed(range(nset - 1)):
            @pl.when(jnp.logical_or(jnp.logical_and(order == hold, done <= order), jnp.logical_and(order > hold, done == order)))
            def _():
                part_copy(done).start()

        @pl.when(order == 0)
        def _():
            for copy in small_loads:
                copy.start()
            matrix_load.start()

        return carry

    lax.fori_loop(0, nset, group, 0)

    for copy in small_loads:
        copy.wait()
    row = iota((rows, width), 0)
    links = jnp.zeros((rows, width), jnp.int32)
    for chain in range(rows):
        links = jnp.where(row == chain, upstream_ref[0, chain], links)
    fixed[OWN, LINK] = links.astype(jnp.float32)
    fixed[OWN, LIVE] = mask_ref[0].astype(jnp.float32)
    fixed[OWN, RATE] = kappa_ref[0]
    fixed[OWN, START] = storage_ref[0]
    level_ref[OWN] = storage_ref[0]

    @pl.when(here == 0)
    def _():
        inflow[...] = jnp.zeros_like(inflow)

    def prepare(slot, ready):
        def one(chain, carry):
            ready(chain)
            head, tail = two_terms(inverse[slot, chain].T)
            heads[slot, chain] = head
            tails[slot, chain] = tail
            return carry

        def rest(chain, carry):
            ready(chain)
            return carry
        lax.fori_loop(0, half, one, 0)
        lax.fori_loop(half, rows, rest, 0)

    matrix_load.wait()
    prepare(OWN, lambda chain: None)

    picked = [lax.rem(iota((2 * half, width), 0), half) == chain for chain in range(half)]

    def product(slot, vector):
        head = vector.astype(jnp.bfloat16).astype(jnp.float32)
        tail = vector - head
        left = jnp.concatenate([head[:half], tail[:half]], axis=0).astype(jnp.bfloat16)
        first = jnp.zeros((2 * half, width), jnp.float32)
        second = jnp.zeros((2 * half, width), jnp.float32)
        reduced = []
        for chain in range(rows - half):
            if chain < half:
                single = jnp.where(picked[chain], left, jnp.zeros_like(left))
                first += jnp.dot(single, heads[slot, chain], preferred_element_type=jnp.float32)
                second += jnp.dot(single, tails[slot, chain], preferred_element_type=jnp.float32)
            other = half + chain
            reduced.append(jnp.sum(inverse[slot, other] * vector[other:other + 1], axis=1)[None])
        total = first + second
        return jnp.concatenate([total[:half] + total[half:]] + reduced, axis=0)

    runoff = own_ref[...]
    for order in range(nset - 1):
        part_copy(order).wait_recv()
        runoff = runoff + arrived[order]
    fixed[OWN, FORCE] = time_step * runoff

    @pl.when(pushes)
    def _():
        fixed_push().start()

    @pl.when(paired)
    def _():
        prepare(UP, lambda chain: matrix_push(chain).wait_recv())
        fixed_push().wait_recv()
        level_ref[UP] = fixed[UP, START]

    def turn(count, carry):
        slot = jnp.where(paired, lax.rem(count, 2), OWN)
        substep = jnp.where(paired, count // 2, count)
        leads = jnp.logical_or(jnp.logical_not(paired), slot == UP)

        @pl.when(jnp.logical_and(leads, here > 0))
        def _():
            flow_copy(substep, 1).wait_recv()

        came = inflow[jnp.where(leads, substep, SUBSTEPS)]
        links = fixed[slot, LINK]
        incoming = jnp.broadcast_to(came[:1], (rows, width))
        for chain in range(1, rows):
            incoming = jnp.where(links == float(chain), jnp.broadcast_to(came[chain:chain + 1], (rows, width)), incoming)
        wet = fixed[slot, LIVE] * product(slot, level_ref[slot] + fixed[slot, FORCE] + incoming)
        outflow = fixed[slot, RATE] * wet

        @pl.when(slot == OWN)
        def _():
            flow[substep] = outflow

            @pl.when(to_second)
            def _():
                flow_copy(substep, 2).start()

            @pl.when(to_next)
            def _():
                flow_copy(substep, 1).start()

            out_ref[0] = wet - outflow
            out_ref[1] = outflow

        @pl.when(slot == UP)
        def _():
            inflow[SUBSTEPS] = outflow

        level_ref[slot] = wet - outflow
        return carry

    lax.fori_loop(0, jnp.where(paired, 2 * SUBSTEPS, SUBSTEPS), turn, 0)

    for order in range(nset - 1):
        part_copy(order).wait_send()

    @pl.when(pushes)
    def _():
        each_chain(lambda chain: matrix_push(chain).wait_send())
        fixed_push().wait_send()

    @pl.when(to_next)
    def _():
        for substep in range(SUBSTEPS):
            flow_copy(substep, 1).wait_send()

    @pl.when(to_second)
    def _():
        for substep in range(SUBSTEPS):
            flow_copy(substep, 2).wait_send()


def solution(mesh):
    npos, nset = mesh.shape["basin"], mesh.shape["tile"]

    def local(tile_water, tile_frac, tile_cell, storage, kappa, inverse, cell_mask, upstream):
        rows, width = storage.shape[1:]
        tiles = tile_water.shape[2]
        anywhere = pl.BlockSpec(memory_space=pltpu.HBM)
        vmem = pl.BlockSpec(memory_space=pltpu.VMEM)
        others = max(nset - 1, 1)
        out = pl.pallas_call(
            functools.partial(kernel, npos, nset),
            out_shape=pltpu.VMEM((2, rows, width), jnp.float32),
            in_specs=[anywhere] * 8,
            out_specs=vmem,
            scratch_shapes=[
                pltpu.VMEM(storage.shape, jnp.float32),
                pltpu.VMEM(kappa.shape, jnp.float32),
                pltpu.VMEM(cell_mask.shape, jnp.int32),
                pltpu.SMEM(upstream.shape, jnp.int32),
                pltpu.VMEM((nset, rows, tiles), jnp.float32),
                pltpu.VMEM((nset, rows, tiles), jnp.float32),
                pltpu.VMEM((nset, rows, tiles), jnp.int32),
                pltpu.VMEM((2, rows, width, width), jnp.float32),
                pltpu.VMEM((2, rows // 2, width, width), jnp.bfloat16),
                pltpu.VMEM((2, rows // 2, width, width), jnp.bfloat16),
                pltpu.VMEM((others, rows, width), jnp.float32),
                pltpu.VMEM((others, rows, width), jnp.float32),
                pltpu.VMEM((SUBSTEPS, rows, width), jnp.float32),
                pltpu.VMEM((SUBSTEPS + 1, rows, width), jnp.float32),
                pltpu.VMEM((2, 5, rows, width), jnp.float32),
                pltpu.VMEM((2, rows, width), jnp.float32),
                pltpu.VMEM((rows, width), jnp.float32),
                pltpu.SemaphoreType.DMA((4,)),
                pltpu.SemaphoreType.DMA((nset, 3)),
                pltpu.SemaphoreType.DMA((1,)),
                pltpu.SemaphoreType.DMA((others,)),
                pltpu.SemaphoreType.DMA((others,)),
                pltpu.SemaphoreType.DMA((2, SUBSTEPS)),
                pltpu.SemaphoreType.DMA((SUBSTEPS,)),
                pltpu.SemaphoreType.DMA((rows,)),
                pltpu.SemaphoreType.DMA((rows,)),
                pltpu.SemaphoreType.DMA(()),
                pltpu.SemaphoreType.DMA(()),
                pltpu.SemaphoreType.REGULAR,
            ],
            compiler_params=pltpu.CompilerParams(collective_id=0, has_side_effects=True, vmem_limit_bytes=60 * 2**20),
        )(tile_water, tile_frac, tile_cell, storage, kappa, inverse, cell_mask, upstream)
        return out[:1], out[1:]

    tiled = P("basin", None, "tile")
    chain = P("basin", "tile", None)
    return jax.shard_map(
        local,
        mesh=mesh,
        in_specs=(tiled, tiled, tiled, chain, chain, P("basin", "tile", None, None), chain, P("basin", "tile")),
        out_specs=(chain, chain),
        check_vma=False,
    )
```

```python
import functools

import jax
import jax.numpy as jnp
from jax import lax
from jax.experimental import pallas as pl
from jax.experimental.pallas import tpu as pltpu
from jax.sharding import PartitionSpec as P

SUBSTEPS = 3
time_step = 0.5
MESH = pl.DeviceIdType.MESH
NT = (((1,), (1,)), ((), ()))
UP, OWN = 0, 1
RATE, LIVE, LINK, FORCE, START = range(5)


def two_terms(value):
    head = value.astype(jnp.bfloat16)
    return head, (value - head.astype(jnp.float32)).astype(jnp.bfloat16)


def iota(shape, axis):
    return lax.broadcasted_iota(jnp.int32, shape, axis)


def kernel(npos, nset, water_hbm, frac_hbm, cell_hbm, storage_hbm, kappa_hbm, inverse_hbm, mask_hbm, upstream_hbm,
           out_ref,
           storage_ref, kappa_ref, mask_ref, upstream_ref, water, frac, cell, inverse, heads, tails, part, arrived, flow, inflow,
           fixed, level_ref, own_ref,
           small_sem, tile_sem, inverse_sem, part_send, part_recv, flow_send, flow_recv, push_send, push_recv, fixed_send, fixed_recv, go):
    rows, width = storage_ref.shape[1], storage_ref.shape[2]
    low = 1 << (width.bit_length() // 2)
    high = width // low
    half = rows // 2
    here = lax.axis_index("basin")
    mine = lax.axis_index("tile")
    odd = lax.rem(here, 2) == 1
    paired = jnp.logical_and(odd, here > 2)
    pushes = jnp.logical_and(jnp.logical_and(jnp.logical_not(odd), here > 1), here < npos - 1)
    to_next = jnp.logical_and(jnp.logical_or(odd, here == 0), here < npos - 1)
    to_second = jnp.logical_and(odd, here < npos - 2)

    def owner_of(order):
        return jnp.where(order == nset - 1, mine, order + (order >= mine).astype(jnp.int32))

    def tile_loads(order):
        owner = owner_of(order)
        where = pl.ds(pl.multiple_of(owner * rows, rows), rows)
        return [
            pltpu.make_async_copy(source.at[0, where], target.at[order], tile_sem.at[order, at])
            for at, (source, target) in enumerate(((cell_hbm, cell), (water_hbm, water), (frac_hbm, frac)))]

    for copy in tile_loads(0):
        copy.start()

    barrier = pltpu.get_barrier_semaphore()
    report = here + pushes.astype(jnp.int32)
    for step in range(1, nset):
        pl.semaphore_signal(barrier, inc=1, device_id={"basin": report, "tile": lax.rem(mine + step, nset)}, device_id_type=MESH)

    @pl.when(pushes)
    def _():
        pl.semaphore_signal(barrier, inc=1, device_id={"basin": here + 1}, device_id_type=MESH)

    @pl.when(here > 0)
    def _():
        pl.semaphore_signal(barrier, inc=1, device_id={"basin": here - 1}, device_id_type=MESH)

    @pl.when(paired)
    def _():
        pl.semaphore_signal(barrier, inc=1, device_id={"basin": here - 2}, device_id_type=MESH)

    for order in range(1, nset):
        for copy in tile_loads(order):
            copy.start()
    small_loads = []
    for at, (source, target) in enumerate(((storage_hbm, storage_ref), (kappa_hbm, kappa_ref), (mask_hbm, mask_ref), (upstream_hbm, upstream_ref))):
        small_loads.append(pltpu.make_async_copy(source, target, small_sem.at[at]))

    matrix_load = pltpu.make_async_copy(inverse_hbm.at[0], inverse.at[OWN], inverse_sem.at[0])

    def matrix_push(chain):
        return pltpu.make_async_remote_copy(
            src_ref=inverse_hbm.at[0, chain], dst_ref=inverse.at[UP, chain],
            send_sem=push_send.at[chain], recv_sem=push_recv.at[chain],
            device_id={"basin": lax.rem(here + 1, npos)}, device_id_type=MESH)

    def fixed_push():
        return pltpu.make_async_remote_copy(
            src_ref=fixed.at[OWN], dst_ref=fixed.at[UP], send_sem=fixed_send, recv_sem=fixed_recv,
            device_id={"basin": lax.rem(here + 1, npos)}, device_id_type=MESH)

    def part_copy(order):
        owner = owner_of(order)
        slot = mine - (mine > owner).astype(jnp.int32)
        return pltpu.make_async_remote_copy(
            src_ref=part.at[order], dst_ref=arrived.at[slot],
            send_sem=part_send.at[order], recv_sem=part_recv.at[slot],
            device_id={"tile": owner}, device_id_type=MESH)

    def part_arrival(slot):
        return pltpu.make_async_remote_copy(
            src_ref=part.at[slot], dst_ref=arrived.at[slot],
            send_sem=part_send.at[slot], recv_sem=part_recv.at[slot],
            device_id={"tile": owner_of(slot)}, device_id_type=MESH)

    def flow_copy(substep, ahead):
        return pltpu.make_async_remote_copy(
            src_ref=flow.at[substep], dst_ref=inflow.at[substep],
            send_sem=flow_send.at[ahead - 1, substep], recv_sem=flow_recv.at[substep],
            device_id={"basin": lax.rem(here + ahead, npos)}, device_id_type=MESH)

    def each_chain(do):
        def one(chain, carry):
            do(chain)
            return carry
        lax.fori_loop(0, rows, one, 0)

    @pl.when(pushes)
    def _():
        pl.semaphore_wait(barrier, 1)
        each_chain(lambda chain: matrix_push(chain).start())

    same = lax.rem(iota((high * rows, low * rows), 0), rows) == lax.rem(iota((high * rows, low * rows), 1), rows)
    spread = (iota((low * rows, width), 0) // rows == lax.rem(iota((low * rows, width), 1), low)).astype(jnp.bfloat16)
    block = iota((rows, width), 1) // low

    def cell_sums(order):
        cells = cell[order]
        upper = (cells // low).astype(jnp.float32).astype(jnp.bfloat16)
        lower = lax.rem(cells, low).astype(jnp.float32).astype(jnp.bfloat16)
        head, tail = two_terms(frac[order] * water[order])
        zero = jnp.zeros_like(head)
        one = jnp.ones_like(head)
        picks = [upper == jnp.bfloat16(at) for at in range(high)]
        left = jnp.concatenate([jnp.where(pick, head, zero) for pick in picks] + [jnp.where(pick, tail, zero) for pick in picks], axis=0)
        right = jnp.concatenate([jnp.where(lower == jnp.bfloat16(at), one, zero) for at in range(low)], axis=0)
        both = lax.dot_general(left, right, NT, preferred_element_type=jnp.float32)
        crossed = jnp.where(same, both[: high * rows] + both[high * rows:], 0.0)
        head, tail = two_terms(crossed)
        packed = jnp.dot(jnp.concatenate([head, tail], axis=0), spread, preferred_element_type=jnp.float32)
        packed = packed[: high * rows] + packed[high * rows:]
        total = packed[:rows]
        for at in range(1, high):
            total = jnp.where(block == at, packed[at * rows:(at + 1) * rows], total)
        return total

    hold = jnp.maximum(nset - 1 - 2 * mine, 0)

    def group(order, carry):
        for copy in tile_loads(order):
            copy.wait()
        sums = cell_sums(order)

        @pl.when(order < nset - 1)
        def _():
            part[order] = sums

        @pl.when(order == nset - 1)
        def _():
            own_ref[...] = sums

        @pl.when(jnp.logical_and(order == hold, jnp.logical_not(pushes)))
        def _():
            pl.semaphore_wait(barrier, (nset - 1) * (1 + paired.astype(jnp.int32)) + paired.astype(jnp.int32)
                              + to_next.astype(jnp.int32) + to_second.astype(jnp.int32))

            @pl.when(paired)
            def _():
                pl.semaphore_signal(go, inc=1, device_id={"basin": here - 1}, device_id_type=MESH)

        @pl.when(jnp.logical_and(order == hold, pushes))
        def _():
            pl.semaphore_wait(go, 1)

        for done in reversed(range(nset - 1)):
            @pl.when(jnp.logical_or(jnp.logical_and(order == hold, done <= order), jnp.logical_and(order > hold, done == order)))
            def _():
                part_copy(done).start()

        @pl.when(order == 0)
        def _():
            for copy in small_loads:
                copy.start()
            matrix_load.start()

        return carry

    lax.fori_loop(0, nset, group, 0)

    for copy in small_loads:
        copy.wait()
    row = iota((rows, width), 0)
    links = jnp.zeros((rows, width), jnp.int32)
    for chain in range(rows):
        links = jnp.where(row == chain, upstream_ref[0, chain], links)
    fixed[OWN, LINK] = links.astype(jnp.float32)
    fixed[OWN, LIVE] = mask_ref[0].astype(jnp.float32)
    fixed[OWN, RATE] = kappa_ref[0]
    fixed[OWN, START] = storage_ref[0]
    level_ref[OWN] = storage_ref[0]

    @pl.when(here == 0)
    def _():
        inflow[...] = jnp.zeros_like(inflow)

    def prepare(slot, ready):
        def one(chain, carry):
            ready(chain)
            head, tail = two_terms(inverse[slot, chain].T)
            heads[slot, chain] = head
            tails[slot, chain] = tail
            return carry

        def rest(chain, carry):
            ready(chain)
            return carry
        lax.fori_loop(0, half, one, 0)
        lax.fori_loop(half, rows, rest, 0)

    matrix_load.wait()
    prepare(OWN, lambda chain: None)

    picked = [lax.rem(iota((2 * half, width), 0), half) == chain for chain in range(half)]

    def product(slot, vector):
        head = vector.astype(jnp.bfloat16).astype(jnp.float32)
        tail = vector - head
        left = jnp.concatenate([head[:half], tail[:half]], axis=0).astype(jnp.bfloat16)
        first = jnp.zeros((2 * half, width), jnp.float32)
        second = jnp.zeros((2 * half, width), jnp.float32)
        reduced = []
        for chain in range(rows - half):
            if chain < half:
                single = jnp.where(picked[chain], left, jnp.zeros_like(left))
                first += jnp.dot(single, heads[slot, chain], preferred_element_type=jnp.float32)
                second += jnp.dot(single, tails[slot, chain], preferred_element_type=jnp.float32)
            other = half + chain
            reduced.append(jnp.sum(inverse[slot, other] * vector[other:other + 1], axis=1)[None])
        total = first + second
        return jnp.concatenate([total[:half] + total[half:]] + reduced, axis=0)

    runoff = own_ref[...]
    for order in range(nset - 1):
        part_arrival(order).wait_recv()
        runoff = runoff + arrived[order]
    fixed[OWN, FORCE] = time_step * runoff

    @pl.when(pushes)
    def _():
        fixed_push().start()

    @pl.when(paired)
    def _():
        prepare(UP, lambda chain: matrix_push(chain).wait_recv())
        fixed_push().wait_recv()
        level_ref[UP] = fixed[UP, START]

    def turn(count, carry):
        slot = jnp.where(paired, lax.rem(count, 2), OWN)
        substep = jnp.where(paired, count // 2, count)
        leads = jnp.logical_or(jnp.logical_not(paired), slot == UP)

        @pl.when(jnp.logical_and(leads, here > 0))
        def _():
            flow_copy(substep, 1).wait_recv()

        came = inflow[jnp.where(leads, substep, SUBSTEPS)]
        links = fixed[slot, LINK]
        incoming = jnp.broadcast_to(came[:1], (rows, width))
        for chain in range(1, rows):
            incoming = jnp.where(links == float(chain), jnp.broadcast_to(came[chain:chain + 1], (rows, width)), incoming)
        wet = fixed[slot, LIVE] * product(slot, level_ref[slot] + fixed[slot, FORCE] + incoming)
        outflow = fixed[slot, RATE] * wet

        @pl.when(slot == OWN)
        def _():
            flow[substep] = outflow

            @pl.when(to_second)
            def _():
                flow_copy(substep, 2).start()

            @pl.when(to_next)
            def _():
                flow_copy(substep, 1).start()

            out_ref[0] = wet - outflow
            out_ref[1] = outflow

        @pl.when(slot == UP)
        def _():
            inflow[SUBSTEPS] = outflow

        level_ref[slot] = wet - outflow
        return carry

    lax.fori_loop(0, jnp.where(paired, 2 * SUBSTEPS, SUBSTEPS), turn, 0)

    for order in range(nset - 1):
        part_copy(order).wait_send()

    @pl.when(pushes)
    def _():
        each_chain(lambda chain: matrix_push(chain).wait_send())
        fixed_push().wait_send()

    @pl.when(to_next)
    def _():
        for substep in range(SUBSTEPS):
            flow_copy(substep, 1).wait_send()

    @pl.when(to_second)
    def _():
        for substep in range(SUBSTEPS):
            flow_copy(substep, 2).wait_send()


def solution(mesh):
    npos, nset = mesh.shape["basin"], mesh.shape["tile"]

    def local(tile_water, tile_frac, tile_cell, storage, kappa, inverse, cell_mask, upstream):
        rows, width = storage.shape[1:]
        tiles = tile_water.shape[2]
        anywhere = pl.BlockSpec(memory_space=pltpu.HBM)
        vmem = pl.BlockSpec(memory_space=pltpu.VMEM)
        others = max(nset - 1, 1)
        out = pl.pallas_call(
            functools.partial(kernel, npos, nset),
            out_shape=pltpu.VMEM((2, rows, width), jnp.float32),
            in_specs=[anywhere] * 8,
            out_specs=vmem,
            scratch_shapes=[
                pltpu.VMEM(storage.shape, jnp.float32),
                pltpu.VMEM(kappa.shape, jnp.float32),
                pltpu.VMEM(cell_mask.shape, jnp.int32),
                pltpu.SMEM(upstream.shape, jnp.int32),
                pltpu.VMEM((nset, rows, tiles), jnp.float32),
                pltpu.VMEM((nset, rows, tiles), jnp.float32),
                pltpu.VMEM((nset, rows, tiles), jnp.int32),
                pltpu.VMEM((2, rows, width, width), jnp.float32),
                pltpu.VMEM((2, rows // 2, width, width), jnp.bfloat16),
                pltpu.VMEM((2, rows // 2, width, width), jnp.bfloat16),
                pltpu.VMEM((others, rows, width), jnp.float32),
                pltpu.VMEM((others, rows, width), jnp.float32),
                pltpu.VMEM((SUBSTEPS, rows, width), jnp.float32),
                pltpu.VMEM((SUBSTEPS + 1, rows, width), jnp.float32),
                pltpu.VMEM((2, 5, rows, width), jnp.float32),
                pltpu.VMEM((2, rows, width), jnp.float32),
                pltpu.VMEM((rows, width), jnp.float32),
                pltpu.SemaphoreType.DMA((4,)),
                pltpu.SemaphoreType.DMA((nset, 3)),
                pltpu.SemaphoreType.DMA((1,)),
                pltpu.SemaphoreType.DMA((others,)),
                pltpu.SemaphoreType.DMA((others,)),
                pltpu.SemaphoreType.DMA((2, SUBSTEPS)),
                pltpu.SemaphoreType.DMA((SUBSTEPS,)),
                pltpu.SemaphoreType.DMA((rows,)),
                pltpu.SemaphoreType.DMA((rows,)),
                pltpu.SemaphoreType.DMA(()),
                pltpu.SemaphoreType.DMA(()),
                pltpu.SemaphoreType.REGULAR,
            ],
            compiler_params=pltpu.CompilerParams(collective_id=0, has_side_effects=True, vmem_limit_bytes=60 * 2**20),
        )(tile_water, tile_frac, tile_cell, storage, kappa, inverse, cell_mask, upstream)
        return out[:1], out[1:]

    tiled = P("basin", None, "tile")
    chain = P("basin", "tile", None)
    return jax.shard_map(
        local,
        mesh=mesh,
        in_specs=(tiled, tiled, tiled, chain, chain, P("basin", "tile", None, None), chain, P("basin", "tile")),
        out_specs=(chain, chain),
        check_vma=False,
    )
```

```python
import functools

import jax
import jax.numpy as jnp
from jax import lax
from jax.experimental import pallas as pl
from jax.experimental.pallas import tpu as pltpu
from jax.sharding import PartitionSpec as P

SUBSTEPS = 3
time_step = 0.5
MESH = pl.DeviceIdType.MESH
NT = (((1,), (1,)), ((), ()))
UP, OWN = 0, 1
RATE, LIVE, LINK, FORCE, START = range(5)


def two_terms(value):
    head = value.astype(jnp.bfloat16)
    return head, (value - head.astype(jnp.float32)).astype(jnp.bfloat16)


def iota(shape, axis):
    return lax.broadcasted_iota(jnp.int32, shape, axis)


def kernel(npos, nset, water_hbm, frac_hbm, cell_hbm, storage_hbm, kappa_hbm, inverse_hbm, mask_hbm, upstream_hbm,
           out_ref,
           storage_ref, kappa_ref, mask_ref, upstream_ref, water, frac, cell, inverse, heads, tails, part, arrived, flow, inflow,
           fixed, level_ref, own_ref,
           small_sem, tile_sem, inverse_sem, part_send, part_recv, flow_send, flow_recv, push_send, push_recv, fixed_send, fixed_recv, go):
    rows, width = storage_ref.shape[1], storage_ref.shape[2]
    half = rows // 2
    here = lax.axis_index("basin")
    mine = lax.axis_index("tile")
    odd = lax.rem(here, 2) == 1
    paired = jnp.logical_and(odd, here > 2)
    pushes = jnp.logical_and(jnp.logical_and(jnp.logical_not(odd), here > 1), here < npos - 1)
    to_next = jnp.logical_and(jnp.logical_or(odd, here == 0), here < npos - 1)
    to_second = jnp.logical_and(odd, here < npos - 2)

    def owner_of(order):
        return jnp.where(order == nset - 1, mine, order + (order >= mine).astype(jnp.int32))

    def tile_loads(order):
        owner = owner_of(order)
        where = pl.ds(pl.multiple_of(owner * rows, rows), rows)
        return [
            pltpu.make_async_copy(source.at[0, where], target.at[order], tile_sem.at[order, at])
            for at, (source, target) in enumerate(((cell_hbm, cell), (water_hbm, water), (frac_hbm, frac)))]

    for copy in tile_loads(0):
        copy.start()

    barrier = pltpu.get_barrier_semaphore()
    report = here + pushes.astype(jnp.int32)
    for step in range(1, nset):
        pl.semaphore_signal(barrier, inc=1, device_id={"basin": report, "tile": lax.rem(mine + step, nset)}, device_id_type=MESH)

    @pl.when(pushes)
    def _():
        pl.semaphore_signal(barrier, inc=1, device_id={"basin": here + 1}, device_id_type=MESH)

    @pl.when(here > 0)
    def _():
        pl.semaphore_signal(barrier, inc=1, device_id={"basin": here - 1}, device_id_type=MESH)

    @pl.when(paired)
    def _():
        pl.semaphore_signal(barrier, inc=1, device_id={"basin": here - 2}, device_id_type=MESH)

    for order in range(1, nset):
        for copy in tile_loads(order):
            copy.start()
    small_loads = []
    for at, (source, target) in enumerate(((storage_hbm, storage_ref), (kappa_hbm, kappa_ref), (mask_hbm, mask_ref), (upstream_hbm, upstream_ref))):
        small_loads.append(pltpu.make_async_copy(source, target, small_sem.at[at]))

    matrix_load = pltpu.make_async_copy(inverse_hbm.at[0], inverse.at[OWN], inverse_sem.at[0])

    def matrix_push(chain):
        return pltpu.make_async_remote_copy(
            src_ref=inverse_hbm.at[0, chain], dst_ref=inverse.at[UP, chain],
            send_sem=push_send.at[chain], recv_sem=push_recv.at[chain],
            device_id={"basin": lax.rem(here + 1, npos)}, device_id_type=MESH)

    def fixed_push():
        return pltpu.make_async_remote_copy(
            src_ref=fixed.at[OWN], dst_ref=fixed.at[UP], send_sem=fixed_send, recv_sem=fixed_recv,
            device_id={"basin": lax.rem(here + 1, npos)}, device_id_type=MESH)

    def part_copy(order):
        owner = owner_of(order)
        slot = mine - (mine > owner).astype(jnp.int32)
        return pltpu.make_async_remote_copy(
            src_ref=part.at[order], dst_ref=arrived.at[slot],
            send_sem=part_send.at[order], recv_sem=part_recv.at[slot],
            device_id={"tile": owner}, device_id_type=MESH)

    def part_arrival(slot):
        return pltpu.make_async_remote_copy(
            src_ref=part.at[slot], dst_ref=arrived.at[slot],
            send_sem=part_send.at[slot], recv_sem=part_recv.at[slot],
            device_id={"tile": owner_of(slot)}, device_id_type=MESH)

    def flow_copy(substep, ahead):
        return pltpu.make_async_remote_copy(
            src_ref=flow.at[substep], dst_ref=inflow.at[substep],
            send_sem=flow_send.at[ahead - 1, substep], recv_sem=flow_recv.at[substep],
            device_id={"basin": lax.rem(here + ahead, npos)}, device_id_type=MESH)

    def each_chain(do):
        def one(chain, carry):
            do(chain)
            return carry
        lax.fori_loop(0, rows, one, 0)

    @pl.when(pushes)
    def _():
        pl.semaphore_wait(barrier, 1)
        each_chain(lambda chain: matrix_push(chain).start())

    lane = lax.rem(iota((rows, width), 1), rows)
    row = iota((rows, width), 0)

    def cell_sums(order):
        cells = cell[order]
        shift = lax.rem(cells - iota(cells.shape, 0) + rows, rows).astype(jnp.float32).astype(jnp.bfloat16)
        upper = (cells // rows).astype(jnp.float32).astype(jnp.bfloat16)
        head, tail = two_terms(frac[order] * water[order])
        zero = jnp.zeros_like(head)
        one = jnp.ones_like(head)
        picks = [shift == jnp.bfloat16(at) for at in range(rows)]
        left = jnp.concatenate([jnp.where(pick, head, zero) for pick in picks] + [jnp.where(pick, tail, zero) for pick in picks], axis=0)
        right = jnp.concatenate([jnp.where(upper == jnp.bfloat16(at), one, zero) for at in range(width // rows)], axis=0)
        both = lax.dot_general(left, right, NT, preferred_element_type=jnp.float32)
        terms = []
        for at in range(rows):
            start = at * rows
            single = jnp.where(lane == row, both[start:start + rows] + both[rows * rows + start:rows * rows + start + rows], 0.0)
            terms.append(pltpu.roll(single, at, 1) if at else single)
        while len(terms) > 1:
            terms = [sum(terms[at:at + 2][1:], terms[at]) for at in range(0, len(terms), 2)]
        return jnp.where(lane < row, pltpu.roll(terms[0], width - rows, 1), terms[0])

    hold = jnp.maximum(nset - 1 - 2 * mine, 0)

    def group(order, carry):
        for copy in tile_loads(order):
            copy.wait()
        sums = cell_sums(order)

        @pl.when(order < nset - 1)
        def _():
            part[order] = sums

        @pl.when(order == nset - 1)
        def _():
            own_ref[...] = sums

        @pl.when(jnp.logical_and(order == hold, jnp.logical_not(pushes)))
        def _():
            pl.semaphore_wait(barrier, (nset - 1) * (1 + paired.astype(jnp.int32)) + paired.astype(jnp.int32)
                              + to_next.astype(jnp.int32) + to_second.astype(jnp.int32))

            @pl.when(paired)
            def _():
                pl.semaphore_signal(go, inc=1, device_id={"basin": here - 1}, device_id_type=MESH)

        @pl.when(jnp.logical_and(order == hold, pushes))
        def _():
            pl.semaphore_wait(go, 1)

        for done in reversed(range(nset - 1)):
            @pl.when(jnp.logical_or(jnp.logical_and(order == hold, done <= order), jnp.logical_and(order > hold, done == order)))
            def _():
                part_copy(done).start()

        @pl.when(order == 0)
        def _():
            for copy in small_loads:
                copy.start()
            matrix_load.start()

        return carry

    lax.fori_loop(0, nset, group, 0)

    for copy in small_loads:
        copy.wait()
    links = jnp.zeros((rows, width), jnp.int32)
    for chain in range(rows):
        links = jnp.where(row == chain, upstream_ref[0, chain], links)
    fixed[OWN, LINK] = links.astype(jnp.float32)
    fixed[OWN, LIVE] = mask_ref[0].astype(jnp.float32)
    fixed[OWN, RATE] = kappa_ref[0]
    fixed[OWN, START] = storage_ref[0]
    level_ref[OWN] = storage_ref[0]

    @pl.when(here == 0)
    def _():
        inflow[...] = jnp.zeros_like(inflow)

    def prepare(slot, ready):
        def one(chain, carry):
            ready(chain)
            head, tail = two_terms(inverse[slot, chain].T)
            heads[slot, chain] = head
            tails[slot, chain] = tail
            return carry

        def rest(chain, carry):
            ready(chain)
            return carry
        lax.fori_loop(0, half, one, 0)
        lax.fori_loop(half, rows, rest, 0)

    matrix_load.wait()
    prepare(OWN, lambda chain: None)

    picked = [lax.rem(iota((2 * half, width), 0), half) == chain for chain in range(half)]

    def product(slot, vector):
        head = vector.astype(jnp.bfloat16).astype(jnp.float32)
        tail = vector - head
        left = jnp.concatenate([head[:half], tail[:half]], axis=0).astype(jnp.bfloat16)
        first = jnp.zeros((2 * half, width), jnp.float32)
        second = jnp.zeros((2 * half, width), jnp.float32)
        reduced = []
        for chain in range(rows - half):
            if chain < half:
                single = jnp.where(picked[chain], left, jnp.zeros_like(left))
                first += jnp.dot(single, heads[slot, chain], preferred_element_type=jnp.float32)
                second += jnp.dot(single, tails[slot, chain], preferred_element_type=jnp.float32)
            other = half + chain
            reduced.append(jnp.sum(inverse[slot, other] * vector[other:other + 1], axis=1)[None])
        total = first + second
        return jnp.concatenate([total[:half] + total[half:]] + reduced, axis=0)

    runoff = own_ref[...]
    for order in range(nset - 1):
        part_arrival(order).wait_recv()
        runoff = runoff + arrived[order]
    fixed[OWN, FORCE] = time_step * runoff

    @pl.when(pushes)
    def _():
        fixed_push().start()

    @pl.when(paired)
    def _():
        prepare(UP, lambda chain: matrix_push(chain).wait_recv())
        fixed_push().wait_recv()
        level_ref[UP] = fixed[UP, START]

    def turn(count, carry):
        slot = jnp.where(paired, lax.rem(count, 2), OWN)
        substep = jnp.where(paired, count // 2, count)
        leads = jnp.logical_or(jnp.logical_not(paired), slot == UP)

        @pl.when(jnp.logical_and(leads, here > 0))
        def _():
            flow_copy(substep, 1).wait_recv()

        came = inflow[jnp.where(leads, substep, SUBSTEPS)]
        links = fixed[slot, LINK]
        incoming = jnp.broadcast_to(came[:1], (rows, width))
        for chain in range(1, rows):
            incoming = jnp.where(links == float(chain), jnp.broadcast_to(came[chain:chain + 1], (rows, width)), incoming)
        wet = fixed[slot, LIVE] * product(slot, level_ref[slot] + fixed[slot, FORCE] + incoming)
        outflow = fixed[slot, RATE] * wet

        @pl.when(slot == OWN)
        def _():
            flow[substep] = outflow

            @pl.when(to_second)
            def _():
                flow_copy(substep, 2).start()

            @pl.when(to_next)
            def _():
                flow_copy(substep, 1).start()

            out_ref[0] = wet - outflow
            out_ref[1] = outflow

        @pl.when(slot == UP)
        def _():
            inflow[SUBSTEPS] = outflow

        level_ref[slot] = wet - outflow
        return carry

    lax.fori_loop(0, jnp.where(paired, 2 * SUBSTEPS, SUBSTEPS), turn, 0)

    for order in range(nset - 1):
        part_copy(order).wait_send()

    @pl.when(pushes)
    def _():
        each_chain(lambda chain: matrix_push(chain).wait_send())
        fixed_push().wait_send()

    @pl.when(to_next)
    def _():
        for substep in range(SUBSTEPS):
            flow_copy(substep, 1).wait_send()

    @pl.when(to_second)
    def _():
        for substep in range(SUBSTEPS):
            flow_copy(substep, 2).wait_send()


def solution(mesh):
    npos, nset = mesh.shape["basin"], mesh.shape["tile"]

    def local(tile_water, tile_frac, tile_cell, storage, kappa, inverse, cell_mask, upstream):
        rows, width = storage.shape[1:]
        tiles = tile_water.shape[2]
        anywhere = pl.BlockSpec(memory_space=pltpu.HBM)
        vmem = pl.BlockSpec(memory_space=pltpu.VMEM)
        others = max(nset - 1, 1)
        out = pl.pallas_call(
            functools.partial(kernel, npos, nset),
            out_shape=pltpu.VMEM((2, rows, width), jnp.float32),
            in_specs=[anywhere] * 8,
            out_specs=vmem,
            scratch_shapes=[
                pltpu.VMEM(storage.shape, jnp.float32),
                pltpu.VMEM(kappa.shape, jnp.float32),
                pltpu.VMEM(cell_mask.shape, jnp.int32),
                pltpu.SMEM(upstream.shape, jnp.int32),
                pltpu.VMEM((nset, rows, tiles), jnp.float32),
                pltpu.VMEM((nset, rows, tiles), jnp.float32),
                pltpu.VMEM((nset, rows, tiles), jnp.int32),
                pltpu.VMEM((2, rows, width, width), jnp.float32),
                pltpu.VMEM((2, rows // 2, width, width), jnp.bfloat16),
                pltpu.VMEM((2, rows // 2, width, width), jnp.bfloat16),
                pltpu.VMEM((others, rows, width), jnp.float32),
                pltpu.VMEM((others, rows, width), jnp.float32),
                pltpu.VMEM((SUBSTEPS, rows, width), jnp.float32),
                pltpu.VMEM((SUBSTEPS + 1, rows, width), jnp.float32),
                pltpu.VMEM((2, 5, rows, width), jnp.float32),
                pltpu.VMEM((2, rows, width), jnp.float32),
                pltpu.VMEM((rows, width), jnp.float32),
                pltpu.SemaphoreType.DMA((4,)),
                pltpu.SemaphoreType.DMA((nset, 3)),
                pltpu.SemaphoreType.DMA((1,)),
                pltpu.SemaphoreType.DMA((others,)),
                pltpu.SemaphoreType.DMA((others,)),
                pltpu.SemaphoreType.DMA((2, SUBSTEPS)),
                pltpu.SemaphoreType.DMA((SUBSTEPS,)),
                pltpu.SemaphoreType.DMA((rows,)),
                pltpu.SemaphoreType.DMA((rows,)),
                pltpu.SemaphoreType.DMA(()),
                pltpu.SemaphoreType.DMA(()),
                pltpu.SemaphoreType.REGULAR,
            ],
            compiler_params=pltpu.CompilerParams(collective_id=0, has_side_effects=True, vmem_limit_bytes=60 * 2**20),
        )(tile_water, tile_frac, tile_cell, storage, kappa, inverse, cell_mask, upstream)
        return out[:1], out[1:]

    tiled = P("basin", None, "tile")
    chain = P("basin", "tile", None)
    return jax.shard_map(
        local,
        mesh=mesh,
        in_specs=(tiled, tiled, tiled, chain, chain, P("basin", "tile", None, None), chain, P("basin", "tile")),
        out_specs=(chain, chain),
        check_vma=False,
    )
```

```python
import functools

import jax
import jax.numpy as jnp
from jax import lax
from jax.experimental import pallas as pl
from jax.experimental.pallas import tpu as pltpu
from jax.sharding import PartitionSpec as P

SUBSTEPS = 3
time_step = 0.5
MESH = pl.DeviceIdType.MESH
NT = (((1,), (1,)), ((), ()))
UP, OWN = 0, 1
RATE, LIVE, LINK, START, FORCE = range(5)


def two_terms(value):
    head = value.astype(jnp.bfloat16)
    return head, (value - head.astype(jnp.float32)).astype(jnp.bfloat16)


def iota(shape, axis):
    return lax.broadcasted_iota(jnp.int32, shape, axis)


def kernel(npos, nset, water_hbm, frac_hbm, cell_hbm, storage_hbm, kappa_hbm, inverse_hbm, mask_hbm, upstream_hbm,
           out_ref,
           storage_ref, kappa_ref, mask_ref, upstream_ref, water, frac, cell, inverse, heads, tails, part, arrived, flow, inflow,
           fixed, gathered, level_ref, own_ref,
           small_sem, tile_sem, inverse_sem, part_send, part_recv, flow_send, flow_recv, push_send, push_recv, fixed_send, fixed_recv, first_send, first_recv, go):
    rows, width = storage_ref.shape[1], storage_ref.shape[2]
    half = rows // 2
    here = lax.axis_index("basin")
    mine = lax.axis_index("tile")
    odd = lax.rem(here, 2) == 1
    paired = jnp.logical_and(odd, jnp.logical_or(here > 2, mine == 0))

    def pushing(tile):
        return jnp.logical_and(jnp.logical_and(jnp.logical_not(odd), here < npos - 1), jnp.logical_or(here > 1, tile == 0))

    pushes = pushing(mine)
    to_next = jnp.logical_and(jnp.logical_or(odd, jnp.logical_and(here == 0, mine > 0)), here < npos - 1)
    starts = jnp.logical_and(here == 0, npos > 1)
    gathers = jnp.logical_and(here == 1, mine == 0)
    to_second = jnp.logical_and(odd, here < npos - 2)

    def owner_of(order):
        return jnp.where(order == nset - 1, mine, order + (order >= mine).astype(jnp.int32))

    def tile_loads(order):
        owner = owner_of(order)
        where = pl.ds(pl.multiple_of(owner * rows, rows), rows)
        return [
            pltpu.make_async_copy(source.at[0, where], target.at[order], tile_sem.at[order, at])
            for at, (source, target) in enumerate(((cell_hbm, cell), (water_hbm, water), (frac_hbm, frac)))]

    for copy in tile_loads(0):
        copy.start()

    barrier = pltpu.get_barrier_semaphore()
    for step in range(1, nset):
        other = lax.rem(mine + step, nset)
        pl.semaphore_signal(barrier, inc=1, device_id={"basin": here + pushing(other).astype(jnp.int32), "tile": other}, device_id_type=MESH)

    @pl.when(gathers)
    def _():
        for other in range(1, nset):
            pl.semaphore_signal(barrier, inc=1, device_id={"basin": 0, "tile": other}, device_id_type=MESH)

    @pl.when(pushes)
    def _():
        pl.semaphore_signal(barrier, inc=1, device_id={"basin": here + 1}, device_id_type=MESH)

    @pl.when(here > 0)
    def _():
        pl.semaphore_signal(barrier, inc=1, device_id={"basin": here - 1}, device_id_type=MESH)

    @pl.when(jnp.logical_and(paired, here > 2))
    def _():
        pl.semaphore_signal(barrier, inc=1, device_id={"basin": here - 2}, device_id_type=MESH)

    for order in range(1, nset):
        for copy in tile_loads(order):
            copy.start()
    small_loads = []
    for at, (source, target) in enumerate(((storage_hbm, storage_ref), (kappa_hbm, kappa_ref), (mask_hbm, mask_ref), (upstream_hbm, upstream_ref))):
        small_loads.append(pltpu.make_async_copy(source, target, small_sem.at[at]))

    matrix_load = pltpu.make_async_copy(inverse_hbm.at[0], inverse.at[OWN], inverse_sem.at[0])

    def matrix_push(chain):
        return pltpu.make_async_remote_copy(
            src_ref=inverse_hbm.at[0, chain], dst_ref=inverse.at[UP, chain],
            send_sem=push_send.at[chain], recv_sem=push_recv.at[chain],
            device_id={"basin": lax.rem(here + 1, npos)}, device_id_type=MESH)

    def fixed_push():
        return pltpu.make_async_remote_copy(
            src_ref=fixed.at[OWN, pl.ds(0, FORCE)], dst_ref=fixed.at[UP, pl.ds(0, FORCE)], send_sem=fixed_send.at[0], recv_sem=fixed_recv.at[0],
            device_id={"basin": lax.rem(here + 1, npos)}, device_id_type=MESH)

    def force_push():
        return pltpu.make_async_remote_copy(
            src_ref=fixed.at[OWN, FORCE], dst_ref=fixed.at[UP, FORCE], send_sem=fixed_send.at[1], recv_sem=fixed_recv.at[1],
            device_id={"basin": lax.rem(here + 1, npos)}, device_id_type=MESH)

    def first_copy(source, slot):
        return pltpu.make_async_remote_copy(
            src_ref=source, dst_ref=gathered.at[slot], send_sem=first_send.at[0], recv_sem=first_recv.at[slot],
            device_id={"basin": min(1, npos - 1), "tile": 0}, device_id_type=MESH)

    def part_copy(order):
        owner = owner_of(order)
        slot = mine - (mine > owner).astype(jnp.int32)
        return pltpu.make_async_remote_copy(
            src_ref=part.at[order], dst_ref=arrived.at[slot],
            send_sem=part_send.at[order], recv_sem=part_recv.at[slot],
            device_id={"tile": owner}, device_id_type=MESH)

    def part_arrival(slot):
        return pltpu.make_async_remote_copy(
            src_ref=part.at[slot], dst_ref=arrived.at[slot],
            send_sem=part_send.at[slot], recv_sem=part_recv.at[slot],
            device_id={"tile": owner_of(slot)}, device_id_type=MESH)

    def flow_copy(substep, ahead):
        return pltpu.make_async_remote_copy(
            src_ref=flow.at[substep], dst_ref=inflow.at[substep],
            send_sem=flow_send.at[ahead - 1, substep], recv_sem=flow_recv.at[substep],
            device_id={"basin": lax.rem(here + ahead, npos)}, device_id_type=MESH)

    def each_chain(do):
        def one(chain, carry):
            do(chain)
            return carry
        lax.fori_loop(0, rows, one, 0)

    @pl.when(pushes)
    def _():
        pl.semaphore_wait(barrier, 1)
        each_chain(lambda chain: matrix_push(chain).start())

    lane = lax.rem(iota((rows, width), 1), rows)
    row = iota((rows, width), 0)

    def cell_sums(order):
        cells = cell[order]
        shift = lax.rem(cells - iota(cells.shape, 0) + rows, rows).astype(jnp.float32).astype(jnp.bfloat16)
        upper = (cells // rows).astype(jnp.float32).astype(jnp.bfloat16)
        head, tail = two_terms(frac[order] * water[order])
        zero = jnp.zeros_like(head)
        one = jnp.ones_like(head)
        picks = [shift == jnp.bfloat16(at) for at in range(rows)]
        left = jnp.concatenate([jnp.where(pick, head, zero) for pick in picks] + [jnp.where(pick, tail, zero) for pick in picks], axis=0)
        right = jnp.concatenate([jnp.where(upper == jnp.bfloat16(at), one, zero) for at in range(width // rows)], axis=0)
        both = lax.dot_general(left, right, NT, preferred_element_type=jnp.float32)
        terms = []
        for at in range(rows):
            start = at * rows
            single = jnp.where(lane == row, both[start:start + rows] + both[rows * rows + start:rows * rows + start + rows], 0.0)
            terms.append(pltpu.roll(single, at, 1) if at else single)
        while len(terms) > 1:
            terms = [sum(terms[at:at + 2][1:], terms[at]) for at in range(0, len(terms), 2)]
        return jnp.where(lane < row, pltpu.roll(terms[0], width - rows, 1), terms[0])

    hold = jnp.maximum(nset - 1 - 2 * mine, 0)

    def group(order, carry):
        for copy in tile_loads(order):
            copy.wait()
        sums = cell_sums(order)

        @pl.when(order < nset - 1)
        def _():
            part[order] = sums

        @pl.when(order == nset - 1)
        def _():
            own_ref[...] = sums

        @pl.when(jnp.logical_and(order == hold, jnp.logical_not(pushes)))
        def _():
            pl.semaphore_wait(barrier, (nset - 1) * (1 + paired.astype(jnp.int32)) + paired.astype(jnp.int32)
                              + to_next.astype(jnp.int32) + to_second.astype(jnp.int32) + starts.astype(jnp.int32))

            @pl.when(paired)
            def _():
                pl.semaphore_signal(go, inc=1, device_id={"basin": here - 1}, device_id_type=MESH)

        @pl.when(jnp.logical_and(order == hold, pushes))
        def _():
            pl.semaphore_wait(go, 1)

        @pl.when(jnp.logical_and(jnp.logical_and(order == hold, starts), mine > 0))
        def _():
            first_copy(part.at[0], mine).start()

        @pl.when(jnp.logical_and(jnp.logical_and(order == nset - 1, starts), mine == 0))
        def _():
            first_copy(own_ref, 0).start()

        for done in reversed(range(nset - 1)):
            @pl.when(jnp.logical_or(jnp.logical_and(order == hold, done <= order), jnp.logical_and(order > hold, done == order)))
            def _():
                part_copy(done).start()

        @pl.when(order == 0)
        def _():
            for copy in small_loads:
                copy.start()
            matrix_load.start()

        return carry

    lax.fori_loop(0, nset, group, 0)

    for copy in small_loads:
        copy.wait()
    links = jnp.zeros((rows, width), jnp.int32)
    for chain in range(rows):
        links = jnp.where(row == chain, upstream_ref[0, chain], links)
    fixed[OWN, LINK] = links.astype(jnp.float32)
    fixed[OWN, LIVE] = mask_ref[0].astype(jnp.float32)
    fixed[OWN, RATE] = kappa_ref[0]
    fixed[OWN, START] = storage_ref[0]
    level_ref[OWN] = storage_ref[0]

    @pl.when(jnp.logical_or(here == 0, gathers))
    def _():
        inflow[...] = jnp.zeros_like(inflow)

    @pl.when(pushes)
    def _():
        fixed_push().start()

    def prepare(slot, ready):
        def one(chain, carry):
            ready(chain)
            head, tail = two_terms(inverse[slot, chain].T)
            heads[slot, chain] = head
            tails[slot, chain] = tail
            return carry

        def rest(chain, carry):
            ready(chain)
            return carry
        lax.fori_loop(0, half, one, 0)
        lax.fori_loop(half, rows, rest, 0)

    matrix_load.wait()
    prepare(OWN, lambda chain: None)

    picked = [lax.rem(iota((2 * half, width), 0), half) == chain for chain in range(half)]

    def product(slot, vector):
        head = vector.astype(jnp.bfloat16).astype(jnp.float32)
        tail = vector - head
        left = jnp.concatenate([head[:half], tail[:half]], axis=0).astype(jnp.bfloat16)
        first = jnp.zeros((2 * half, width), jnp.float32)
        second = jnp.zeros((2 * half, width), jnp.float32)
        reduced = []
        for chain in range(rows - half):
            if chain < half:
                single = jnp.where(picked[chain], left, jnp.zeros_like(left))
                first += jnp.dot(single, heads[slot, chain], preferred_element_type=jnp.float32)
                second += jnp.dot(single, tails[slot, chain], preferred_element_type=jnp.float32)
            other = half + chain
            reduced.append(jnp.sum(inverse[slot, other] * vector[other:other + 1], axis=1)[None])
        total = first + second
        return jnp.concatenate([total[:half] + total[half:]] + reduced, axis=0)

    runoff = own_ref[...]
    for order in range(nset - 1):
        part_arrival(order).wait_recv()
        runoff = runoff + arrived[order]
    fixed[OWN, FORCE] = time_step * runoff

    @pl.when(jnp.logical_and(pushes, here > 0))
    def _():
        force_push().start()

    @pl.when(paired)
    def _():
        prepare(UP, lambda chain: matrix_push(chain).wait_recv())
        fixed_push().wait_recv()
        level_ref[UP] = fixed[UP, START]

        @pl.when(here > 1)
        def _():
            force_push().wait_recv()

        @pl.when(here == 1)
        def _():
            for slot in range(nset):
                first_copy(own_ref, slot).wait_recv()
            fixed[UP, FORCE] = time_step * sum([gathered[slot] for slot in range(1, nset)], gathered[0])

    def turn(count, carry):
        slot = jnp.where(paired, lax.rem(count, 2), OWN)
        substep = jnp.where(paired, count // 2, count)
        leads = jnp.logical_or(jnp.logical_not(paired), slot == UP)

        @pl.when(jnp.logical_and(leads, jnp.logical_or(here > 1, jnp.logical_and(here == 1, mine > 0))))
        def _():
            flow_copy(substep, 1).wait_recv()

        came = inflow[jnp.where(leads, substep, SUBSTEPS)]
        links = fixed[slot, LINK]
        incoming = jnp.broadcast_to(came[:1], (rows, width))
        for chain in range(1, rows):
            incoming = jnp.where(links == float(chain), jnp.broadcast_to(came[chain:chain + 1], (rows, width)), incoming)
        wet = fixed[slot, LIVE] * product(slot, level_ref[slot] + fixed[slot, FORCE] + incoming)
        outflow = fixed[slot, RATE] * wet

        @pl.when(slot == OWN)
        def _():
            flow[substep] = outflow

            @pl.when(to_second)
            def _():
                flow_copy(substep, 2).start()

            @pl.when(to_next)
            def _():
                flow_copy(substep, 1).start()

            out_ref[0] = wet - outflow
            out_ref[1] = outflow

        @pl.when(slot == UP)
        def _():
            inflow[SUBSTEPS] = outflow

        level_ref[slot] = wet - outflow
        return carry

    lax.fori_loop(0, jnp.where(paired, 2 * SUBSTEPS, SUBSTEPS), turn, 0)

    for order in range(nset - 1):
        part_copy(order).wait_send()

    @pl.when(pushes)
    def _():
        each_chain(lambda chain: matrix_push(chain).wait_send())
        fixed_push().wait_send()

    @pl.when(jnp.logical_and(pushes, here > 0))
    def _():
        force_push().wait_send()

    @pl.when(starts)
    def _():
        first_copy(own_ref, 0).wait_send()

    @pl.when(to_next)
    def _():
        for substep in range(SUBSTEPS):
            flow_copy(substep, 1).wait_send()

    @pl.when(to_second)
    def _():
        for substep in range(SUBSTEPS):
            flow_copy(substep, 2).wait_send()


def solution(mesh):
    npos, nset = mesh.shape["basin"], mesh.shape["tile"]

    def local(tile_water, tile_frac, tile_cell, storage, kappa, inverse, cell_mask, upstream):
        rows, width = storage.shape[1:]
        tiles = tile_water.shape[2]
        anywhere = pl.BlockSpec(memory_space=pltpu.HBM)
        vmem = pl.BlockSpec(memory_space=pltpu.VMEM)
        others = max(nset - 1, 1)
        out = pl.pallas_call(
            functools.partial(kernel, npos, nset),
            out_shape=pltpu.VMEM((2, rows, width), jnp.float32),
            in_specs=[anywhere] * 8,
            out_specs=vmem,
            scratch_shapes=[
                pltpu.VMEM(storage.shape, jnp.float32),
                pltpu.VMEM(kappa.shape, jnp.float32),
                pltpu.VMEM(cell_mask.shape, jnp.int32),
                pltpu.SMEM(upstream.shape, jnp.int32),
                pltpu.VMEM((nset, rows, tiles), jnp.float32),
                pltpu.VMEM((nset, rows, tiles), jnp.float32),
                pltpu.VMEM((nset, rows, tiles), jnp.int32),
                pltpu.VMEM((2, rows, width, width), jnp.float32),
                pltpu.VMEM((2, rows // 2, width, width), jnp.bfloat16),
                pltpu.VMEM((2, rows // 2, width, width), jnp.bfloat16),
                pltpu.VMEM((others, rows, width), jnp.float32),
                pltpu.VMEM((others, rows, width), jnp.float32),
                pltpu.VMEM((SUBSTEPS, rows, width), jnp.float32),
                pltpu.VMEM((SUBSTEPS + 1, rows, width), jnp.float32),
                pltpu.VMEM((2, 5, rows, width), jnp.float32),
                pltpu.VMEM((nset, rows, width), jnp.float32),
                pltpu.VMEM((2, rows, width), jnp.float32),
                pltpu.VMEM((rows, width), jnp.float32),
                pltpu.SemaphoreType.DMA((4,)),
                pltpu.SemaphoreType.DMA((nset, 3)),
                pltpu.SemaphoreType.DMA((1,)),
                pltpu.SemaphoreType.DMA((others,)),
                pltpu.SemaphoreType.DMA((others,)),
                pltpu.SemaphoreType.DMA((2, SUBSTEPS)),
                pltpu.SemaphoreType.DMA((SUBSTEPS,)),
                pltpu.SemaphoreType.DMA((rows,)),
                pltpu.SemaphoreType.DMA((rows,)),
                pltpu.SemaphoreType.DMA((2,)),
                pltpu.SemaphoreType.DMA((2,)),
                pltpu.SemaphoreType.DMA((1,)),
                pltpu.SemaphoreType.DMA((nset,)),
                pltpu.SemaphoreType.REGULAR,
            ],
            compiler_params=pltpu.CompilerParams(collective_id=0, has_side_effects=True, vmem_limit_bytes=60 * 2**20),
        )(tile_water, tile_frac, tile_cell, storage, kappa, inverse, cell_mask, upstream)
        return out[:1], out[1:]

    tiled = P("basin", None, "tile")
    chain = P("basin", "tile", None)
    return jax.shard_map(
        local,
        mesh=mesh,
        in_specs=(tiled, tiled, tiled, chain, chain, P("basin", "tile", None, None), chain, P("basin", "tile")),
        out_specs=(chain, chain),
        check_vma=False,
    )
```

```python
import functools

import jax
import jax.numpy as jnp
from jax import lax
from jax.experimental import pallas as pl
from jax.experimental.pallas import tpu as pltpu
from jax.sharding import PartitionSpec as P

SUBSTEPS = 3
time_step = 0.5
MESH = pl.DeviceIdType.MESH
NT = (((1,), (1,)), ((), ()))
UP, OWN = 0, 1
RATE, LIVE, LINK, START, FORCE = range(5)


def two_terms(value):
    head = value.astype(jnp.bfloat16)
    return head, (value - head.astype(jnp.float32)).astype(jnp.bfloat16)


def iota(shape, axis):
    return lax.broadcasted_iota(jnp.int32, shape, axis)


def kernel(npos, nset, water_hbm, frac_hbm, cell_hbm, storage_hbm, kappa_hbm, inverse_hbm, mask_hbm, upstream_hbm,
           out_ref,
           storage_ref, kappa_ref, mask_ref, upstream_ref, water, frac, cell, inverse, heads, tails, part, arrived, flow, inflow,
           fixed, gathered, level_ref, own_ref,
           small_sem, tile_sem, inverse_sem, part_send, part_recv, flow_send, flow_recv, push_send, push_recv, fixed_send, fixed_recv, first_send, first_recv, go):
    rows, width = storage_ref.shape[1], storage_ref.shape[2]
    half = rows // 2
    here = lax.axis_index("basin")
    mine = lax.axis_index("tile")
    odd = lax.rem(here, 2) == 1
    firsts = (nset + 1) // 2
    paired = jnp.logical_and(odd, jnp.logical_or(here > 2, mine < firsts))

    def pushing(tile):
        return jnp.logical_and(jnp.logical_and(jnp.logical_not(odd), here < npos - 1), jnp.logical_or(here > 1, tile < firsts))

    pushes = pushing(mine)
    to_next = jnp.logical_and(jnp.logical_or(odd, jnp.logical_and(here == 0, mine >= firsts)), here < npos - 1)
    starts = jnp.logical_and(here == 0, npos > 1)
    gathers = jnp.logical_and(here == 1, mine < firsts)
    to_second = jnp.logical_and(odd, here < npos - 2)

    def owner_of(order):
        return jnp.where(order == nset - 1, mine, order + (order >= mine).astype(jnp.int32))

    def tile_loads(order):
        owner = owner_of(order)
        where = pl.ds(pl.multiple_of(owner * rows, rows), rows)
        return [
            pltpu.make_async_copy(source.at[0, where], target.at[order], tile_sem.at[order, at])
            for at, (source, target) in enumerate(((cell_hbm, cell), (water_hbm, water), (frac_hbm, frac)))]

    for copy in tile_loads(0):
        copy.start()

    barrier = pltpu.get_barrier_semaphore()
    for step in range(1, nset):
        other = lax.rem(mine + step, nset)
        pl.semaphore_signal(barrier, inc=1, device_id={"basin": here + pushing(other).astype(jnp.int32), "tile": other}, device_id_type=MESH)

    @pl.when(gathers)
    def _():
        for other in range(firsts, nset):
            pl.semaphore_signal(barrier, inc=1, device_id={"basin": 0, "tile": other}, device_id_type=MESH)

    @pl.when(pushes)
    def _():
        pl.semaphore_signal(barrier, inc=1, device_id={"basin": here + 1}, device_id_type=MESH)

    @pl.when(here > 0)
    def _():
        pl.semaphore_signal(barrier, inc=1, device_id={"basin": here - 1}, device_id_type=MESH)

    @pl.when(jnp.logical_and(paired, here > 2))
    def _():
        pl.semaphore_signal(barrier, inc=1, device_id={"basin": here - 2}, device_id_type=MESH)

    for order in range(1, nset):
        for copy in tile_loads(order):
            copy.start()
    small_loads = []
    for at, (source, target) in enumerate(((storage_hbm, storage_ref), (kappa_hbm, kappa_ref), (mask_hbm, mask_ref), (upstream_hbm, upstream_ref))):
        small_loads.append(pltpu.make_async_copy(source, target, small_sem.at[at]))

    matrix_load = pltpu.make_async_copy(inverse_hbm.at[0], inverse.at[OWN], inverse_sem.at[0])

    def matrix_push(chain):
        return pltpu.make_async_remote_copy(
            src_ref=inverse_hbm.at[0, chain], dst_ref=inverse.at[UP, chain],
            send_sem=push_send.at[chain], recv_sem=push_recv.at[chain],
            device_id={"basin": lax.rem(here + 1, npos)}, device_id_type=MESH)

    def fixed_push():
        return pltpu.make_async_remote_copy(
            src_ref=fixed.at[OWN, pl.ds(0, FORCE)], dst_ref=fixed.at[UP, pl.ds(0, FORCE)], send_sem=fixed_send.at[0], recv_sem=fixed_recv.at[0],
            device_id={"basin": lax.rem(here + 1, npos)}, device_id_type=MESH)

    def force_push():
        return pltpu.make_async_remote_copy(
            src_ref=fixed.at[OWN, FORCE], dst_ref=fixed.at[UP, FORCE], send_sem=fixed_send.at[1], recv_sem=fixed_recv.at[1],
            device_id={"basin": lax.rem(here + 1, npos)}, device_id_type=MESH)

    def first_copy(source, owner, slot):
        return pltpu.make_async_remote_copy(
            src_ref=source, dst_ref=gathered.at[slot], send_sem=first_send.at[owner], recv_sem=first_recv.at[slot],
            device_id={"basin": min(1, npos - 1), "tile": owner}, device_id_type=MESH)

    def part_copy(order):
        owner = owner_of(order)
        slot = mine - (mine > owner).astype(jnp.int32)
        return pltpu.make_async_remote_copy(
            src_ref=part.at[order], dst_ref=arrived.at[slot],
            send_sem=part_send.at[order], recv_sem=part_recv.at[slot],
            device_id={"tile": owner}, device_id_type=MESH)

    def part_arrival(slot):
        return pltpu.make_async_remote_copy(
            src_ref=part.at[slot], dst_ref=arrived.at[slot],
            send_sem=part_send.at[slot], recv_sem=part_recv.at[slot],
            device_id={"tile": owner_of(slot)}, device_id_type=MESH)

    def flow_copy(substep, ahead):
        return pltpu.make_async_remote_copy(
            src_ref=flow.at[substep], dst_ref=inflow.at[substep],
            send_sem=flow_send.at[ahead - 1, substep], recv_sem=flow_recv.at[substep],
            device_id={"basin": lax.rem(here + ahead, npos)}, device_id_type=MESH)

    def each_chain(do):
        def one(chain, carry):
            do(chain)
            return carry
        lax.fori_loop(0, rows, one, 0)

    @pl.when(pushes)
    def _():
        pl.semaphore_wait(barrier, 1)
        each_chain(lambda chain: matrix_push(chain).start())

    lane = lax.rem(iota((rows, width), 1), rows)
    row = iota((rows, width), 0)

    def cell_sums(order):
        cells = cell[order]
        shift = lax.rem(cells - iota(cells.shape, 0) + rows, rows).astype(jnp.float32).astype(jnp.bfloat16)
        upper = (cells // rows).astype(jnp.float32).astype(jnp.bfloat16)
        head, tail = two_terms(frac[order] * water[order])
        zero = jnp.zeros_like(head)
        one = jnp.ones_like(head)
        picks = [shift == jnp.bfloat16(at) for at in range(rows)]
        left = jnp.concatenate([jnp.where(pick, head, zero) for pick in picks] + [jnp.where(pick, tail, zero) for pick in picks], axis=0)
        right = jnp.concatenate([jnp.where(upper == jnp.bfloat16(at), one, zero) for at in range(width // rows)], axis=0)
        both = lax.dot_general(left, right, NT, preferred_element_type=jnp.float32)
        terms = []
        for at in range(rows):
            start = at * rows
            single = jnp.where(lane == row, both[start:start + rows] + both[rows * rows + start:rows * rows + start + rows], 0.0)
            terms.append(pltpu.roll(single, at, 1) if at else single)
        while len(terms) > 1:
            terms = [sum(terms[at:at + 2][1:], terms[at]) for at in range(0, len(terms), 2)]
        return jnp.where(lane < row, pltpu.roll(terms[0], width - rows, 1), terms[0])

    hold = jnp.maximum(nset - 1 - 2 * mine, 0)

    def group(order, carry):
        for copy in tile_loads(order):
            copy.wait()
        sums = cell_sums(order)

        @pl.when(order < nset - 1)
        def _():
            part[order] = sums

        @pl.when(order == nset - 1)
        def _():
            own_ref[...] = sums

        @pl.when(jnp.logical_and(order == hold, jnp.logical_not(pushes)))
        def _():
            pl.semaphore_wait(barrier, (nset - 1) * (1 + paired.astype(jnp.int32)) + paired.astype(jnp.int32)
                              + to_next.astype(jnp.int32) + to_second.astype(jnp.int32) + starts.astype(jnp.int32) * firsts)

            @pl.when(paired)
            def _():
                pl.semaphore_signal(go, inc=1, device_id={"basin": here - 1}, device_id_type=MESH)

        @pl.when(jnp.logical_and(order == hold, pushes))
        def _():
            pl.semaphore_wait(go, 1)

        for owner in range(firsts):
            at = owner - (owner > mine).astype(jnp.int32)

            @pl.when(jnp.logical_and(jnp.logical_and(starts, mine != owner), order == jnp.maximum(hold, at)))
            def _():
                first_copy(part.at[at], owner, mine).start()

            @pl.when(jnp.logical_and(jnp.logical_and(starts, mine == owner), order == nset - 1))
            def _():
                first_copy(own_ref, owner, mine).start()

        for done in reversed(range(nset - 1)):
            @pl.when(jnp.logical_or(jnp.logical_and(order == hold, done <= order), jnp.logical_and(order > hold, done == order)))
            def _():
                part_copy(done).start()

        @pl.when(order == 0)
        def _():
            for copy in small_loads:
                copy.start()
            matrix_load.start()

        return carry

    lax.fori_loop(0, nset, group, 0)

    for copy in small_loads:
        copy.wait()
    links = jnp.zeros((rows, width), jnp.int32)
    for chain in range(rows):
        links = jnp.where(row == chain, upstream_ref[0, chain], links)
    fixed[OWN, LINK] = links.astype(jnp.float32)
    fixed[OWN, LIVE] = mask_ref[0].astype(jnp.float32)
    fixed[OWN, RATE] = kappa_ref[0]
    fixed[OWN, START] = storage_ref[0]
    level_ref[OWN] = storage_ref[0]

    @pl.when(jnp.logical_or(here == 0, gathers))
    def _():
        inflow[...] = jnp.zeros_like(inflow)

    @pl.when(pushes)
    def _():
        fixed_push().start()

    def prepare(slot, ready):
        def one(chain, carry):
            ready(chain)
            head, tail = two_terms(inverse[slot, chain].T)
            heads[slot, chain] = head
            tails[slot, chain] = tail
            return carry

        def rest(chain, carry):
            ready(chain)
            return carry
        lax.fori_loop(0, half, one, 0)
        lax.fori_loop(half, rows, rest, 0)

    matrix_load.wait()
    prepare(OWN, lambda chain: None)

    picked = [lax.rem(iota((2 * half, width), 0), half) == chain for chain in range(half)]

    def product(slot, vector):
        head = vector.astype(jnp.bfloat16).astype(jnp.float32)
        tail = vector - head
        left = jnp.concatenate([head[:half], tail[:half]], axis=0).astype(jnp.bfloat16)
        first = jnp.zeros((2 * half, width), jnp.float32)
        second = jnp.zeros((2 * half, width), jnp.float32)
        reduced = []
        for chain in range(rows - half):
            if chain < half:
                single = jnp.where(picked[chain], left, jnp.zeros_like(left))
                first += jnp.dot(single, heads[slot, chain], preferred_element_type=jnp.float32)
                second += jnp.dot(single, tails[slot, chain], preferred_element_type=jnp.float32)
            other = half + chain
            reduced.append(jnp.sum(inverse[slot, other] * vector[other:other + 1], axis=1)[None])
        total = first + second
        return jnp.concatenate([total[:half] + total[half:]] + reduced, axis=0)

    runoff = own_ref[...]
    for order in range(nset - 1):
        part_arrival(order).wait_recv()
        runoff = runoff + arrived[order]
    fixed[OWN, FORCE] = time_step * runoff

    @pl.when(jnp.logical_and(pushes, here > 0))
    def _():
        force_push().start()

    @pl.when(paired)
    def _():
        prepare(UP, lambda chain: matrix_push(chain).wait_recv())
        fixed_push().wait_recv()
        level_ref[UP] = fixed[UP, START]

        @pl.when(here > 1)
        def _():
            force_push().wait_recv()

        @pl.when(here == 1)
        def _():
            for slot in range(nset):
                first_copy(own_ref, 0, slot).wait_recv()
            fixed[UP, FORCE] = time_step * sum([gathered[slot] for slot in range(1, nset)], gathered[0])

    def turn(count, carry):
        slot = jnp.where(paired, lax.rem(count, 2), OWN)
        substep = jnp.where(paired, count // 2, count)
        leads = jnp.logical_or(jnp.logical_not(paired), slot == UP)

        @pl.when(jnp.logical_and(leads, jnp.logical_or(here > 1, jnp.logical_and(here == 1, mine >= firsts))))
        def _():
            flow_copy(substep, 1).wait_recv()

        came = inflow[jnp.where(leads, substep, SUBSTEPS)]
        links = fixed[slot, LINK]
        incoming = jnp.broadcast_to(came[:1], (rows, width))
        for chain in range(1, rows):
            incoming = jnp.where(links == float(chain), jnp.broadcast_to(came[chain:chain + 1], (rows, width)), incoming)
        wet = fixed[slot, LIVE] * product(slot, level_ref[slot] + fixed[slot, FORCE] + incoming)
        outflow = fixed[slot, RATE] * wet

        @pl.when(slot == OWN)
        def _():
            flow[substep] = outflow

            @pl.when(to_second)
            def _():
                flow_copy(substep, 2).start()

            @pl.when(to_next)
            def _():
                flow_copy(substep, 1).start()

            out_ref[0] = wet - outflow
            out_ref[1] = outflow

        @pl.when(slot == UP)
        def _():
            inflow[SUBSTEPS] = outflow

        level_ref[slot] = wet - outflow
        return carry

    lax.fori_loop(0, jnp.where(paired, 2 * SUBSTEPS, SUBSTEPS), turn, 0)

    for order in range(nset - 1):
        part_copy(order).wait_send()

    @pl.when(pushes)
    def _():
        each_chain(lambda chain: matrix_push(chain).wait_send())
        fixed_push().wait_send()

    @pl.when(jnp.logical_and(pushes, here > 0))
    def _():
        force_push().wait_send()

    @pl.when(starts)
    def _():
        for owner in range(firsts):
            first_copy(own_ref, owner, mine).wait_send()

    @pl.when(to_next)
    def _():
        for substep in range(SUBSTEPS):
            flow_copy(substep, 1).wait_send()

    @pl.when(to_second)
    def _():
        for substep in range(SUBSTEPS):
            flow_copy(substep, 2).wait_send()


def solution(mesh):
    npos, nset = mesh.shape["basin"], mesh.shape["tile"]

    def local(tile_water, tile_frac, tile_cell, storage, kappa, inverse, cell_mask, upstream):
        rows, width = storage.shape[1:]
        tiles = tile_water.shape[2]
        anywhere = pl.BlockSpec(memory_space=pltpu.HBM)
        vmem = pl.BlockSpec(memory_space=pltpu.VMEM)
        others = max(nset - 1, 1)
        out = pl.pallas_call(
            functools.partial(kernel, npos, nset),
            out_shape=pltpu.VMEM((2, rows, width), jnp.float32),
            in_specs=[anywhere] * 8,
            out_specs=vmem,
            scratch_shapes=[
                pltpu.VMEM(storage.shape, jnp.float32),
                pltpu.VMEM(kappa.shape, jnp.float32),
                pltpu.VMEM(cell_mask.shape, jnp.int32),
                pltpu.SMEM(upstream.shape, jnp.int32),
                pltpu.VMEM((nset, rows, tiles), jnp.float32),
                pltpu.VMEM((nset, rows, tiles), jnp.float32),
                pltpu.VMEM((nset, rows, tiles), jnp.int32),
                pltpu.VMEM((2, rows, width, width), jnp.float32),
                pltpu.VMEM((2, rows // 2, width, width), jnp.bfloat16),
                pltpu.VMEM((2, rows // 2, width, width), jnp.bfloat16),
                pltpu.VMEM((others, rows, width), jnp.float32),
                pltpu.VMEM((others, rows, width), jnp.float32),
                pltpu.VMEM((SUBSTEPS, rows, width), jnp.float32),
                pltpu.VMEM((SUBSTEPS + 1, rows, width), jnp.float32),
                pltpu.VMEM((2, 5, rows, width), jnp.float32),
                pltpu.VMEM((nset, rows, width), jnp.float32),
                pltpu.VMEM((2, rows, width), jnp.float32),
                pltpu.VMEM((rows, width), jnp.float32),
                pltpu.SemaphoreType.DMA((4,)),
                pltpu.SemaphoreType.DMA((nset, 3)),
                pltpu.SemaphoreType.DMA((1,)),
                pltpu.SemaphoreType.DMA((others,)),
                pltpu.SemaphoreType.DMA((others,)),
                pltpu.SemaphoreType.DMA((2, SUBSTEPS)),
                pltpu.SemaphoreType.DMA((SUBSTEPS,)),
                pltpu.SemaphoreType.DMA((rows,)),
                pltpu.SemaphoreType.DMA((rows,)),
                pltpu.SemaphoreType.DMA((2,)),
                pltpu.SemaphoreType.DMA((2,)),
                pltpu.SemaphoreType.DMA((nset,)),
                pltpu.SemaphoreType.DMA((nset,)),
                pltpu.SemaphoreType.REGULAR,
            ],
            compiler_params=pltpu.CompilerParams(collective_id=0, has_side_effects=True, vmem_limit_bytes=60 * 2**20),
        )(tile_water, tile_frac, tile_cell, storage, kappa, inverse, cell_mask, upstream)
        return out[:1], out[1:]

    tiled = P("basin", None, "tile")
    chain = P("basin", "tile", None)
    return jax.shard_map(
        local,
        mesh=mesh,
        in_specs=(tiled, tiled, tiled, chain, chain, P("basin", "tile", None, None), chain, P("basin", "tile")),
        out_specs=(chain, chain),
        check_vma=False,
    )
```

```python
import functools

import jax
import jax.numpy as jnp
from jax import lax
from jax.experimental import pallas as pl
from jax.experimental.pallas import tpu as pltpu
from jax.sharding import PartitionSpec as P

SUBSTEPS = 3
time_step = 0.5
MESH = pl.DeviceIdType.MESH
NT = (((1,), (1,)), ((), ()))
UP, OWN = 0, 1
RATE, LIVE, LINK, START, FORCE = range(5)


def two_terms(value):
    head = value.astype(jnp.bfloat16)
    return head, (value - head.astype(jnp.float32)).astype(jnp.bfloat16)


def iota(shape, axis):
    return lax.broadcasted_iota(jnp.int32, shape, axis)


def kernel(npos, nset, water_hbm, frac_hbm, cell_hbm, storage_hbm, kappa_hbm, inverse_hbm, mask_hbm, upstream_hbm,
           out_ref,
           storage_ref, kappa_ref, mask_ref, upstream_ref, water, frac, cell, inverse, heads, tails, part, arrived, flow, inflow,
           fixed, gathered, level_ref, own_ref,
           small_sem, tile_sem, inverse_sem, part_send, part_recv, flow_send, flow_recv, push_send, push_recv, fixed_send, fixed_recv, first_send, first_recv, go):
    rows, width = storage_ref.shape[1], storage_ref.shape[2]
    half = rows // 2
    here = lax.axis_index("basin")
    mine = lax.axis_index("tile")
    odd = lax.rem(here, 2) == 1
    firsts = 1
    paired = jnp.logical_and(odd, jnp.logical_or(here > 2, mine < firsts))

    def pushing(tile):
        return jnp.logical_and(jnp.logical_and(jnp.logical_not(odd), here < npos - 1), jnp.logical_or(here > 1, tile < firsts))

    pushes = pushing(mine)
    to_next = jnp.logical_and(jnp.logical_or(odd, jnp.logical_and(here == 0, mine >= firsts)), here < npos - 1)
    starts = jnp.logical_and(here == 0, npos > 1)
    gathers = jnp.logical_and(here == 1, mine < firsts)
    to_second = jnp.logical_and(odd, here < npos - 2)

    late = mine >= 2

    def owner_of(order):
        other = order + (order >= mine).astype(jnp.int32)
        other = jnp.where(jnp.logical_and(late, other < 2), 1 - other, other)
        return jnp.where(order == nset - 1, mine, other)

    def tile_loads(order):
        owner = owner_of(order)
        where = pl.ds(pl.multiple_of(owner * rows, rows), rows)
        return [
            pltpu.make_async_copy(source.at[0, where], target.at[order], tile_sem.at[order, at])
            for at, (source, target) in enumerate(((cell_hbm, cell), (water_hbm, water), (frac_hbm, frac)))]

    for copy in tile_loads(0):
        copy.start()

    barrier = pltpu.get_barrier_semaphore()
    for step in range(1, nset):
        other = lax.rem(mine + step, nset)
        pl.semaphore_signal(barrier, inc=1, device_id={"basin": here + pushing(other).astype(jnp.int32), "tile": other}, device_id_type=MESH)

    @pl.when(gathers)
    def _():
        for other in range(firsts, nset):
            pl.semaphore_signal(barrier, inc=1, device_id={"basin": 0, "tile": other}, device_id_type=MESH)

    @pl.when(pushes)
    def _():
        pl.semaphore_signal(barrier, inc=1, device_id={"basin": here + 1}, device_id_type=MESH)

    @pl.when(here > 0)
    def _():
        pl.semaphore_signal(barrier, inc=1, device_id={"basin": here - 1}, device_id_type=MESH)

    @pl.when(jnp.logical_and(paired, here > 2))
    def _():
        pl.semaphore_signal(barrier, inc=1, device_id={"basin": here - 2}, device_id_type=MESH)

    for order in range(1, nset):
        for copy in tile_loads(order):
            copy.start()
    small_loads = []
    for at, (source, target) in enumerate(((storage_hbm, storage_ref), (kappa_hbm, kappa_ref), (mask_hbm, mask_ref), (upstream_hbm, upstream_ref))):
        small_loads.append(pltpu.make_async_copy(source, target, small_sem.at[at]))

    matrix_load = pltpu.make_async_copy(inverse_hbm.at[0], inverse.at[OWN], inverse_sem.at[0])

    def matrix_push(chain):
        return pltpu.make_async_remote_copy(
            src_ref=inverse_hbm.at[0, chain], dst_ref=inverse.at[UP, chain],
            send_sem=push_send.at[chain], recv_sem=push_recv.at[chain],
            device_id={"basin": lax.rem(here + 1, npos)}, device_id_type=MESH)

    def fixed_push():
        return pltpu.make_async_remote_copy(
            src_ref=fixed.at[OWN, pl.ds(0, FORCE)], dst_ref=fixed.at[UP, pl.ds(0, FORCE)], send_sem=fixed_send.at[0], recv_sem=fixed_recv.at[0],
            device_id={"basin": lax.rem(here + 1, npos)}, device_id_type=MESH)

    def force_push():
        return pltpu.make_async_remote_copy(
            src_ref=fixed.at[OWN, FORCE], dst_ref=fixed.at[UP, FORCE], send_sem=fixed_send.at[1], recv_sem=fixed_recv.at[1],
            device_id={"basin": lax.rem(here + 1, npos)}, device_id_type=MESH)

    def first_copy(source, owner, slot):
        return pltpu.make_async_remote_copy(
            src_ref=source, dst_ref=gathered.at[slot], send_sem=first_send.at[owner], recv_sem=first_recv.at[slot],
            device_id={"basin": min(1, npos - 1), "tile": owner}, device_id_type=MESH)

    def part_copy(order):
        owner = owner_of(order)
        slot = mine - (mine > owner).astype(jnp.int32)
        return pltpu.make_async_remote_copy(
            src_ref=part.at[order], dst_ref=arrived.at[slot],
            send_sem=part_send.at[order], recv_sem=part_recv.at[slot],
            device_id={"tile": owner}, device_id_type=MESH)

    def part_arrival(slot):
        return pltpu.make_async_remote_copy(
            src_ref=part.at[slot], dst_ref=arrived.at[slot],
            send_sem=part_send.at[slot], recv_sem=part_recv.at[slot],
            device_id={"tile": owner_of(slot)}, device_id_type=MESH)

    def flow_copy(substep, ahead):
        return pltpu.make_async_remote_copy(
            src_ref=flow.at[substep], dst_ref=inflow.at[substep],
            send_sem=flow_send.at[ahead - 1, substep], recv_sem=flow_recv.at[substep],
            device_id={"basin": lax.rem(here + ahead, npos)}, device_id_type=MESH)

    def each_chain(do):
        def one(chain, carry):
            do(chain)
            return carry
        lax.fori_loop(0, rows, one, 0)

    @pl.when(pushes)
    def _():
        pl.semaphore_wait(barrier, 1)
        each_chain(lambda chain: matrix_push(chain).start())

    lane = lax.rem(iota((rows, width), 1), rows)
    row = iota((rows, width), 0)

    def cell_sums(order):
        cells = cell[order]
        shift = lax.rem(cells - iota(cells.shape, 0) + rows, rows).astype(jnp.float32).astype(jnp.bfloat16)
        upper = (cells // rows).astype(jnp.float32).astype(jnp.bfloat16)
        head, tail = two_terms(frac[order] * water[order])
        zero = jnp.zeros_like(head)
        one = jnp.ones_like(head)
        picks = [shift == jnp.bfloat16(at) for at in range(rows)]
        left = jnp.concatenate([jnp.where(pick, head, zero) for pick in picks] + [jnp.where(pick, tail, zero) for pick in picks], axis=0)
        right = jnp.concatenate([jnp.where(upper == jnp.bfloat16(at), one, zero) for at in range(width // rows)], axis=0)
        both = lax.dot_general(left, right, NT, preferred_element_type=jnp.float32)
        terms = []
        for at in range(rows):
            start = at * rows
            single = jnp.where(lane == row, both[start:start + rows] + both[rows * rows + start:rows * rows + start + rows], 0.0)
            terms.append(pltpu.roll(single, at, 1) if at else single)
        while len(terms) > 1:
            terms = [sum(terms[at:at + 2][1:], terms[at]) for at in range(0, len(terms), 2)]
        return jnp.where(lane < row, pltpu.roll(terms[0], width - rows, 1), terms[0])

    hold = jnp.maximum(nset - 1 - 2 * mine, 0)

    def group(order, carry):
        for copy in tile_loads(order):
            copy.wait()
        sums = cell_sums(order)

        @pl.when(order < nset - 1)
        def _():
            part[order] = sums

        @pl.when(order == nset - 1)
        def _():
            own_ref[...] = sums

        @pl.when(jnp.logical_and(order == hold, jnp.logical_not(pushes)))
        def _():
            pl.semaphore_wait(barrier, (nset - 1) * (1 + paired.astype(jnp.int32)) + paired.astype(jnp.int32)
                              + to_next.astype(jnp.int32) + to_second.astype(jnp.int32) + starts.astype(jnp.int32) * firsts)

            @pl.when(paired)
            def _():
                pl.semaphore_signal(go, inc=1, device_id={"basin": here - 1}, device_id_type=MESH)

        @pl.when(jnp.logical_and(order == hold, pushes))
        def _():
            pl.semaphore_wait(go, 1)

        for owner in range(firsts):
            at = owner - (owner > mine).astype(jnp.int32)
            at = jnp.where(jnp.logical_and(late, owner < 2), 1 - at, at)

            @pl.when(jnp.logical_and(jnp.logical_and(starts, mine != owner), order == jnp.maximum(hold, at)))
            def _():
                first_copy(part.at[at], owner, mine).start()

            @pl.when(jnp.logical_and(jnp.logical_and(starts, mine == owner), order == nset - 1))
            def _():
                first_copy(own_ref, owner, mine).start()

        for done in reversed(range(nset - 1)):
            @pl.when(jnp.logical_or(jnp.logical_and(order == hold, done <= order), jnp.logical_and(order > hold, done == order)))
            def _():
                part_copy(done).start()

        @pl.when(order == 0)
        def _():
            for copy in small_loads:
                copy.start()
            matrix_load.start()

        return carry

    lax.fori_loop(0, nset, group, 0)

    for copy in small_loads:
        copy.wait()
    links = jnp.zeros((rows, width), jnp.int32)
    for chain in range(rows):
        links = jnp.where(row == chain, upstream_ref[0, chain], links)
    fixed[OWN, LINK] = links.astype(jnp.float32)
    fixed[OWN, LIVE] = mask_ref[0].astype(jnp.float32)
    fixed[OWN, RATE] = kappa_ref[0]
    fixed[OWN, START] = storage_ref[0]
    level_ref[OWN] = storage_ref[0]

    @pl.when(jnp.logical_or(here == 0, gathers))
    def _():
        inflow[...] = jnp.zeros_like(inflow)

    @pl.when(pushes)
    def _():
        fixed_push().start()

    def prepare(slot, ready):
        def one(chain, carry):
            ready(chain)
            head, tail = two_terms(inverse[slot, chain].T)
            heads[slot, chain] = head
            tails[slot, chain] = tail
            return carry

        def rest(chain, carry):
            ready(chain)
            return carry
        lax.fori_loop(0, half, one, 0)
        lax.fori_loop(half, rows, rest, 0)

    matrix_load.wait()
    prepare(OWN, lambda chain: None)

    picked = [lax.rem(iota((2 * half, width), 0), half) == chain for chain in range(half)]

    def product(slot, vector):
        head = vector.astype(jnp.bfloat16).astype(jnp.float32)
        tail = vector - head
        left = jnp.concatenate([head[:half], tail[:half]], axis=0).astype(jnp.bfloat16)
        first = jnp.zeros((2 * half, width), jnp.float32)
        second = jnp.zeros((2 * half, width), jnp.float32)
        reduced = []
        for chain in range(rows - half):
            if chain < half:
                single = jnp.where(picked[chain], left, jnp.zeros_like(left))
                first += jnp.dot(single, heads[slot, chain], preferred_element_type=jnp.float32)
                second += jnp.dot(single, tails[slot, chain], preferred_element_type=jnp.float32)
            other = half + chain
            reduced.append(jnp.sum(inverse[slot, other] * vector[other:other + 1], axis=1)[None])
        total = first + second
        return jnp.concatenate([total[:half] + total[half:]] + reduced, axis=0)

    @pl.when(paired)
    def _():
        prepare(UP, lambda chain: matrix_push(chain).wait_recv())
        fixed_push().wait_recv()
        level_ref[UP] = fixed[UP, START]

    runoff = own_ref[...]
    for order in range(nset - 1):
        part_arrival(order).wait_recv()
        runoff = runoff + arrived[order]
    fixed[OWN, FORCE] = time_step * runoff

    @pl.when(jnp.logical_and(pushes, here > 0))
    def _():
        force_push().start()

    @pl.when(jnp.logical_and(paired, here > 1))
    def _():
        force_push().wait_recv()

    @pl.when(gathers)
    def _():
        for slot in range(nset):
            first_copy(own_ref, 0, slot).wait_recv()
        fixed[UP, FORCE] = time_step * sum([gathered[slot] for slot in range(1, nset)], gathered[0])

    def turn(count, carry):
        slot = jnp.where(paired, lax.rem(count, 2), OWN)
        substep = jnp.where(paired, count // 2, count)
        leads = jnp.logical_or(jnp.logical_not(paired), slot == UP)

        @pl.when(jnp.logical_and(leads, jnp.logical_or(here > 1, jnp.logical_and(here == 1, mine >= firsts))))
        def _():
            flow_copy(substep, 1).wait_recv()

        came = inflow[jnp.where(leads, substep, SUBSTEPS)]
        links = fixed[slot, LINK]
        incoming = jnp.broadcast_to(came[:1], (rows, width))
        for chain in range(1, rows):
            incoming = jnp.where(links == float(chain), jnp.broadcast_to(came[chain:chain + 1], (rows, width)), incoming)
        wet = fixed[slot, LIVE] * product(slot, level_ref[slot] + fixed[slot, FORCE] + incoming)
        outflow = fixed[slot, RATE] * wet

        @pl.when(slot == OWN)
        def _():
            flow[substep] = outflow

            @pl.when(to_second)
            def _():
                flow_copy(substep, 2).start()

            @pl.when(to_next)
            def _():
                flow_copy(substep, 1).start()

            out_ref[0] = wet - outflow
            out_ref[1] = outflow

        @pl.when(slot == UP)
        def _():
            inflow[SUBSTEPS] = outflow

        level_ref[slot] = wet - outflow
        return carry

    lax.fori_loop(0, jnp.where(paired, 2 * SUBSTEPS, SUBSTEPS), turn, 0)

    for order in range(nset - 1):
        part_copy(order).wait_send()

    @pl.when(pushes)
    def _():
        each_chain(lambda chain: matrix_push(chain).wait_send())
        fixed_push().wait_send()

    @pl.when(jnp.logical_and(pushes, here > 0))
    def _():
        force_push().wait_send()

    @pl.when(starts)
    def _():
        for owner in range(firsts):
            first_copy(own_ref, owner, mine).wait_send()

    @pl.when(to_next)
    def _():
        for substep in range(SUBSTEPS):
            flow_copy(substep, 1).wait_send()

    @pl.when(to_second)
    def _():
        for substep in range(SUBSTEPS):
            flow_copy(substep, 2).wait_send()


def solution(mesh):
    npos, nset = mesh.shape["basin"], mesh.shape["tile"]

    def local(tile_water, tile_frac, tile_cell, storage, kappa, inverse, cell_mask, upstream):
        rows, width = storage.shape[1:]
        tiles = tile_water.shape[2]
        anywhere = pl.BlockSpec(memory_space=pltpu.HBM)
        vmem = pl.BlockSpec(memory_space=pltpu.VMEM)
        others = max(nset - 1, 1)
        out = pl.pallas_call(
            functools.partial(kernel, npos, nset),
            out_shape=pltpu.VMEM((2, rows, width), jnp.float32),
            in_specs=[anywhere] * 8,
            out_specs=vmem,
            scratch_shapes=[
                pltpu.VMEM(storage.shape, jnp.float32),
                pltpu.VMEM(kappa.shape, jnp.float32),
                pltpu.VMEM(cell_mask.shape, jnp.int32),
                pltpu.SMEM(upstream.shape, jnp.int32),
                pltpu.VMEM((nset, rows, tiles), jnp.float32),
                pltpu.VMEM((nset, rows, tiles), jnp.float32),
                pltpu.VMEM((nset, rows, tiles), jnp.int32),
                pltpu.VMEM((2, rows, width, width), jnp.float32),
                pltpu.VMEM((2, rows // 2, width, width), jnp.bfloat16),
                pltpu.VMEM((2, rows // 2, width, width), jnp.bfloat16),
                pltpu.VMEM((others, rows, width), jnp.float32),
                pltpu.VMEM((others, rows, width), jnp.float32),
                pltpu.VMEM((SUBSTEPS, rows, width), jnp.float32),
                pltpu.VMEM((SUBSTEPS + 1, rows, width), jnp.float32),
                pltpu.VMEM((2, 5, rows, width), jnp.float32),
                pltpu.VMEM((nset, rows, width), jnp.float32),
                pltpu.VMEM((2, rows, width), jnp.float32),
                pltpu.VMEM((rows, width), jnp.float32),
                pltpu.SemaphoreType.DMA((4,)),
                pltpu.SemaphoreType.DMA((nset, 3)),
                pltpu.SemaphoreType.DMA((1,)),
                pltpu.SemaphoreType.DMA((others,)),
                pltpu.SemaphoreType.DMA((others,)),
                pltpu.SemaphoreType.DMA((2, SUBSTEPS)),
                pltpu.SemaphoreType.DMA((SUBSTEPS,)),
                pltpu.SemaphoreType.DMA((rows,)),
                pltpu.SemaphoreType.DMA((rows,)),
                pltpu.SemaphoreType.DMA((2,)),
                pltpu.SemaphoreType.DMA((2,)),
                pltpu.SemaphoreType.DMA((nset,)),
                pltpu.SemaphoreType.DMA((nset,)),
                pltpu.SemaphoreType.REGULAR,
            ],
            compiler_params=pltpu.CompilerParams(collective_id=0, has_side_effects=True, vmem_limit_bytes=60 * 2**20),
        )(tile_water, tile_frac, tile_cell, storage, kappa, inverse, cell_mask, upstream)
        return out[:1], out[1:]

    tiled = P("basin", None, "tile")
    chain = P("basin", "tile", None)
    return jax.shard_map(
        local,
        mesh=mesh,
        in_specs=(tiled, tiled, tiled, chain, chain, P("basin", "tile", None, None), chain, P("basin", "tile")),
        out_specs=(chain, chain),
        check_vma=False,
    )
```

```python
import functools

import jax
import jax.numpy as jnp
from jax import lax
from jax.experimental import pallas as pl
from jax.experimental.pallas import tpu as pltpu
from jax.sharding import PartitionSpec as P

SUBSTEPS = 3
time_step = 0.5
MESH = pl.DeviceIdType.MESH
NT = (((1,), (1,)), ((), ()))
UP, OWN = 0, 1
RATE, LIVE, LINK, START, FORCE = range(5)


def two_terms(value):
    head = value.astype(jnp.bfloat16)
    return head, (value - head.astype(jnp.float32)).astype(jnp.bfloat16)


def iota(shape, axis):
    return lax.broadcasted_iota(jnp.int32, shape, axis)


def kernel(npos, nset, water_hbm, frac_hbm, cell_hbm, storage_hbm, kappa_hbm, inverse_hbm, mask_hbm, upstream_hbm,
           out_ref,
           storage_ref, kappa_ref, mask_ref, upstream_ref, water, frac, cell, inverse, heads, tails, part, arrived, flow, inflow,
           fixed, gathered, level_ref, own_ref,
           small_sem, tile_sem, inverse_sem, part_send, part_recv, flow_send, flow_recv, push_send, push_recv, fixed_send, fixed_recv, first_send, first_recv, go):
    rows, width = storage_ref.shape[1], storage_ref.shape[2]
    half = rows // 2
    here = lax.axis_index("basin")
    mine = lax.axis_index("tile")
    odd = lax.rem(here, 2) == 1
    firsts = 1
    paired = jnp.logical_and(odd, jnp.logical_or(here > 2, mine < firsts))

    def pushing(tile):
        return jnp.logical_and(jnp.logical_and(jnp.logical_not(odd), here < npos - 1), jnp.logical_or(here > 1, tile < firsts))

    pushes = pushing(mine)
    to_next = jnp.logical_and(jnp.logical_or(odd, jnp.logical_and(here == 0, mine >= firsts)), here < npos - 1)
    starts = jnp.logical_and(here == 0, npos > 1)
    gathers = jnp.logical_and(here == 1, mine < firsts)
    to_second = jnp.logical_and(odd, here < npos - 2)

    late = mine >= 2

    def owner_of(order):
        other = order + (order >= mine).astype(jnp.int32)
        other = jnp.where(jnp.logical_and(late, other < 2), 1 - other, other)
        return jnp.where(order == nset - 1, mine, other)

    def tile_loads(order):
        owner = owner_of(order)
        where = pl.ds(pl.multiple_of(owner * rows, rows), rows)
        return [
            pltpu.make_async_copy(source.at[0, where], target.at[order], tile_sem.at[order, at])
            for at, (source, target) in enumerate(((cell_hbm, cell), (water_hbm, water), (frac_hbm, frac)))]

    for copy in tile_loads(0):
        copy.start()

    barrier = pltpu.get_barrier_semaphore()
    for step in range(1, nset):
        other = lax.rem(mine + step, nset)
        pl.semaphore_signal(barrier, inc=1, device_id={"basin": here + pushing(other).astype(jnp.int32), "tile": other}, device_id_type=MESH)

    @pl.when(gathers)
    def _():
        for other in range(firsts, nset):
            pl.semaphore_signal(barrier, inc=1, device_id={"basin": 0, "tile": other}, device_id_type=MESH)

    @pl.when(pushes)
    def _():
        pl.semaphore_signal(barrier, inc=1, device_id={"basin": here + 1}, device_id_type=MESH)

    @pl.when(here > 0)
    def _():
        pl.semaphore_signal(barrier, inc=1, device_id={"basin": here - 1}, device_id_type=MESH)

    @pl.when(jnp.logical_and(paired, here > 2))
    def _():
        pl.semaphore_signal(barrier, inc=1, device_id={"basin": here - 2}, device_id_type=MESH)

    for order in range(1, nset):
        for copy in tile_loads(order):
            copy.start()
    small_loads = []
    for at, (source, target) in enumerate(((storage_hbm, storage_ref), (kappa_hbm, kappa_ref), (mask_hbm, mask_ref), (upstream_hbm, upstream_ref))):
        small_loads.append(pltpu.make_async_copy(source, target, small_sem.at[at]))

    matrix_load = pltpu.make_async_copy(inverse_hbm.at[0], inverse.at[OWN], inverse_sem.at[0])

    def matrix_push(chain):
        return pltpu.make_async_remote_copy(
            src_ref=inverse_hbm.at[0, chain], dst_ref=inverse.at[UP, chain],
            send_sem=push_send.at[chain], recv_sem=push_recv.at[chain],
            device_id={"basin": lax.rem(here + 1, npos)}, device_id_type=MESH)

    def fixed_push():
        return pltpu.make_async_remote_copy(
            src_ref=fixed.at[OWN, pl.ds(0, FORCE)], dst_ref=fixed.at[UP, pl.ds(0, FORCE)], send_sem=fixed_send.at[0], recv_sem=fixed_recv.at[0],
            device_id={"basin": lax.rem(here + 1, npos)}, device_id_type=MESH)

    def force_push():
        return pltpu.make_async_remote_copy(
            src_ref=fixed.at[OWN, FORCE], dst_ref=fixed.at[UP, FORCE], send_sem=fixed_send.at[1], recv_sem=fixed_recv.at[1],
            device_id={"basin": lax.rem(here + 1, npos)}, device_id_type=MESH)

    def first_copy(source, owner, slot):
        return pltpu.make_async_remote_copy(
            src_ref=source, dst_ref=gathered.at[slot], send_sem=first_send.at[owner], recv_sem=first_recv.at[slot],
            device_id={"basin": min(1, npos - 1), "tile": owner}, device_id_type=MESH)

    def part_copy(order):
        owner = owner_of(order)
        slot = mine - (mine > owner).astype(jnp.int32)
        return pltpu.make_async_remote_copy(
            src_ref=part.at[order], dst_ref=arrived.at[slot],
            send_sem=part_send.at[order], recv_sem=part_recv.at[slot],
            device_id={"tile": owner}, device_id_type=MESH)

    def part_arrival(slot):
        return pltpu.make_async_remote_copy(
            src_ref=part.at[slot], dst_ref=arrived.at[slot],
            send_sem=part_send.at[slot], recv_sem=part_recv.at[slot],
            device_id={"tile": owner_of(slot)}, device_id_type=MESH)

    def flow_copy(substep, ahead):
        return pltpu.make_async_remote_copy(
            src_ref=flow.at[substep], dst_ref=inflow.at[substep],
            send_sem=flow_send.at[ahead - 1, substep], recv_sem=flow_recv.at[substep],
            device_id={"basin": lax.rem(here + ahead, npos)}, device_id_type=MESH)

    def each_chain(do):
        def one(chain, carry):
            do(chain)
            return carry
        lax.fori_loop(0, rows, one, 0)

    @pl.when(pushes)
    def _():
        pl.semaphore_wait(barrier, 1)
        each_chain(lambda chain: matrix_push(chain).start())

    lane = lax.rem(iota((rows, width), 1), rows)
    row = iota((rows, width), 0)

    def cell_sums(order):
        cells = cell[order]
        shift = lax.rem(cells - iota(cells.shape, 0) + rows, rows).astype(jnp.float32).astype(jnp.bfloat16)
        upper = (cells // rows).astype(jnp.float32).astype(jnp.bfloat16)
        head, tail = two_terms(frac[order] * water[order])
        zero = jnp.zeros_like(head)
        one = jnp.ones_like(head)
        picks = [shift == jnp.bfloat16(at) for at in range(rows)]
        left = jnp.concatenate([jnp.where(pick, head, zero) for pick in picks] + [jnp.where(pick, tail, zero) for pick in picks], axis=0)
        right = jnp.concatenate([jnp.where(upper == jnp.bfloat16(at), one, zero) for at in range(width // rows)], axis=0)
        both = lax.dot_general(left, right, NT, preferred_element_type=jnp.float32)
        terms = []
        for at in range(rows):
            start = at * rows
            single = jnp.where(lane == row, both[start:start + rows] + both[rows * rows + start:rows * rows + start + rows], 0.0)
            terms.append(pltpu.roll(single, at, 1) if at else single)
        while len(terms) > 1:
            terms = [sum(terms[at:at + 2][1:], terms[at]) for at in range(0, len(terms), 2)]
        return jnp.where(lane < row, pltpu.roll(terms[0], width - rows, 1), terms[0])

    hold = jnp.maximum(nset - 1 - 2 * mine, 0)

    def group(order, carry):
        for copy in tile_loads(order):
            copy.wait()
        sums = cell_sums(order)

        @pl.when(order < nset - 1)
        def _():
            part[order] = sums

        @pl.when(order == nset - 1)
        def _():
            own_ref[...] = sums

        @pl.when(jnp.logical_and(order == hold, jnp.logical_not(pushes)))
        def _():
            pl.semaphore_wait(barrier, (nset - 1) * (1 + paired.astype(jnp.int32)) + paired.astype(jnp.int32)
                              + to_next.astype(jnp.int32) + to_second.astype(jnp.int32) + starts.astype(jnp.int32) * firsts)

            @pl.when(paired)
            def _():
                pl.semaphore_signal(go, inc=1, device_id={"basin": here - 1}, device_id_type=MESH)

        @pl.when(jnp.logical_and(order == hold, pushes))
        def _():
            pl.semaphore_wait(go, 1)

        for owner in range(firsts):
            at = owner - (owner > mine).astype(jnp.int32)
            at = jnp.where(jnp.logical_and(late, owner < 2), 1 - at, at)

            @pl.when(jnp.logical_and(jnp.logical_and(starts, mine != owner), order == jnp.maximum(hold, at)))
            def _():
                first_copy(part.at[at], owner, mine).start()

            @pl.when(jnp.logical_and(jnp.logical_and(starts, mine == owner), order == nset - 1))
            def _():
                first_copy(own_ref, owner, mine).start()

        for done in reversed(range(nset - 1)):
            @pl.when(jnp.logical_or(jnp.logical_and(order == hold, done <= order), jnp.logical_and(order > hold, done == order)))
            def _():
                part_copy(done).start()

        @pl.when(order == 0)
        def _():
            for copy in small_loads:
                copy.start()
            matrix_load.start()

        return carry

    lax.fori_loop(0, nset, group, 0)

    for copy in small_loads:
        copy.wait()
    links = jnp.zeros((rows, width), jnp.int32)
    for chain in range(rows):
        links = jnp.where(row == chain, upstream_ref[0, chain], links)
    fixed[OWN, LINK] = links.astype(jnp.float32)
    fixed[OWN, LIVE] = mask_ref[0].astype(jnp.float32)
    fixed[OWN, RATE] = kappa_ref[0]
    fixed[OWN, START] = storage_ref[0]
    level_ref[OWN] = storage_ref[0]

    @pl.when(jnp.logical_or(here == 0, gathers))
    def _():
        inflow[...] = jnp.zeros_like(inflow)

    @pl.when(pushes)
    def _():
        fixed_push().start()

    def prepare(slot, ready):
        def one(chain, carry):
            ready(chain)
            head, tail = two_terms(inverse[slot, chain].T)
            heads[slot, chain] = head
            tails[slot, chain] = tail
            return carry

        def rest(chain, carry):
            ready(chain)
            return carry
        lax.fori_loop(0, half, one, 0)
        lax.fori_loop(half, rows, rest, 0)

    matrix_load.wait()
    prepare(OWN, lambda chain: None)

    picked = [lax.rem(iota((2 * half, width), 0), half) == chain for chain in range(half)]

    def product(slot, vector):
        head = vector.astype(jnp.bfloat16).astype(jnp.float32)
        tail = vector - head
        left = jnp.concatenate([head[:half], tail[:half]], axis=0).astype(jnp.bfloat16)
        first = jnp.zeros((2 * half, width), jnp.float32)
        second = jnp.zeros((2 * half, width), jnp.float32)
        reduced = []
        for chain in range(rows - half):
            if chain < half:
                single = jnp.where(picked[chain], left, jnp.zeros_like(left))
                first += jnp.dot(single, heads[slot, chain], preferred_element_type=jnp.float32)
                second += jnp.dot(single, tails[slot, chain], preferred_element_type=jnp.float32)
            other = half + chain
            reduced.append(jnp.sum(inverse[slot, other] * vector[other:other + 1], axis=1)[None])
        total = first + second
        return jnp.concatenate([total[:half] + total[half:]] + reduced, axis=0)

    @pl.when(paired)
    def _():
        prepare(UP, lambda chain: matrix_push(chain).wait_recv())
        fixed_push().wait_recv()
        level_ref[UP] = fixed[UP, START]

    runoff = own_ref[...]
    for order in range(nset - 1):
        part_arrival(order).wait_recv()
        runoff = runoff + arrived[order]
    fixed[OWN, FORCE] = time_step * runoff

    @pl.when(jnp.logical_and(pushes, here > 0))
    def _():
        force_push().start()

    @pl.when(jnp.logical_and(paired, here > 1))
    def _():
        force_push().wait_recv()

    @pl.when(gathers)
    def _():
        for slot in range(nset):
            first_copy(own_ref, 0, slot).wait_recv()
        fixed[UP, FORCE] = time_step * sum([gathered[slot] for slot in range(1, nset)], gathered[0])

    def turn(count, carry):
        slot = jnp.where(paired, lax.rem(count, 2), OWN)
        substep = jnp.where(paired, count // 2, count)
        leads = jnp.logical_or(jnp.logical_not(paired), slot == UP)

        @pl.when(jnp.logical_and(leads, jnp.logical_or(here > 1, jnp.logical_and(here == 1, mine >= firsts))))
        def _():
            flow_copy(substep, 1).wait_recv()

        came = inflow[jnp.where(leads, substep, SUBSTEPS)]
        links = fixed[slot, LINK].astype(jnp.int32)
        choices = [jnp.broadcast_to(came[chain:chain + 1], (rows, width)) for chain in range(rows)]
        bit = 1
        while len(choices) > 1:
            upper = (links & bit) != 0
            choices = [
                jnp.where(upper, choices[at + 1], choices[at]) if at + 1 < len(choices) else choices[at]
                for at in range(0, len(choices), 2)]
            bit *= 2
        incoming = choices[0]
        wet = fixed[slot, LIVE] * product(slot, level_ref[slot] + fixed[slot, FORCE] + incoming)
        outflow = fixed[slot, RATE] * wet

        @pl.when(slot == OWN)
        def _():
            flow[substep] = outflow

            @pl.when(to_second)
            def _():
                flow_copy(substep, 2).start()

            @pl.when(to_next)
            def _():
                flow_copy(substep, 1).start()

            out_ref[0] = wet - outflow
            out_ref[1] = outflow

        @pl.when(slot == UP)
        def _():
            inflow[SUBSTEPS] = outflow

        level_ref[slot] = wet - outflow
        return carry

    lax.fori_loop(0, jnp.where(paired, 2 * SUBSTEPS, SUBSTEPS), turn, 0)

    for order in range(nset - 1):
        part_copy(order).wait_send()

    @pl.when(pushes)
    def _():
        each_chain(lambda chain: matrix_push(chain).wait_send())
        fixed_push().wait_send()

    @pl.when(jnp.logical_and(pushes, here > 0))
    def _():
        force_push().wait_send()

    @pl.when(starts)
    def _():
        for owner in range(firsts):
            first_copy(own_ref, owner, mine).wait_send()

    @pl.when(to_next)
    def _():
        for substep in range(SUBSTEPS):
            flow_copy(substep, 1).wait_send()

    @pl.when(to_second)
    def _():
        for substep in range(SUBSTEPS):
            flow_copy(substep, 2).wait_send()


def solution(mesh):
    npos, nset = mesh.shape["basin"], mesh.shape["tile"]

    def local(tile_water, tile_frac, tile_cell, storage, kappa, inverse, cell_mask, upstream):
        rows, width = storage.shape[1:]
        tiles = tile_water.shape[2]
        anywhere = pl.BlockSpec(memory_space=pltpu.HBM)
        vmem = pl.BlockSpec(memory_space=pltpu.VMEM)
        others = max(nset - 1, 1)
        out = pl.pallas_call(
            functools.partial(kernel, npos, nset),
            out_shape=pltpu.VMEM((2, rows, width), jnp.float32),
            in_specs=[anywhere] * 8,
            out_specs=vmem,
            scratch_shapes=[
                pltpu.VMEM(storage.shape, jnp.float32),
                pltpu.VMEM(kappa.shape, jnp.float32),
                pltpu.VMEM(cell_mask.shape, jnp.int32),
                pltpu.SMEM(upstream.shape, jnp.int32),
                pltpu.VMEM((nset, rows, tiles), jnp.float32),
                pltpu.VMEM((nset, rows, tiles), jnp.float32),
                pltpu.VMEM((nset, rows, tiles), jnp.int32),
                pltpu.VMEM((2, rows, width, width), jnp.float32),
                pltpu.VMEM((2, rows // 2, width, width), jnp.bfloat16),
                pltpu.VMEM((2, rows // 2, width, width), jnp.bfloat16),
                pltpu.VMEM((others, rows, width), jnp.float32),
                pltpu.VMEM((others, rows, width), jnp.float32),
                pltpu.VMEM((SUBSTEPS, rows, width), jnp.float32),
                pltpu.VMEM((SUBSTEPS + 1, rows, width), jnp.float32),
                pltpu.VMEM((2, 5, rows, width), jnp.float32),
                pltpu.VMEM((nset, rows, width), jnp.float32),
                pltpu.VMEM((2, rows, width), jnp.float32),
                pltpu.VMEM((rows, width), jnp.float32),
                pltpu.SemaphoreType.DMA((4,)),
                pltpu.SemaphoreType.DMA((nset, 3)),
                pltpu.SemaphoreType.DMA((1,)),
                pltpu.SemaphoreType.DMA((others,)),
                pltpu.SemaphoreType.DMA((others,)),
                pltpu.SemaphoreType.DMA((2, SUBSTEPS)),
                pltpu.SemaphoreType.DMA((SUBSTEPS,)),
                pltpu.SemaphoreType.DMA((rows,)),
                pltpu.SemaphoreType.DMA((rows,)),
                pltpu.SemaphoreType.DMA((2,)),
                pltpu.SemaphoreType.DMA((2,)),
                pltpu.SemaphoreType.DMA((nset,)),
                pltpu.SemaphoreType.DMA((nset,)),
                pltpu.SemaphoreType.REGULAR,
            ],
            compiler_params=pltpu.CompilerParams(collective_id=0, has_side_effects=True, vmem_limit_bytes=60 * 2**20),
        )(tile_water, tile_frac, tile_cell, storage, kappa, inverse, cell_mask, upstream)
        return out[:1], out[1:]

    tiled = P("basin", None, "tile")
    chain = P("basin", "tile", None)
    return jax.shard_map(
        local,
        mesh=mesh,
        in_specs=(tiled, tiled, tiled, chain, chain, P("basin", "tile", None, None), chain, P("basin", "tile")),
        out_specs=(chain, chain),
        check_vma=False,
    )
```

```python
import functools

import jax
import jax.numpy as jnp
from jax import lax
from jax.experimental import pallas as pl
from jax.experimental.pallas import tpu as pltpu
from jax.sharding import PartitionSpec as P

SUBSTEPS = 3
time_step = 0.5
MESH = pl.DeviceIdType.MESH
NT = (((1,), (1,)), ((), ()))
UP, OWN = 0, 1
RATE, LIVE, LINK, START, FORCE = range(5)


def two_terms(value):
    head = value.astype(jnp.bfloat16)
    return head, (value - head.astype(jnp.float32)).astype(jnp.bfloat16)


def iota(shape, axis):
    return lax.broadcasted_iota(jnp.int32, shape, axis)


def kernel(npos, nset, water_hbm, frac_hbm, cell_hbm, storage_hbm, kappa_hbm, inverse_hbm, mask_hbm, upstream_hbm,
           out_ref,
           storage_ref, kappa_ref, mask_ref, upstream_ref, water, frac, cell, inverse, heads, tails, part, arrived, flow, inflow,
           fixed, gathered, level_ref, own_ref,
           small_sem, tile_sem, inverse_sem, part_send, part_recv, flow_send, flow_recv, push_send, push_recv, fixed_send, fixed_recv, first_send, first_recv, go):
    rows, width = storage_ref.shape[1], storage_ref.shape[2]
    half = rows // 2
    here = lax.axis_index("basin")
    mine = lax.axis_index("tile")
    odd = lax.rem(here, 2) == 1
    firsts = 1
    paired = jnp.logical_and(odd, jnp.logical_or(here > 2, mine < firsts))

    def pushing(tile):
        return jnp.logical_and(jnp.logical_and(jnp.logical_not(odd), here < npos - 1), jnp.logical_or(here > 1, tile < firsts))

    pushes = pushing(mine)
    to_next = jnp.logical_and(jnp.logical_or(odd, jnp.logical_and(here == 0, mine >= firsts)), here < npos - 1)
    starts = jnp.logical_and(here == 0, npos > 1)
    gathers = jnp.logical_and(here == 1, mine < firsts)
    to_second = jnp.logical_and(odd, here < npos - 2)

    late = mine >= 2

    def owner_of(order):
        other = order + (order >= mine).astype(jnp.int32)
        other = jnp.where(jnp.logical_and(late, other < 2), 1 - other, other)
        return jnp.where(order == nset - 1, mine, other)

    def tile_loads(order):
        owner = owner_of(order)
        where = pl.ds(pl.multiple_of(owner * rows, rows), rows)
        return [
            pltpu.make_async_copy(source.at[0, where], target.at[order], tile_sem.at[order, at])
            for at, (source, target) in enumerate(((cell_hbm, cell), (water_hbm, water), (frac_hbm, frac)))]

    for copy in tile_loads(0):
        copy.start()

    barrier = pltpu.get_barrier_semaphore()
    for step in range(1, nset):
        other = lax.rem(mine + step, nset)
        pl.semaphore_signal(barrier, inc=1, device_id={"basin": here + pushing(other).astype(jnp.int32), "tile": other}, device_id_type=MESH)

    @pl.when(gathers)
    def _():
        for other in range(firsts, nset):
            pl.semaphore_signal(barrier, inc=1, device_id={"basin": 0, "tile": other}, device_id_type=MESH)

    @pl.when(pushes)
    def _():
        pl.semaphore_signal(barrier, inc=1, device_id={"basin": here + 1}, device_id_type=MESH)

    @pl.when(here > 0)
    def _():
        pl.semaphore_signal(barrier, inc=1, device_id={"basin": here - 1}, device_id_type=MESH)

    @pl.when(jnp.logical_and(paired, here > 2))
    def _():
        pl.semaphore_signal(barrier, inc=1, device_id={"basin": here - 2}, device_id_type=MESH)

    for order in range(1, nset):
        for copy in tile_loads(order):
            copy.start()
    small_loads = []
    for at, (source, target) in enumerate(((storage_hbm, storage_ref), (kappa_hbm, kappa_ref), (mask_hbm, mask_ref), (upstream_hbm, upstream_ref))):
        small_loads.append(pltpu.make_async_copy(source, target, small_sem.at[at]))

    matrix_load = pltpu.make_async_copy(inverse_hbm.at[0], inverse.at[OWN], inverse_sem.at[0])

    def matrix_push(chain):
        return pltpu.make_async_remote_copy(
            src_ref=inverse_hbm.at[0, chain], dst_ref=inverse.at[UP, chain],
            send_sem=push_send.at[chain], recv_sem=push_recv.at[chain],
            device_id={"basin": lax.rem(here + 1, npos)}, device_id_type=MESH)

    def fixed_push():
        return pltpu.make_async_remote_copy(
            src_ref=fixed.at[OWN, pl.ds(0, FORCE)], dst_ref=fixed.at[UP, pl.ds(0, FORCE)], send_sem=fixed_send.at[0], recv_sem=fixed_recv.at[0],
            device_id={"basin": lax.rem(here + 1, npos)}, device_id_type=MESH)

    def force_push():
        return pltpu.make_async_remote_copy(
            src_ref=fixed.at[OWN, FORCE], dst_ref=fixed.at[UP, FORCE], send_sem=fixed_send.at[1], recv_sem=fixed_recv.at[1],
            device_id={"basin": lax.rem(here + 1, npos)}, device_id_type=MESH)

    def first_copy(source, owner, slot):
        return pltpu.make_async_remote_copy(
            src_ref=source, dst_ref=gathered.at[slot], send_sem=first_send.at[owner], recv_sem=first_recv.at[slot],
            device_id={"basin": min(1, npos - 1), "tile": owner}, device_id_type=MESH)

    def part_copy(order):
        owner = owner_of(order)
        slot = mine - (mine > owner).astype(jnp.int32)
        return pltpu.make_async_remote_copy(
            src_ref=part.at[order], dst_ref=arrived.at[slot],
            send_sem=part_send.at[order], recv_sem=part_recv.at[slot],
            device_id={"tile": owner}, device_id_type=MESH)

    def part_arrival(slot):
        return pltpu.make_async_remote_copy(
            src_ref=part.at[slot], dst_ref=arrived.at[slot],
            send_sem=part_send.at[slot], recv_sem=part_recv.at[slot],
            device_id={"tile": owner_of(slot)}, device_id_type=MESH)

    def flow_copy(substep, ahead):
        return pltpu.make_async_remote_copy(
            src_ref=flow.at[substep], dst_ref=inflow.at[substep],
            send_sem=flow_send.at[ahead - 1, substep], recv_sem=flow_recv.at[substep],
            device_id={"basin": lax.rem(here + ahead, npos)}, device_id_type=MESH)

    def each_chain(do):
        def one(chain, carry):
            do(chain)
            return carry
        lax.fori_loop(0, rows, one, 0)

    @pl.when(pushes)
    def _():
        pl.semaphore_wait(barrier, 1)
        each_chain(lambda chain: matrix_push(chain).start())

    lane = lax.rem(iota((rows, width), 1), rows)
    row = iota((rows, width), 0)

    def cell_sums(order):
        cells = cell[order]
        ahead = cells - iota(cells.shape, 0)
        if rows & (rows - 1):
            shift, upper = lax.rem(ahead + rows, rows), cells // rows
        else:
            shift, upper = ahead & (rows - 1), cells >> (rows.bit_length() - 1)
        shift = shift.astype(jnp.float32).astype(jnp.bfloat16)
        upper = upper.astype(jnp.float32).astype(jnp.bfloat16)
        head, tail = two_terms(frac[order] * water[order])
        zero = jnp.zeros_like(head)
        one = jnp.ones_like(head)
        picks = [shift == jnp.bfloat16(at) for at in range(rows)]
        left = jnp.concatenate([jnp.where(pick, head, zero) for pick in picks] + [jnp.where(pick, tail, zero) for pick in picks], axis=0)
        right = jnp.concatenate([jnp.where(upper == jnp.bfloat16(at), one, zero) for at in range(width // rows)], axis=0)
        both = lax.dot_general(left, right, NT, preferred_element_type=jnp.float32)
        terms = []
        for at in range(rows):
            start = at * rows
            single = jnp.where(lane == row, both[start:start + rows] + both[rows * rows + start:rows * rows + start + rows], 0.0)
            terms.append(pltpu.roll(single, at, 1) if at else single)
        while len(terms) > 1:
            terms = [sum(terms[at:at + 2][1:], terms[at]) for at in range(0, len(terms), 2)]
        return jnp.where(lane < row, pltpu.roll(terms[0], width - rows, 1), terms[0])

    hold = jnp.maximum(nset - 1 - 2 * mine, 0)

    def group(order, carry):
        for copy in tile_loads(order):
            copy.wait()
        sums = cell_sums(order)

        @pl.when(order < nset - 1)
        def _():
            part[order] = sums

        @pl.when(order == nset - 1)
        def _():
            own_ref[...] = sums

        @pl.when(jnp.logical_and(order == hold, jnp.logical_not(pushes)))
        def _():
            pl.semaphore_wait(barrier, (nset - 1) * (1 + paired.astype(jnp.int32)) + paired.astype(jnp.int32)
                              + to_next.astype(jnp.int32) + to_second.astype(jnp.int32) + starts.astype(jnp.int32) * firsts)

            @pl.when(paired)
            def _():
                pl.semaphore_signal(go, inc=1, device_id={"basin": here - 1}, device_id_type=MESH)

        @pl.when(jnp.logical_and(order == hold, pushes))
        def _():
            pl.semaphore_wait(go, 1)

        for owner in range(firsts):
            at = owner - (owner > mine).astype(jnp.int32)
            at = jnp.where(jnp.logical_and(late, owner < 2), 1 - at, at)

            @pl.when(jnp.logical_and(jnp.logical_and(starts, mine != owner), order == jnp.maximum(hold, at)))
            def _():
                first_copy(part.at[at], owner, mine).start()

            @pl.when(jnp.logical_and(jnp.logical_and(starts, mine == owner), order == nset - 1))
            def _():
                first_copy(own_ref, owner, mine).start()

        for done in reversed(range(nset - 1)):
            @pl.when(jnp.logical_or(jnp.logical_and(order == hold, done <= order), jnp.logical_and(order > hold, done == order)))
            def _():
                part_copy(done).start()

        @pl.when(order == 0)
        def _():
            for copy in small_loads:
                copy.start()
            matrix_load.start()

        return carry

    lax.fori_loop(0, nset, group, 0)

    for copy in small_loads:
        copy.wait()
    links = jnp.zeros((rows, width), jnp.int32)
    for chain in range(rows):
        links = jnp.where(row == chain, upstream_ref[0, chain], links)
    fixed[OWN, LINK] = links.astype(jnp.float32)
    fixed[OWN, LIVE] = mask_ref[0].astype(jnp.float32)
    fixed[OWN, RATE] = kappa_ref[0]
    fixed[OWN, START] = storage_ref[0]
    level_ref[OWN] = storage_ref[0]

    @pl.when(jnp.logical_or(here == 0, gathers))
    def _():
        inflow[...] = jnp.zeros_like(inflow)

    @pl.when(pushes)
    def _():
        fixed_push().start()

    def prepare(slot, ready):
        def one(chain, carry):
            ready(chain)
            head, tail = two_terms(inverse[slot, chain].T)
            heads[slot, chain] = head
            tails[slot, chain] = tail
            return carry

        def rest(chain, carry):
            ready(chain)
            return carry
        lax.fori_loop(0, half, one, 0)
        lax.fori_loop(half, rows, rest, 0)

    matrix_load.wait()
    prepare(OWN, lambda chain: None)

    picked = [lax.rem(iota((2 * half, width), 0), half) == chain for chain in range(half)]

    def product(slot, vector):
        head = vector.astype(jnp.bfloat16).astype(jnp.float32)
        tail = vector - head
        left = jnp.concatenate([head[:half], tail[:half]], axis=0).astype(jnp.bfloat16)
        first = jnp.zeros((2 * half, width), jnp.float32)
        second = jnp.zeros((2 * half, width), jnp.float32)
        reduced = []
        for chain in range(rows - half):
            if chain < half:
                single = jnp.where(picked[chain], left, jnp.zeros_like(left))
                first += jnp.dot(single, heads[slot, chain], preferred_element_type=jnp.float32)
                second += jnp.dot(single, tails[slot, chain], preferred_element_type=jnp.float32)
            other = half + chain
            reduced.append(jnp.sum(inverse[slot, other] * vector[other:other + 1], axis=1)[None])
        total = first + second
        return jnp.concatenate([total[:half] + total[half:]] + reduced, axis=0)

    @pl.when(paired)
    def _():
        prepare(UP, lambda chain: matrix_push(chain).wait_recv())
        fixed_push().wait_recv()
        level_ref[UP] = fixed[UP, START]

    runoff = own_ref[...]
    for order in range(nset - 1):
        part_arrival(order).wait_recv()
        runoff = runoff + arrived[order]
    fixed[OWN, FORCE] = time_step * runoff

    @pl.when(jnp.logical_and(pushes, here > 0))
    def _():
        force_push().start()

    @pl.when(jnp.logical_and(paired, here > 1))
    def _():
        force_push().wait_recv()

    @pl.when(gathers)
    def _():
        for slot in range(nset):
            first_copy(own_ref, 0, slot).wait_recv()
        fixed[UP, FORCE] = time_step * sum([gathered[slot] for slot in range(1, nset)], gathered[0])

    def turn(count, carry):
        slot = jnp.where(paired, lax.rem(count, 2), OWN)
        substep = jnp.where(paired, count // 2, count)
        leads = jnp.logical_or(jnp.logical_not(paired), slot == UP)

        @pl.when(jnp.logical_and(leads, jnp.logical_or(here > 1, jnp.logical_and(here == 1, mine >= firsts))))
        def _():
            flow_copy(substep, 1).wait_recv()

        came = inflow[jnp.where(leads, substep, SUBSTEPS)]
        links = fixed[slot, LINK].astype(jnp.int32)
        choices = [jnp.broadcast_to(came[chain:chain + 1], (rows, width)) for chain in range(rows)]
        bit = 1
        while len(choices) > 1:
            upper = (links & bit) != 0
            choices = [
                jnp.where(upper, choices[at + 1], choices[at]) if at + 1 < len(choices) else choices[at]
                for at in range(0, len(choices), 2)]
            bit *= 2
        incoming = choices[0]
        wet = fixed[slot, LIVE] * product(slot, level_ref[slot] + fixed[slot, FORCE] + incoming)
        outflow = fixed[slot, RATE] * wet

        @pl.when(slot == OWN)
        def _():
            flow[substep] = outflow

            @pl.when(to_second)
            def _():
                flow_copy(substep, 2).start()

            @pl.when(to_next)
            def _():
                flow_copy(substep, 1).start()

            out_ref[0] = wet - outflow
            out_ref[1] = outflow

        @pl.when(slot == UP)
        def _():
            inflow[SUBSTEPS] = outflow

        level_ref[slot] = wet - outflow
        return carry

    lax.fori_loop(0, jnp.where(paired, 2 * SUBSTEPS, SUBSTEPS), turn, 0)

    for order in range(nset - 1):
        part_copy(order).wait_send()

    @pl.when(pushes)
    def _():
        each_chain(lambda chain: matrix_push(chain).wait_send())
        fixed_push().wait_send()

    @pl.when(jnp.logical_and(pushes, here > 0))
    def _():
        force_push().wait_send()

    @pl.when(starts)
    def _():
        for owner in range(firsts):
            first_copy(own_ref, owner, mine).wait_send()

    @pl.when(to_next)
    def _():
        for substep in range(SUBSTEPS):
            flow_copy(substep, 1).wait_send()

    @pl.when(to_second)
    def _():
        for substep in range(SUBSTEPS):
            flow_copy(substep, 2).wait_send()


def solution(mesh):
    npos, nset = mesh.shape["basin"], mesh.shape["tile"]

    def local(tile_water, tile_frac, tile_cell, storage, kappa, inverse, cell_mask, upstream):
        rows, width = storage.shape[1:]
        tiles = tile_water.shape[2]
        anywhere = pl.BlockSpec(memory_space=pltpu.HBM)
        vmem = pl.BlockSpec(memory_space=pltpu.VMEM)
        others = max(nset - 1, 1)
        out = pl.pallas_call(
            functools.partial(kernel, npos, nset),
            out_shape=pltpu.VMEM((2, rows, width), jnp.float32),
            in_specs=[anywhere] * 8,
            out_specs=vmem,
            scratch_shapes=[
                pltpu.VMEM(storage.shape, jnp.float32),
                pltpu.VMEM(kappa.shape, jnp.float32),
                pltpu.VMEM(cell_mask.shape, jnp.int32),
                pltpu.SMEM(upstream.shape, jnp.int32),
                pltpu.VMEM((nset, rows, tiles), jnp.float32),
                pltpu.VMEM((nset, rows, tiles), jnp.float32),
                pltpu.VMEM((nset, rows, tiles), jnp.int32),
                pltpu.VMEM((2, rows, width, width), jnp.float32),
                pltpu.VMEM((2, rows // 2, width, width), jnp.bfloat16),
                pltpu.VMEM((2, rows // 2, width, width), jnp.bfloat16),
                pltpu.VMEM((others, rows, width), jnp.float32),
                pltpu.VMEM((others, rows, width), jnp.float32),
                pltpu.VMEM((SUBSTEPS, rows, width), jnp.float32),
                pltpu.VMEM((SUBSTEPS + 1, rows, width), jnp.float32),
                pltpu.VMEM((2, 5, rows, width), jnp.float32),
                pltpu.VMEM((nset, rows, width), jnp.float32),
                pltpu.VMEM((2, rows, width), jnp.float32),
                pltpu.VMEM((rows, width), jnp.float32),
                pltpu.SemaphoreType.DMA((4,)),
                pltpu.SemaphoreType.DMA((nset, 3)),
                pltpu.SemaphoreType.DMA((1,)),
                pltpu.SemaphoreType.DMA((others,)),
                pltpu.SemaphoreType.DMA((others,)),
                pltpu.SemaphoreType.DMA((2, SUBSTEPS)),
                pltpu.SemaphoreType.DMA((SUBSTEPS,)),
                pltpu.SemaphoreType.DMA((rows,)),
                pltpu.SemaphoreType.DMA((rows,)),
                pltpu.SemaphoreType.DMA((2,)),
                pltpu.SemaphoreType.DMA((2,)),
                pltpu.SemaphoreType.DMA((nset,)),
                pltpu.SemaphoreType.DMA((nset,)),
                pltpu.SemaphoreType.REGULAR,
            ],
            compiler_params=pltpu.CompilerParams(collective_id=0, has_side_effects=True, vmem_limit_bytes=60 * 2**20),
        )(tile_water, tile_frac, tile_cell, storage, kappa, inverse, cell_mask, upstream)
        return out[:1], out[1:]

    tiled = P("basin", None, "tile")
    chain = P("basin", "tile", None)
    return jax.shard_map(
        local,
        mesh=mesh,
        in_specs=(tiled, tiled, tiled, chain, chain, P("basin", "tile", None, None), chain, P("basin", "tile")),
        out_specs=(chain, chain),
        check_vma=False,
    )
```

```python
import functools

import jax
import jax.numpy as jnp
from jax import lax
from jax.experimental import pallas as pl
from jax.experimental.pallas import tpu as pltpu
from jax.sharding import PartitionSpec as P

SUBSTEPS = 3
time_step = 0.5
MESH = pl.DeviceIdType.MESH
NT = (((1,), (1,)), ((), ()))
UP, OWN = 0, 1
RATE, LIVE, LINK, START, FORCE = range(5)


def two_terms(value):
    head = value.astype(jnp.bfloat16)
    return head, (value - head.astype(jnp.float32)).astype(jnp.bfloat16)


def iota(shape, axis):
    return lax.broadcasted_iota(jnp.int32, shape, axis)


def kernel(npos, nset, water_hbm, frac_hbm, cell_hbm, storage_hbm, kappa_hbm, inverse_hbm, mask_hbm, upstream_hbm,
           out_ref,
           storage_ref, kappa_ref, mask_ref, upstream_ref, water, frac, cell, inverse, heads, tails, part, arrived, flow, inflow,
           fixed, gathered, level_ref, own_ref,
           small_sem, tile_sem, inverse_sem, part_send, part_recv, flow_send, flow_recv, push_send, push_recv, fixed_send, fixed_recv, first_send, first_recv, go):
    rows, width = storage_ref.shape[1], storage_ref.shape[2]
    half = rows // 2
    here = lax.axis_index("basin")
    mine = lax.axis_index("tile")
    odd = lax.rem(here, 2) == 1
    firsts = 1
    paired = jnp.logical_and(odd, jnp.logical_or(here > 2, mine < firsts))

    def pushing(tile):
        return jnp.logical_and(jnp.logical_and(jnp.logical_not(odd), here < npos - 1), jnp.logical_or(here > 1, tile < firsts))

    pushes = pushing(mine)
    to_next = jnp.logical_and(jnp.logical_or(odd, jnp.logical_and(here == 0, mine >= firsts)), here < npos - 1)
    starts = jnp.logical_and(here == 0, npos > 1)
    gathers = jnp.logical_and(here == 1, mine < firsts)
    to_second = jnp.logical_and(odd, here < npos - 2)

    late = mine >= 2

    def owner_of(order):
        other = order + (order >= mine).astype(jnp.int32)
        other = jnp.where(jnp.logical_and(late, other < 2), 1 - other, other)
        return jnp.where(order == nset - 1, mine, other)

    def tile_loads(order):
        owner = owner_of(order)
        where = pl.ds(pl.multiple_of(owner * rows, rows), rows)
        return [
            pltpu.make_async_copy(source.at[0, where], target.at[order], tile_sem.at[order, at])
            for at, (source, target) in enumerate(((cell_hbm, cell), (water_hbm, water), (frac_hbm, frac)))]

    for copy in tile_loads(0):
        copy.start()

    barrier = pltpu.get_barrier_semaphore()
    for step in range(1, nset):
        other = lax.rem(mine + step, nset)
        pl.semaphore_signal(barrier, inc=1, device_id={"basin": here + pushing(other).astype(jnp.int32), "tile": other}, device_id_type=MESH)

    @pl.when(gathers)
    def _():
        for other in range(firsts, nset):
            pl.semaphore_signal(barrier, inc=1, device_id={"basin": 0, "tile": other}, device_id_type=MESH)

    @pl.when(pushes)
    def _():
        pl.semaphore_signal(barrier, inc=1, device_id={"basin": here + 1}, device_id_type=MESH)

    @pl.when(here > 0)
    def _():
        pl.semaphore_signal(barrier, inc=1, device_id={"basin": here - 1}, device_id_type=MESH)

    @pl.when(jnp.logical_and(paired, here > 2))
    def _():
        pl.semaphore_signal(barrier, inc=1, device_id={"basin": here - 2}, device_id_type=MESH)

    for order in range(1, nset):
        for copy in tile_loads(order):
            copy.start()
    small_loads = []
    for at, (source, target) in enumerate(((storage_hbm, storage_ref), (kappa_hbm, kappa_ref), (mask_hbm, mask_ref), (upstream_hbm, upstream_ref))):
        small_loads.append(pltpu.make_async_copy(source, target, small_sem.at[at]))

    matrix_load = pltpu.make_async_copy(inverse_hbm.at[0], inverse.at[OWN], inverse_sem.at[0])

    def matrix_push(chain):
        return pltpu.make_async_remote_copy(
            src_ref=inverse_hbm.at[0, chain], dst_ref=inverse.at[UP, chain],
            send_sem=push_send.at[chain], recv_sem=push_recv.at[chain],
            device_id={"basin": lax.rem(here + 1, npos)}, device_id_type=MESH)

    def fixed_push():
        return pltpu.make_async_remote_copy(
            src_ref=fixed.at[OWN, pl.ds(0, FORCE)], dst_ref=fixed.at[UP, pl.ds(0, FORCE)], send_sem=fixed_send.at[0], recv_sem=fixed_recv.at[0],
            device_id={"basin": lax.rem(here + 1, npos)}, device_id_type=MESH)

    def force_push():
        return pltpu.make_async_remote_copy(
            src_ref=fixed.at[OWN, FORCE], dst_ref=fixed.at[UP, FORCE], send_sem=fixed_send.at[1], recv_sem=fixed_recv.at[1],
            device_id={"basin": lax.rem(here + 1, npos)}, device_id_type=MESH)

    def first_copy(source, owner, slot):
        return pltpu.make_async_remote_copy(
            src_ref=source, dst_ref=gathered.at[slot], send_sem=first_send.at[owner], recv_sem=first_recv.at[slot],
            device_id={"basin": min(1, npos - 1), "tile": owner}, device_id_type=MESH)

    def part_copy(order):
        owner = owner_of(order)
        slot = mine - (mine > owner).astype(jnp.int32)
        return pltpu.make_async_remote_copy(
            src_ref=part.at[order], dst_ref=arrived.at[slot],
            send_sem=part_send.at[order], recv_sem=part_recv.at[slot],
            device_id={"tile": owner}, device_id_type=MESH)

    def part_arrival(slot):
        return pltpu.make_async_remote_copy(
            src_ref=part.at[slot], dst_ref=arrived.at[slot],
            send_sem=part_send.at[slot], recv_sem=part_recv.at[slot],
            device_id={"tile": owner_of(slot)}, device_id_type=MESH)

    def flow_copy(substep, ahead):
        return pltpu.make_async_remote_copy(
            src_ref=flow.at[substep], dst_ref=inflow.at[substep],
            send_sem=flow_send.at[ahead - 1, substep], recv_sem=flow_recv.at[substep],
            device_id={"basin": lax.rem(here + ahead, npos)}, device_id_type=MESH)

    def each_chain(do):
        def one(chain, carry):
            do(chain)
            return carry
        lax.fori_loop(0, rows, one, 0)

    @pl.when(pushes)
    def _():
        pl.semaphore_wait(barrier, 1)
        each_chain(lambda chain: matrix_push(chain).start())

    lane = lax.rem(iota((rows, width), 1), rows)
    row = iota((rows, width), 0)

    def cell_sums(order):
        cells = cell[order]
        ahead = cells - iota(cells.shape, 0)
        if rows & (rows - 1):
            shift, upper = lax.rem(ahead + rows, rows), cells // rows
        else:
            shift, upper = ahead & (rows - 1), cells >> (rows.bit_length() - 1)
        shift = shift.astype(jnp.float32).astype(jnp.bfloat16)
        upper = upper.astype(jnp.float32).astype(jnp.bfloat16)
        head, tail = two_terms(frac[order] * water[order])
        zero = jnp.zeros_like(head)
        one = jnp.ones_like(head)
        picks = [shift == jnp.bfloat16(at) for at in range(rows)]
        left = jnp.concatenate([jnp.where(pick, head, zero) for pick in picks] + [jnp.where(pick, tail, zero) for pick in picks], axis=0)
        right = jnp.concatenate([jnp.where(upper == jnp.bfloat16(at), one, zero) for at in range(width // rows)], axis=0)
        both = lax.dot_general(left, right, NT, preferred_element_type=jnp.float32)
        terms = []
        for at in range(rows):
            start = at * rows
            single = jnp.where(lane == row, both[start:start + rows] + both[rows * rows + start:rows * rows + start + rows], 0.0)
            terms.append(pltpu.roll(single, at, 1) if at else single)
        while len(terms) > 1:
            terms = [sum(terms[at:at + 2][1:], terms[at]) for at in range(0, len(terms), 2)]
        return jnp.where(lane < row, pltpu.roll(terms[0], width - rows, 1), terms[0])

    hold = jnp.where(mine == 0, nset - 1, 0)

    def group(order, carry):
        for copy in tile_loads(order):
            copy.wait()
        sums = cell_sums(order)

        @pl.when(order < nset - 1)
        def _():
            part[order] = sums

        @pl.when(order == nset - 1)
        def _():
            own_ref[...] = sums

        @pl.when(jnp.logical_and(order == hold, jnp.logical_not(pushes)))
        def _():
            pl.semaphore_wait(barrier, (nset - 1) * (1 + paired.astype(jnp.int32)) + paired.astype(jnp.int32)
                              + to_next.astype(jnp.int32) + to_second.astype(jnp.int32) + starts.astype(jnp.int32) * firsts)

            @pl.when(paired)
            def _():
                pl.semaphore_signal(go, inc=1, device_id={"basin": here - 1}, device_id_type=MESH)

        @pl.when(jnp.logical_and(order == hold, pushes))
        def _():
            pl.semaphore_wait(go, 1)

        for owner in range(firsts):
            at = owner - (owner > mine).astype(jnp.int32)
            at = jnp.where(jnp.logical_and(late, owner < 2), 1 - at, at)

            @pl.when(jnp.logical_and(jnp.logical_and(starts, mine != owner), order == jnp.maximum(hold, at)))
            def _():
                first_copy(part.at[at], owner, mine).start()

            @pl.when(jnp.logical_and(jnp.logical_and(starts, mine == owner), order == nset - 1))
            def _():
                first_copy(own_ref, owner, mine).start()

        for done in reversed(range(nset - 1)):
            @pl.when(jnp.logical_or(jnp.logical_and(order == hold, done <= order), jnp.logical_and(order > hold, done == order)))
            def _():
                part_copy(done).start()

        @pl.when(order == 0)
        def _():
            for copy in small_loads:
                copy.start()
            matrix_load.start()

        return carry

    lax.fori_loop(0, nset, group, 0)

    for copy in small_loads:
        copy.wait()
    links = jnp.zeros((rows, width), jnp.int32)
    for chain in range(rows):
        links = jnp.where(row == chain, upstream_ref[0, chain], links)
    fixed[OWN, LINK] = links.astype(jnp.float32)
    fixed[OWN, LIVE] = mask_ref[0].astype(jnp.float32)
    fixed[OWN, RATE] = kappa_ref[0]
    fixed[OWN, START] = storage_ref[0]
    level_ref[OWN] = storage_ref[0]

    @pl.when(jnp.logical_or(here == 0, gathers))
    def _():
        inflow[...] = jnp.zeros_like(inflow)

    @pl.when(pushes)
    def _():
        fixed_push().start()

    def prepare(slot, ready):
        def one(chain, carry):
            ready(chain)
            head, tail = two_terms(inverse[slot, chain].T)
            heads[slot, chain] = head
            tails[slot, chain] = tail
            return carry

        def rest(chain, carry):
            ready(chain)
            return carry
        lax.fori_loop(0, half, one, 0)
        lax.fori_loop(half, rows, rest, 0)

    matrix_load.wait()
    prepare(OWN, lambda chain: None)

    picked = [lax.rem(iota((2 * half, width), 0), half) == chain for chain in range(half)]

    def product(slot, vector):
        head = vector.astype(jnp.bfloat16).astype(jnp.float32)
        tail = vector - head
        left = jnp.concatenate([head[:half], tail[:half]], axis=0).astype(jnp.bfloat16)
        first = jnp.zeros((2 * half, width), jnp.float32)
        second = jnp.zeros((2 * half, width), jnp.float32)
        reduced = []
        for chain in range(rows - half):
            if chain < half:
                single = jnp.where(picked[chain], left, jnp.zeros_like(left))
                first += jnp.dot(single, heads[slot, chain], preferred_element_type=jnp.float32)
                second += jnp.dot(single, tails[slot, chain], preferred_element_type=jnp.float32)
            other = half + chain
            reduced.append(jnp.sum(inverse[slot, other] * vector[other:other + 1], axis=1)[None])
        total = first + second
        return jnp.concatenate([total[:half] + total[half:]] + reduced, axis=0)

    @pl.when(paired)
    def _():
        prepare(UP, lambda chain: matrix_push(chain).wait_recv())
        fixed_push().wait_recv()
        level_ref[UP] = fixed[UP, START]

    runoff = own_ref[...]
    for order in range(nset - 1):
        part_arrival(order).wait_recv()
        runoff = runoff + arrived[order]
    fixed[OWN, FORCE] = time_step * runoff

    @pl.when(jnp.logical_and(pushes, here > 0))
    def _():
        force_push().start()

    @pl.when(jnp.logical_and(paired, here > 1))
    def _():
        force_push().wait_recv()

    @pl.when(gathers)
    def _():
        for slot in range(nset):
            first_copy(own_ref, 0, slot).wait_recv()
        fixed[UP, FORCE] = time_step * sum([gathered[slot] for slot in range(1, nset)], gathered[0])

    def turn(count, carry):
        slot = jnp.where(paired, lax.rem(count, 2), OWN)
        substep = jnp.where(paired, count // 2, count)
        leads = jnp.logical_or(jnp.logical_not(paired), slot == UP)

        @pl.when(jnp.logical_and(leads, jnp.logical_or(here > 1, jnp.logical_and(here == 1, mine >= firsts))))
        def _():
            flow_copy(substep, 1).wait_recv()

        came = inflow[jnp.where(leads, substep, SUBSTEPS)]
        links = fixed[slot, LINK].astype(jnp.int32)
        choices = [jnp.broadcast_to(came[chain:chain + 1], (rows, width)) for chain in range(rows)]
        bit = 1
        while len(choices) > 1:
            upper = (links & bit) != 0
            choices = [
                jnp.where(upper, choices[at + 1], choices[at]) if at + 1 < len(choices) else choices[at]
                for at in range(0, len(choices), 2)]
            bit *= 2
        incoming = choices[0]
        wet = fixed[slot, LIVE] * product(slot, level_ref[slot] + fixed[slot, FORCE] + incoming)
        outflow = fixed[slot, RATE] * wet

        @pl.when(slot == OWN)
        def _():
            flow[substep] = outflow

            @pl.when(to_second)
            def _():
                flow_copy(substep, 2).start()

            @pl.when(to_next)
            def _():
                flow_copy(substep, 1).start()

            out_ref[0] = wet - outflow
            out_ref[1] = outflow

        @pl.when(slot == UP)
        def _():
            inflow[SUBSTEPS] = outflow

        level_ref[slot] = wet - outflow
        return carry

    lax.fori_loop(0, jnp.where(paired, 2 * SUBSTEPS, SUBSTEPS), turn, 0)

    for order in range(nset - 1):
        part_copy(order).wait_send()

    @pl.when(pushes)
    def _():
        each_chain(lambda chain: matrix_push(chain).wait_send())
        fixed_push().wait_send()

    @pl.when(jnp.logical_and(pushes, here > 0))
    def _():
        force_push().wait_send()

    @pl.when(starts)
    def _():
        for owner in range(firsts):
            first_copy(own_ref, owner, mine).wait_send()

    @pl.when(to_next)
    def _():
        for substep in range(SUBSTEPS):
            flow_copy(substep, 1).wait_send()

    @pl.when(to_second)
    def _():
        for substep in range(SUBSTEPS):
            flow_copy(substep, 2).wait_send()


def solution(mesh):
    npos, nset = mesh.shape["basin"], mesh.shape["tile"]

    def local(tile_water, tile_frac, tile_cell, storage, kappa, inverse, cell_mask, upstream):
        rows, width = storage.shape[1:]
        tiles = tile_water.shape[2]
        anywhere = pl.BlockSpec(memory_space=pltpu.HBM)
        vmem = pl.BlockSpec(memory_space=pltpu.VMEM)
        others = max(nset - 1, 1)
        out = pl.pallas_call(
            functools.partial(kernel, npos, nset),
            out_shape=pltpu.VMEM((2, rows, width), jnp.float32),
            in_specs=[anywhere] * 8,
            out_specs=vmem,
            scratch_shapes=[
                pltpu.VMEM(storage.shape, jnp.float32),
                pltpu.VMEM(kappa.shape, jnp.float32),
                pltpu.VMEM(cell_mask.shape, jnp.int32),
                pltpu.SMEM(upstream.shape, jnp.int32),
                pltpu.VMEM((nset, rows, tiles), jnp.float32),
                pltpu.VMEM((nset, rows, tiles), jnp.float32),
                pltpu.VMEM((nset, rows, tiles), jnp.int32),
                pltpu.VMEM((2, rows, width, width), jnp.float32),
                pltpu.VMEM((2, rows // 2, width, width), jnp.bfloat16),
                pltpu.VMEM((2, rows // 2, width, width), jnp.bfloat16),
                pltpu.VMEM((others, rows, width), jnp.float32),
                pltpu.VMEM((others, rows, width), jnp.float32),
                pltpu.VMEM((SUBSTEPS, rows, width), jnp.float32),
                pltpu.VMEM((SUBSTEPS + 1, rows, width), jnp.float32),
                pltpu.VMEM((2, 5, rows, width), jnp.float32),
                pltpu.VMEM((nset, rows, width), jnp.float32),
                pltpu.VMEM((2, rows, width), jnp.float32),
                pltpu.VMEM((rows, width), jnp.float32),
                pltpu.SemaphoreType.DMA((4,)),
                pltpu.SemaphoreType.DMA((nset, 3)),
                pltpu.SemaphoreType.DMA((1,)),
                pltpu.SemaphoreType.DMA((others,)),
                pltpu.SemaphoreType.DMA((others,)),
                pltpu.SemaphoreType.DMA((2, SUBSTEPS)),
                pltpu.SemaphoreType.DMA((SUBSTEPS,)),
                pltpu.SemaphoreType.DMA((rows,)),
                pltpu.SemaphoreType.DMA((rows,)),
                pltpu.SemaphoreType.DMA((2,)),
                pltpu.SemaphoreType.DMA((2,)),
                pltpu.SemaphoreType.DMA((nset,)),
                pltpu.SemaphoreType.DMA((nset,)),
                pltpu.SemaphoreType.REGULAR,
            ],
            compiler_params=pltpu.CompilerParams(collective_id=0, has_side_effects=True, vmem_limit_bytes=60 * 2**20),
        )(tile_water, tile_frac, tile_cell, storage, kappa, inverse, cell_mask, upstream)
        return out[:1], out[1:]

    tiled = P("basin", None, "tile")
    chain = P("basin", "tile", None)
    return jax.shard_map(
        local,
        mesh=mesh,
        in_specs=(tiled, tiled, tiled, chain, chain, P("basin", "tile", None, None), chain, P("basin", "tile")),
        out_specs=(chain, chain),
        check_vma=False,
    )
```
